128 devices in a mesh: pipe: 2 (over y_lo), tensor: 8 (over y_hi, x), dp: 8 (over z, core).
Axes of the slice: x: 4, y: 4 (y_hi: 2, y_lo: 2; y = y_hi * 2 + y_lo), z: 4, core: 2. Of those that a mesh axis runs over, the one named last changes fastest.
Arguments:
- section_input: bfloat16 [8192, 1024], P('dp'), may hold values from -6 to 6
- segment_ids: int32 [8192], P('dp'), may hold values from 0 to 127, never falling along the last dimension, each value on 1 to 256 neighbouring positions
- w_qkv: bfloat16 [2, 1024, 3, 1024], P('pipe', None, None, 'tensor'), may hold values from -0.1875 to 0.1875
- qv_bias: float32 [2, 2, 1024], P('pipe', None, 'tensor'), may hold values from -3 to 3
- w_out: bfloat16 [2, 1024, 1024], P('pipe', 'tensor'), may hold values from -0.75 to 0.75
- out_bias: float32 [2, 1024], P('pipe'), may hold values from -3 to 3
- w_up: bfloat16 [2, 1024, 4096], P('pipe', None, 'tensor'), may hold values from -0.1875 to 0.1875
- up_bias: float32 [2, 4096], P('pipe', 'tensor'), may hold values from -3 to 3
- w_down: bfloat16 [2, 4096, 1024], P('pipe', 'tensor'), may hold values from -0.09375 to 0.09375
- down_bias: float32 [2, 1024], P('pipe'), may hold values from -4 to 4
- norm_gains: float32 [2, 2, 1024], P('pipe'), may hold values from 0.25 to 1.75
- norm_shifts: float32 [2, 2, 1024], P('pipe'), may hold values from -2 to 2
- out_grad: bfloat16 [8192, 1024], P('dp'), may hold values from -6 to 6
Outputs:
- section_outputs: bfloat16 [2, 8192, 1024], P('pipe', 'dp')
- input_grads: bfloat16 [2, 8192, 1024], P('pipe', 'dp')
- grad_qkv: float32 [2, 1024, 3, 1024], P('pipe', None, None, 'tensor')
- grad_qv_bias: float32 [2, 2, 1024], P('pipe', None, 'tensor')
- grad_w_out: float32 [2, 1024, 1024], P('pipe', 'tensor')
- grad_out_bias: float32 [2, 1024], P('pipe')
- grad_w_up: float32 [2, 1024, 4096], P('pipe', None, 'tensor')
- grad_up_bias: float32 [2, 4096], P('pipe', 'tensor')
- grad_w_down: float32 [2, 4096, 1024], P('pipe', 'tensor')
- grad_down_bias: float32 [2, 1024], P('pipe')
- grad_gains: float32 [2, 2, 1024], P('pipe')
- grad_shifts: float32 [2, 2, 1024], P('pipe')
The draws below stay inside these ranges and needn't reach their ends.
Inputs may be any that keep to these rules, and one draw needn't show every extreme that they name: `segment_ids`: ids never fall along the tokens; one document is 1 to 256 tokens.
All inputs are finite; a program needn't handle non-finite values.
Results may differ from the reference program's by a relative error of at most 0.035.
Values may be sent and summed in bfloat16 or wider, within the bound.
A program may use at most 128 MiB of HBM per device.

```python
import math
import jax
import jax.numpy as jnp
import numpy as np
from jax import lax

D = 1024
HEADS = 16
HEAD_DIM = 64
FF = 4096
SEQ_LEN = 256
TOKENS = 8192


def shard_levels(own_key, extent, shards, least, high):
    def one(axis_at, parts):
        draws = jax.random.uniform(jax.random.fold_in(jax.random.fold_in(own_key, 6), axis_at), (parts,), jnp.float32, least / len(shards), high / len(shards))
        return jnp.repeat(jnp.exp(draws), extent[axis_at] // parts).reshape((-1,) + (1,) * (len(extent) - axis_at - 1))

    loudness = one(*shards[0])
    for cut in shards[1:]:
        loudness = loudness * one(*cut)
    return loudness


def profile(amount, total, most, slope):
    weights = [(1 << 20) // math.isqrt(rank ** slope) + 1 for rank in range(2, amount + 1)]
    spare, given = total - most - (amount - 1), [1] * (amount - 1)
    while spare > 0:
        free = [i for i in range(amount - 1) if given[i] < most]
        whole, budget = sum([weights[i] for i in free]), spare
        for i in free:
            addition = min(most - given[i], max(1, budget * weights[i] // whole), spare)
            given[i] = given[i] + addition
            spare = spare - addition
    return np.array([most] + given)


def ragged(rng, count, total, most, skew):
    if count == 2:
        one = jax.random.randint(rng, (), max(1, total - most), min(most, total - 1) + 1)
        return jnp.stack([one, total - one])
    lengths = jnp.asarray(profile(count, total, most, skew), jnp.int32)
    pairs = (count - 1) // 2
    donor, taker = lengths[1:1 + 2 * pairs:2], lengths[2:2 + 2 * pairs:2]
    slack = jnp.minimum(donor - 1, most - taker)
    moved = jax.random.randint(jax.random.fold_in(rng, 1), (pairs,), 0, 1 << 20) % (slack + 1)
    lengths = lengths.at[1:1 + 2 * pairs:2].set(donor - moved).at[2:2 + 2 * pairs:2].set(taker + moved)
    return lengths[jax.random.permutation(jax.random.fold_in(rng, 2), count)]


def scatter_about(rng, dims, spread, reach, shards=(), held_as=jnp.bfloat16):
    level = shard_levels(rng, dims, shards, -0.22, 0.18) if shards else 1.0
    array = jax.random.normal(rng, dims, jnp.float32) * spread * level
    return jnp.minimum(jnp.maximum(array, -reach), reach).astype(held_as)


def setup_inputs(seed: int = 0) -> dict:
    splits = jax.random.split(jax.random.key(seed), 14)
    section_input = scatter_about(splits[0], (TOKENS, D), 1.0, 6.0, ((0, 8),))
    segment_ids = jnp.searchsorted(jnp.cumsum(ragged(splits[1], TOKENS // min(64, SEQ_LEN // 2), TOKENS, SEQ_LEN, 1)), jnp.arange(TOKENS), side="right").astype(jnp.int32)
    w_qkv = scatter_about(splits[2], (2, D, 3, D), D ** -0.5, 0.1875, ((0, 2), (3, 8)))
    qv_bias = scatter_about(splits[3], (2, 2, D), 0.5, 3.0, ((0, 2), (2, 8)), jnp.float32)
    w_out = scatter_about(splits[4], (2, D, D), (D // 16) ** -0.5, 0.75, ((0, 2), (1, 8)))
    out_bias = scatter_about(splits[5], (2, D), 0.5, 3.0, ((0, 2),), jnp.float32)
    w_up = scatter_about(splits[6], (2, D, FF), D ** -0.5, 0.1875, ((0, 2), (2, 8)))
    up_bias = scatter_about(splits[7], (2, FF), 0.5, 3.0, ((0, 2), (1, 8)), jnp.float32)
    w_down = scatter_about(splits[8], (2, FF, D), FF ** -0.5, 0.09375, ((0, 2), (1, 8)))
    down_bias = scatter_about(splits[9], (2, D), 0.8, 4.0, ((0, 2),), jnp.float32)
    norm_gains = jnp.clip(1.0 + 0.15 * jax.random.normal(splits[10], (2, 2, D), jnp.float32), 0.25, 1.75)
    norm_shifts = scatter_about(splits[11], (2, 2, D), 0.3, 2.0, ((0, 2),), jnp.float32)
    out_grad = scatter_about(splits[12], (TOKENS, D), 1.0, 6.0, ((0, 8),))
    return dict(section_input=section_input, segment_ids=segment_ids, w_qkv=w_qkv, qv_bias=qv_bias, w_out=w_out, out_bias=out_bias, w_up=w_up, up_bias=up_bias, w_down=w_down, down_bias=down_bias, norm_gains=norm_gains, norm_shifts=norm_shifts, out_grad=out_grad)


NORM_EPS = 1e-05
GELU_COEF = 0.7978845608028654
CUBIC_COEF = 0.044715
MASKED_SCORE = -1e+30

def gelu_pair(pre_act):
    tanh_val = jnp.tanh(GELU_COEF * (pre_act + CUBIC_COEF * pre_act * pre_act * pre_act))
    gelu_value = 0.5 * pre_act * (1.0 + tanh_val)
    act_slope = 0.5 * (1.0 + tanh_val) + 0.5 * pre_act * (1.0 - tanh_val * tanh_val) * GELU_COEF * (1.0 + 3.0 * CUBIC_COEF * pre_act * pre_act)
    return (gelu_value, act_slope)

def layer_norm(rows_in, norm_gain, norm_shift):
    centred = rows_in - lax.optimization_barrier(jnp.mean(rows_in, axis=-1, keepdims=True))
    inv_std = lax.rsqrt(lax.optimization_barrier(jnp.mean(centred * centred, axis=-1, keepdims=True)) + NORM_EPS)
    normed = centred * inv_std
    return (normed * norm_gain + norm_shift, normed, inv_std)

def norm_back(grad_out, normed, inv_std, norm_gain):
    scaled = grad_out * norm_gain
    return inv_std * (scaled - lax.optimization_barrier(jnp.mean(scaled, axis=-1, keepdims=True)) - normed * lax.optimization_barrier(jnp.mean(scaled * normed, axis=-1, keepdims=True)))

def visible(seg_rows):
    length = seg_rows.shape[-1]
    position = jnp.arange(length)
    causal = position[:, None] >= position[None, :]
    same_doc = seg_rows[:, :, None] == seg_rows[:, None, :]
    return (causal[None] & same_doc)[:, None]

def wide_product(form, left_arr, right_arr):
    return jnp.einsum(form, left_arr.astype(jnp.float32), right_arr.astype(jnp.float32), precision=lax.Precision.HIGHEST)

def scores_of(query_rows, key_rows, seg_rows):
    score_scale = query_rows.shape[-1] ** (-0.5)
    raw_scores = wide_product('sqhe,skhe->shqk', query_rows, key_rows) * score_scale
    return (jnp.where(visible(seg_rows), raw_scores, MASKED_SCORE), score_scale)

def attend(query_rows, key_rows, value_rows, seg_rows):
    scores, score_scale = scores_of(query_rows, key_rows, seg_rows)
    row_max = lax.optimization_barrier(jnp.max(scores, axis=-1, keepdims=True))
    log_total = row_max + jnp.log(lax.optimization_barrier(jnp.sum(jnp.exp(scores - row_max), axis=-1, keepdims=True)))
    prob_rows = jnp.exp(scores - log_total).astype(jnp.bfloat16)
    mix_rows = wide_product('shqk,skhe->sqhe', prob_rows, value_rows).astype(jnp.bfloat16)
    return (mix_rows, log_total)

def attend_back(query_rows, key_rows, value_rows, seg_rows, log_total, grad_mix):
    scores, score_scale = scores_of(query_rows, key_rows, seg_rows)
    prob_rows = jnp.exp(scores - log_total)
    grad_prob = wide_product('sqhe,skhe->shqk', grad_mix, value_rows)
    row_delta = lax.optimization_barrier(jnp.sum(prob_rows * grad_prob, axis=-1, keepdims=True))
    grad_scores = (prob_rows * (grad_prob - row_delta) * score_scale).astype(jnp.bfloat16)
    g_query = wide_product('shqk,skhe->sqhe', grad_scores, key_rows).astype(jnp.bfloat16)
    g_key = wide_product('shqk,sqhe->skhe', grad_scores, query_rows).astype(jnp.bfloat16)
    g_value = wide_product('shqk,sqhe->skhe', prob_rows.astype(jnp.bfloat16), grad_mix).astype(jnp.bfloat16)
    return (g_query, g_key, g_value)

def section_forward(rows_in, seg_rows, params):
    proj_in, qkv_shift, proj_out, out_shift, up_proj, up_shift, down_proj, down_shift, norm_gain, norm_shift = params
    count_rows = rows_in.shape[0]
    seq_count = count_rows // SEQ_LEN
    residual = rows_in.astype(jnp.float32)
    first_norm, normed1, inv1 = layer_norm(residual, norm_gain[0], norm_shift[0])
    first_in = first_norm.astype(jnp.bfloat16)
    qkv = (wide_product('td,dgc->tgc', first_in, proj_in) + qkv_shift).astype(jnp.bfloat16)
    shaped = qkv.reshape(seq_count, SEQ_LEN, 3, HEADS, HEAD_DIM)
    mix_rows, log_total = attend(shaped[:, :, 0], shaped[:, :, 1], shaped[:, :, 2], seg_rows)
    mix_flat = mix_rows.reshape(count_rows, D)
    middle = residual + wide_product('tc,cd->td', mix_flat, proj_out) + out_shift
    second_norm, normed2, inv2 = layer_norm(middle, norm_gain[1], norm_shift[1])
    second_in = second_norm.astype(jnp.bfloat16)
    pre_act = wide_product('td,df->tf', second_in, up_proj) + up_shift
    gelu_value, act_slope = gelu_pair(pre_act)
    hidden = gelu_value.astype(jnp.bfloat16)
    result = (middle + wide_product('tf,fd->td', hidden, down_proj) + down_shift).astype(jnp.bfloat16)
    kept_state = (normed1, inv1, first_in, qkv, mix_flat, log_total, normed2, inv2, second_in, act_slope, hidden)
    return (result, kept_state)

def section_backward(grad_rows, kept_state, seg_rows, params):
    proj_in, qkv_shift, proj_out, out_shift, up_proj, up_shift, down_proj, down_shift, norm_gain, norm_shift = params
    normed1, inv1, first_in, qkv, mix_flat, log_total, normed2, inv2, second_in, act_slope, hidden = kept_state
    count_rows = grad_rows.shape[0]
    seq_count = count_rows // SEQ_LEN
    grad_top = grad_rows.astype(jnp.float32)
    g_down = wide_product('tf,td->fd', hidden, grad_rows)
    g_down_shift = lax.optimization_barrier(jnp.sum(grad_top, axis=0))
    g_hidden = wide_product('td,fd->tf', grad_rows, down_proj)
    g_pre = (g_hidden * act_slope).astype(jnp.bfloat16)
    g_up = wide_product('td,tf->df', second_in, g_pre)
    g_up_shift = lax.optimization_barrier(jnp.sum(g_pre.astype(jnp.float32), axis=0))
    g_second = wide_product('tf,df->td', g_pre, up_proj)
    g_middle = grad_top + norm_back(g_second, normed2, inv2, norm_gain[1])
    g_gain2 = lax.optimization_barrier(jnp.sum(g_second * normed2, axis=0))
    g_shift2 = lax.optimization_barrier(jnp.sum(g_second, axis=0))
    middle_low = g_middle.astype(jnp.bfloat16)
    g_proj_out = wide_product('tc,td->cd', mix_flat, middle_low)
    g_out_shift = lax.optimization_barrier(jnp.sum(g_middle, axis=0))
    g_mix = wide_product('td,cd->tc', middle_low, proj_out).astype(jnp.bfloat16)
    shaped = qkv.reshape(seq_count, SEQ_LEN, 3, HEADS, HEAD_DIM)
    g_query, g_key, g_value = attend_back(shaped[:, :, 0], shaped[:, :, 1], shaped[:, :, 2], seg_rows, log_total, g_mix.reshape(seq_count, SEQ_LEN, HEADS, HEAD_DIM))
    g_qkv = jnp.stack([g_query, g_key, g_value], axis=2).reshape(count_rows, 3, D)
    g_proj_in = wide_product('td,tgc->dgc', first_in, g_qkv)
    qkv_sums = lax.optimization_barrier(jnp.sum(g_qkv.astype(jnp.float32), axis=0))
    g_qv = jnp.stack([qkv_sums[0], qkv_sums[2]], axis=0)
    g_first = wide_product('tgc,dgc->td', g_qkv, proj_in)
    g_gain1 = lax.optimization_barrier(jnp.sum(g_first * normed1, axis=0))
    g_shift1 = lax.optimization_barrier(jnp.sum(g_first, axis=0))
    g_low = (g_middle + norm_back(g_first, normed1, inv1, norm_gain[0])).astype(jnp.bfloat16)
    grads = (g_proj_in, g_qv, g_proj_out, g_out_shift, g_up, g_up_shift, g_down, g_down_shift, jnp.stack([g_gain1, g_gain2]), jnp.stack([g_shift1, g_shift2]))
    return (g_low, grads)

def reference(section_input, segment_ids, w_qkv, qv_bias, w_out, out_bias, w_up, up_bias, w_down, down_bias, norm_gains, norm_shifts, out_grad):
    seg_rows = segment_ids.reshape(-1, SEQ_LEN)
    all_params = []
    for section_index in range(2):
        zero_row = jnp.zeros((1, D), jnp.float32)
        qkv_shift = jnp.concatenate([qv_bias[section_index][0:1], zero_row, qv_bias[section_index][1:2]], axis=0)
        all_params.append((w_qkv[section_index], qkv_shift, w_out[section_index], out_bias[section_index], w_up[section_index], up_bias[section_index], w_down[section_index], down_bias[section_index], norm_gains[section_index], norm_shifts[section_index]))
    held_rows = section_input
    outputs = []
    states = []
    for section_index in range(2):
        held_rows, kept_state = section_forward(held_rows, seg_rows, all_params[section_index])
        outputs.append(held_rows)
        states.append(kept_state)
    cotangent = out_grad
    input_list = [None, None]
    grad_list = [None, None]
    for section_index in (1, 0):
        cotangent, grads = section_backward(cotangent, states[section_index], seg_rows, all_params[section_index])
        input_list[section_index] = cotangent
        grad_list[section_index] = grads
    stacked = [jnp.stack([grad_list[0][member], grad_list[1][member]]) for member in range(10)]
    return (jnp.stack(outputs), jnp.stack(input_list), stacked[0], stacked[1], stacked[2], stacked[3], stacked[4], stacked[5], stacked[6], stacked[7], stacked[8], stacked[9])
```

```python
import jax
import jax.numpy as jnp
from jax import lax
from jax.experimental import pallas as pl
from jax.experimental.pallas import tpu as pltpu
from jax.sharding import PartitionSpec as P

MESH = pl.DeviceIdType.MESH
F32 = jnp.float32
BF16 = jnp.bfloat16

SEQ = 256
D = 1024
R = 64
NORM_EPS = 1e-05
GELU_COEF = 0.7978845608028654
CUBIC_COEF = 0.044715
MASKED_SCORE = -1e30
SCALE = 0.125
WQ, WO, WU, WD = range(4)
ROWS = (1024, 128, 1024, 512)
COLS = (384, 1024, 512, 1024)


def dot_nn(a, b):
    return jnp.dot(a, b, preferred_element_type=F32)


def dot_nt(a, b):
    return lax.dot_general(a, b, (((1,), (1,)), ((), ())), preferred_element_type=F32)


def dot_tn(a, b):
    return lax.dot_general(a, b, (((0,), (0,)), ((), ())), preferred_element_type=F32)


def loop(n, body):
    lax.fori_loop(0, n, lambda i, c: (body(i), c)[1], 0)


def ds(start, size):
    return pl.ds(pl.multiple_of(start, size), size)


def norm(rows):
    centred = rows - jnp.mean(rows, axis=-1, keepdims=True)
    inv = lax.rsqrt(jnp.mean(centred * centred, axis=-1, keepdims=True) + NORM_EPS)
    return centred * inv, inv


def norm_back(grad, normed, inv, gain):
    e = grad * gain
    return inv * (
        e - jnp.mean(e, axis=-1, keepdims=True) - normed * jnp.mean(e * normed, axis=-1, keepdims=True)
    )


def kernel(
    x_in, seg_in, wq_in, qvb_in, wo_in, outb_in, wu_in, upb_in, wd_in, downb_in, gain_in, shift_in, og_in,
    so_out, ig_out, gq_out, go_out, gu_out, gd_out, small_out, up_out, qv_out,
    wq, wo, wu, wd, prm, mask, xs_buf, g_buf, a1, a2, dyb, xo, ig0, qkv, prob, mix, hid, slope, du, dqkv, acc,
    rs_out, rs_in, n1, n2, i1, i2, yrow, dyrow,
    gq, go, gu, gd, cq, co, cu, cd, yq, yo, yu, yd, zq, zo, zu, zd, sm, sm2, sm3, smy, smz, smx,
    x_s, x_r, wy_s, wy_r, wc_s, wc_r, pr_s, pr_r, loc, gc_s, gc_r, gy_s, gy_r, gz_s, gz_r, ga_s, ga_r, gl,
    sm_s, sm_r, o_s, o_r, o_l,
):
    p = lax.axis_index("pipe")
    t = lax.axis_index("tensor")
    dp = lax.axis_index("dp")
    h_me, x = lax.div(t, 4), lax.rem(t, 4)
    z, c = lax.div(dp, 2), lax.rem(dp, 2)
    y = h_me * 2 + p

    def dev(xx, yy, zz, cc):
        return {"pipe": lax.rem(yy, 2), "tensor": lax.div(yy, 2) * 4 + xx, "dp": zz * 2 + cc}

    def xp(d):
        return lax.rem(x + d, 4)

    def yp(d):
        return lax.rem(y + d, 4)

    def zp(d):
        return lax.rem(z + d, 4)

    core_peer = dev(x, y, z, 1 - c)

    def remote(src, dst, ss, rs, device):
        return pltpu.make_async_remote_copy(
            src_ref=src, dst_ref=dst, send_sem=ss, recv_sem=rs, device_id=device, device_id_type=MESH
        )

    own = ds(x * R, R)
    w_in = (wq_in, wo_in, wu_in, wd_in)
    w_all = (wq, wo, wu, wd)
    g_all = (gq, go, gu, gd)
    c_all = (cq, co, cu, cd)
    y_all = (yq, yo, yu, yd)
    z_all = (zq, zo, zu, zd)
    g_outs = (gq_out, go_out, gu_out, gd_out)

    zc_peers = [(dz, dc) for dz in range(4) for dc in range(2) if (dz, dc) != (0, 0)]

    barrier = pltpu.get_barrier_semaphore()
    peers = [dev(xp(d), y, z, c) for d in (1, 2, 3)]
    peers += [dev(x, yp(d), z, c) for d in (1, 2, 3)]
    peers += [dev(x, y, zp(dz), lax.rem(c + dc, 2)) for dz, dc in zc_peers]
    for peer in peers:
        pl.semaphore_signal(barrier, inc=1, device_id=peer, device_id_type=MESH)

    load_x = pltpu.make_async_copy(x_in.at[ds(y * SEQ, SEQ)], xs_buf.at[0], loc.at[0])
    load_g = pltpu.make_async_copy(og_in.at[ds(y * SEQ, SEQ)], g_buf.at[1], loc.at[1])
    load_x.start()
    load_g.start()
    load_w = [pltpu.make_async_copy(w_in[k], w_all[k].at[y], loc.at[2 + k]) for k in range(4)]
    for copy in load_w:
        copy.start()

    prm[y] = jnp.zeros((8, D), F32)
    prm[y, 0:1, :] = outb_in[...]
    prm[y, 1:2, :] = downb_in[...]
    prm[y, 2:4, :] = gain_in[...]
    prm[y, 4:6, :] = shift_in[...]
    prm[y, 6:7, 0:512] = upb_in[...]
    prm[y, 7:8, 0:128] = qvb_in[0:1, :]
    prm[y, 7:8, 128:256] = qvb_in[1:2, :]
    sm[...] = jnp.zeros_like(sm)

    pl.semaphore_wait(barrier, len(peers))

    def send_prm(d):
        return remote(prm.at[y], prm.at[y], pr_s.at[d - 1], pr_r.at[d - 1], dev(x, yp(d), z, c))

    for d in (1, 2, 3):
        send_prm(d).start()

    def half_rows(k, which):
        return ds(which * (ROWS[k] // 2), ROWS[k] // 2)

    def w_send(k, d):
        rows = half_rows(k, c)
        i = k * 3 + d - 1
        return remote(w_in[k].at[rows], w_all[k].at[y, rows], wy_s.at[i], wy_r.at[i], dev(x, yp(d), z, c))

    def w_pass(k, d):
        rows = half_rows(k, c)
        i = k * 3 + d - 1
        block = w_all[k].at[lax.rem(y - d + 4, 4), rows]
        return remote(block, block, wc_s.at[i], wc_r.at[i], core_peer)

    def w_send_all(s):
        @pl.when(p == s)
        def _():
            for k in range(4):
                for d in (2, 1, 3):
                    w_send(k, d).start()

    def w_forward(s, k):
        @pl.when(p == s)
        def _():
            w_send(k, 2).wait_recv()
            w_pass(k, 2).start()

        @pl.when(p != s)
        def _():
            for d in (1, 3):
                w_send(k, d).wait_recv()
                w_pass(k, d).start()

    def w_ready(s, k):
        @pl.when(p == s)
        def _():
            load_w[k].wait()
            w_pass(k, 2).wait_recv()

        @pl.when(p != s)
        def _():
            for d in (1, 3):
                w_pass(k, d).wait_recv()

    def rs_copy(k, d):
        dest = xp(d)
        return remote(
            rs_out.at[k // 2, ds(dest * R, R)], rs_in.at[k // 2, d - 1], x_s.at[k * 3 + d - 1], x_r.at[k * 3 + d - 1],
            dev(dest, y, z, c),
        )

    def rs_start(k):
        for d in (2, 1, 3):
            rs_copy(k, d).start()

    def rs_finish(k):
        total = acc[own, :]
        for d in (1, 3, 2):
            rs_copy(k, d).wait_recv()
            total = total + rs_in[k // 2, d - 1].astype(F32)
        return total

    def ag_copy(k, ref, d):
        return remote(ref.at[own], ref.at[own], x_s.at[k * 3 + d - 1], x_r.at[k * 3 + d - 1], dev(xp(d), y, z, c))

    def ag_start(k, ref):
        for d in (2, 1, 3):
            ag_copy(k, ref, d).start()

    def ag_finish(k, ref):
        for d in (1, 3, 2):
            ag_copy(k, ref, d).wait_recv()

    def out_copy(i, ref, out, d):
        rows = ds(y * SEQ, SEQ)
        j = i * 3 + d - 1
        return remote(ref, out.at[rows], o_s.at[j], o_r.at[j], dev(x, yp(d), z, c))

    def out_local(i, ref, out):
        return pltpu.make_async_copy(ref, out.at[ds(y * SEQ, SEQ)], o_l.at[i])

    def out_start(i, s, ref, out):
        for d in (1, 2, 3):
            @pl.when(lax.rem(y + d, 2) == s)
            def _():
                out_copy(i, ref, out, d).start()

        @pl.when(p == s)
        def _():
            out_local(i, ref, out).start()

    def out_finish(i, s, ref, out):
        for d in (1, 2, 3):
            @pl.when(lax.rem(y + d, 2) == s)
            def _():
                out_copy(i, ref, out, d).wait_send()

        @pl.when(p == s)
        def _():
            out_local(i, ref, out).wait()
            for d in (1, 2, 3):
                out_copy(i, ref, out, d).wait_recv()

    def gc_copy(s, k, h):
        i = (s * 4 + k) * 2 + h
        return remote(g_all[k].at[s, h, half_rows(k, 1 - c)], c_all[k].at[s, h], gc_s.at[i], gc_r.at[i], core_peer)

    def gc_start(s, k):
        for h in (0, 1):
            gc_copy(s, k, h).start()

    def sum_rows(k, target, base, sources, rows):
        step = min(rows, 64)

        def body(r):
            here = pl.ds(pl.multiple_of(base + r * step, 16), step)
            there = pl.ds(pl.multiple_of(r * step, 16), step)
            total = target[here, :].astype(F32)
            for source in sources:
                total = total + source[there, :].astype(F32)
            target[here, :] = total.astype(BF16)

        loop(rows // step, body)

    def gy_copy(s, k, h):
        d = lax.rem(2 * h + s - y + 4, 4)
        i = (s * 4 + k) * 2 + h
        return remote(
            g_all[k].at[s, h, half_rows(k, c)], y_all[k].at[d - 1], gy_s.at[i], gy_r.at[k * 3 + d - 1],
            dev(x, 2 * h + s, z, c),
        )

    def gy_start(s, k):
        for h in (0, 1):
            gc_copy(s, k, h).wait_recv()
            sum_rows(k, g_all[k].at[s, h], c * (ROWS[k] // 2), [c_all[k].at[s, h]], ROWS[k] // 2)

            @pl.when(y != 2 * h + s)
            def _():
                gy_copy(s, k, h).start()

    def piece(k, zz):
        q = ROWS[k] // 8
        return pl.ds(pl.multiple_of(c * (ROWS[k] // 2) + zz * q, 16), q)

    def gz_copy(s, k, d):
        zz = zp(d)
        i = k * 3 + d - 1
        return remote(
            g_all[k].at[s, h_me, piece(k, zz)], z_all[k].at[d - 1], gz_s.at[i], gz_r.at[i], dev(x, y, zz, c)
        )

    def gz_start(s, k):
        @pl.when(p == s)
        def _():
            for d in (1, 2, 3):
                slot = y_all[k].at[d - 1]
                remote(slot, slot, gy_s.at[0], gy_r.at[k * 3 + d - 1], dev(x, yp(d), z, c)).wait_recv()
            sum_rows(
                k, g_all[k].at[s, h_me], c * (ROWS[k] // 2), [y_all[k].at[j] for j in range(3)], ROWS[k] // 2
            )
            for d in (2, 1, 3):
                gz_copy(s, k, d).start()

    def ga_copy(s, k, j):
        dz, dc = zc_peers[j]
        i = k * 7 + j
        rows = piece(k, z)
        return remote(
            g_all[k].at[s, h_me, rows], g_outs[k].at[rows], ga_s.at[i], ga_r.at[i],
            dev(x, y, zp(dz), lax.rem(c + dc, 2)),
        )

    def ga_local(s, k):
        rows = piece(k, z)
        return pltpu.make_async_copy(g_all[k].at[s, h_me, rows], g_outs[k].at[rows], gl.at[k])

    def ga_start(s, k):
        @pl.when(p == s)
        def _():
            q = ROWS[k] // 8
            for d in (1, 3, 2):
                gz_copy(s, k, d).wait_recv()
            sum_rows(
                k, g_all[k].at[s, h_me], c * (ROWS[k] // 2) + z * q, [z_all[k].at[j] for j in range(3)], q
            )
            for j in range(7):
                ga_copy(s, k, j).start()
            ga_local(s, k).start()

    def ga_finish(s, k):
        @pl.when(p == s)
        def _():
            ga_local(s, k).wait()
            for j in range(7):
                ga_copy(s, k, j).wait_recv()

    w_send_all(0)

    seg = seg_in[pl.ds(y, 1), :].astype(F32)
    seg_b = jnp.broadcast_to(seg, (SEQ, SEQ))
    rows_i = lax.broadcasted_iota(jnp.int32, (SEQ, SEQ), 0)
    cols_i = lax.broadcasted_iota(jnp.int32, (SEQ, SEQ), 1)
    mask[...] = jnp.where((rows_i >= cols_i) & (seg_b == seg_b.T), 0.0, MASKED_SCORE)

    low_lanes = lax.broadcasted_iota(jnp.int32, (SEQ, 128), 1) < 64

    def pick_head(value, e):
        keep = low_lanes if e == 0 else jnp.logical_not(low_lanes)
        return jnp.where(keep, value, jnp.zeros_like(value))

    def first_norm(s):
        def body(r):
            rows = ds(r * R, R)
            normed, _ = norm(xs_buf[s, rows, :].astype(F32))
            a1[s, rows, :] = (normed * prm[s, 2:3, :] + prm[s, 4:5, :]).astype(BF16)

        loop(4, body)
        normed, inv = norm(xs_buf[s, own, :].astype(F32))
        n1[s] = normed
        i1[s] = jnp.broadcast_to(inv, (R, 128))

    def attention(s):
        def body(h):
            b = 2 * h + s
            bias = jnp.concatenate(
                [prm[b, 7:8, 0:128], jnp.zeros((1, 128), F32), prm[b, 7:8, 128:256]], axis=1
            )
            qkv[s, h] = (dot_nn(a1[s], wq[b]) + bias).astype(BF16)
            query, key, value = qkv[s, h, :, 0:128], qkv[s, h, :, 128:256], qkv[s, h, :, 256:384]
            parts = []
            for e in (0, 1):
                scores = dot_nt(pick_head(query, e), key) * SCALE + mask[...]
                weights = jnp.exp(scores - jnp.max(scores, axis=-1, keepdims=True))
                probs = (weights / jnp.sum(weights, axis=-1, keepdims=True)).astype(BF16)
                prob[s, h, e] = probs
                parts.append(dot_nn(probs, value))
            mix[s, h] = jnp.where(low_lanes, parts[0], parts[1]).astype(BF16)

        loop(2, body)

    def partial(k, tile):
        def body(n):
            cols = ds(n * 256, 256)
            value = tile(cols)
            acc[:, cols] = value
            rs_out[k // 2, :, cols] = value.astype(BF16)

        loop(4, body)

    def feed_up(s):
        def body(i):
            h, n = lax.div(i, 2), lax.rem(i, 2)
            b = 2 * h + s
            cols = ds(n * 256, 256)
            u = dot_nn(a2[s], wu[b, :, cols]) + prm[b, 6:7, cols]
            th = jnp.tanh(GELU_COEF * (u + CUBIC_COEF * u * u * u))
            hid[s, h, :, cols] = (0.5 * u * (1.0 + th)).astype(BF16)
            slope[s, h, :, cols] = 0.5 * (1.0 + th) + 0.5 * u * (1.0 - th * th) * GELU_COEF * (
                1.0 + 3.0 * CUBIC_COEF * u * u
            )

        loop(4, body)

    def forward(s, hooks):
        w_forward(s, WQ)
        w_forward(s, WO)
        first_norm(s)
        w_ready(s, WQ)
        attention(s)
        w_ready(s, WO)
        partial(4 * s, lambda cols: dot_nn(mix[s, 0], wo[s, :, cols]) + dot_nn(mix[s, 1], wo[s + 2, :, cols]))
        k = 4 * s
        rs_start(k)
        hooks[0]()
        w_forward(s, WU)
        middle = xs_buf[s, own, :].astype(F32) + rs_finish(k) + prm[s, 0:1, :]
        yrow[...] = middle
        normed, inv = norm(middle)
        n2[s] = normed
        i2[s] = jnp.broadcast_to(inv, (R, 128))
        a2[s, own, :] = (normed * prm[s, 3:4, :] + prm[s, 5:6, :]).astype(BF16)
        ag_start(k + 1, a2.at[s])
        w_forward(s, WD)
        w_ready(s, WU)
        ag_finish(k + 1, a2.at[s])
        feed_up(s)
        w_ready(s, WD)
        partial(k + 2, lambda cols: dot_nn(hid[s, 0], wd[s, :, cols]) + dot_nn(hid[s, 1], wd[s + 2, :, cols]))
        rs_start(k + 2)
        result = (yrow[...] + rs_finish(k + 2) + prm[s, 1:2, :]).astype(BF16)
        target = xs_buf.at[1] if s == 0 else xo
        target[own, :] = result
        ag_start(k + 3, target)

    load_x.wait()
    for d in (1, 2, 3):
        send_prm(d).wait_recv()

    forward(0, [lambda: w_send_all(1)])
    ag_finish(3, xs_buf.at[1])
    out_start(0, 0, xs_buf.at[1], so_out)
    forward(1, [lambda: None])
    load_g.wait()

    def backward(s, k, hooks):
        def grad_up_tile(i):
            h, n = lax.div(i, 2), lax.rem(i, 2)
            b = 2 * h + s
            cols = ds(n * 256, 256)
            value = (dot_nt(g_buf[s], wd[b, cols, :]) * slope[s, h, :, cols]).astype(BF16)
            du[h, :, cols] = value

        loop(4, grad_up_tile)
        partial(k, lambda cols: dot_nt(du[0], wu[s, cols, :]) + dot_nt(du[1], wu[s + 2, cols, :]))
        rs_start(k)

        def grad_down(i):
            h, n = lax.div(i, 2), lax.rem(i, 2)
            rows = ds(n * 256, 256)
            gd[s, h, rows, :] = dot_tn(hid[s, h, :, rows], g_buf[s]).astype(BF16)

        loop(4, grad_down)
        gc_start(s, WD)

        def grad_up(i):
            h, n = lax.div(i, 4), lax.rem(i, 4)
            rows = ds(n * 256, 256)
            gu[s, h, rows, :] = dot_tn(a2[s, :, rows], du[h]).astype(BF16)

        loop(8, grad_up)
        gc_start(s, WU)
        for h in (0, 1):
            sm[s, 6:7, h * 512 : h * 512 + 512] = jnp.sum(du[h].astype(F32), axis=0, keepdims=True)
        hooks[0]()

        top = g_buf[s, own, :].astype(F32)
        sm[s, 1:2, :] = jnp.sum(top, axis=0, keepdims=True)
        g_second = rs_finish(k)
        normed = n2[s]
        sm[s, 3:4, :] = jnp.sum(g_second * normed, axis=0, keepdims=True)
        sm[s, 5:6, :] = jnp.sum(g_second, axis=0, keepdims=True)
        dy = top + norm_back(g_second, normed, i2[s, :, 0:1], prm[s, 3:4, :])
        dyrow[...] = dy
        sm[s, 0:1, :] = jnp.sum(dy, axis=0, keepdims=True)
        dyb[s, own, :] = dy.astype(BF16)
        ag_start(k + 1, dyb.at[s])
        hooks[1]()
        ag_finish(k + 1, dyb.at[s])

        def attention_back(h):
            b = 2 * h + s
            go[s, h] = dot_tn(mix[s, h], dyb[s]).astype(BF16)
            grad_mix = dot_nt(dyb[s], wo[b]).astype(BF16)
            query, key, value = qkv[s, h, :, 0:128], qkv[s, h, :, 128:256], qkv[s, h, :, 256:384]
            parts = []
            for e in (0, 1):
                probs = prob[s, h, e]
                wide = probs.astype(F32)
                grad_prob = dot_nt(pick_head(grad_mix, e), value)
                delta = jnp.sum(wide * grad_prob, axis=-1, keepdims=True)
                grad_scores = (wide * (grad_prob - delta) * SCALE).astype(BF16)
                parts.append((dot_nn(grad_scores, key), dot_tn(grad_scores, query), dot_tn(probs, grad_mix)))
            for j in range(3):
                both = jnp.where(low_lanes, parts[0][j], parts[1][j]).astype(BF16)
                dqkv[h, :, j * 128 : j * 128 + 128] = both

        loop(2, attention_back)
        partial(k + 2, lambda cols: dot_nt(dqkv[0], wq[s, cols, :]) + dot_nt(dqkv[1], wq[s + 2, cols, :]))
        rs_start(k + 2)
        gc_start(s, WO)

        def grad_qkv(i):
            h, n = lax.div(i, 4), lax.rem(i, 4)
            rows = ds(n * 256, 256)
            gq[s, h, rows, :] = dot_tn(a1[s, :, rows], dqkv[h]).astype(BF16)

        loop(8, grad_qkv)
        gc_start(s, WQ)
        for h in (0, 1):
            sums = jnp.sum(dqkv[h].astype(F32), axis=0, keepdims=True)
            sm[s, 7:8, h * 256 : h * 256 + 128] = sums[:, 0:128]
            sm[s, 7:8, h * 256 + 128 : h * 256 + 256] = sums[:, 256:384]
        hooks[2]()
        g_first = rs_finish(k + 2)
        normed = n1[s]
        sm[s, 2:3, :] = jnp.sum(g_first * normed, axis=0, keepdims=True)
        sm[s, 4:5, :] = jnp.sum(g_first, axis=0, keepdims=True)
        low = dyrow[...] + norm_back(g_first, normed, i1[s, :, 0:1], prm[s, 2:3, :])
        target = g_buf.at[0] if s == 1 else ig0
        target[own, :] = low.astype(BF16)
        ag_start(k + 3, target)
        hooks[3]()
        ag_finish(k + 3, target)

    def b1_0():
        ag_finish(7, xo)
        out_start(1, 1, xo, so_out)

    def b1_1():
        gy_start(1, WD)

    def b1_2():
        gy_start(1, WU)

    def b1_3():
        gy_start(1, WO)
        gy_start(1, WQ)

    backward(1, 8, [b1_0, b1_1, b1_2, b1_3])
    out_start(2, 1, g_buf.at[0], ig_out)

    def b0_0():
        gz_start(1, WD)

    def b0_1():
        gy_start(0, WD)
        gy_start(0, WU)
        gz_start(1, WU)

    def b0_2():
        gz_start(1, WO)
        gz_start(1, WQ)
        gy_start(0, WO)

    def b0_3():
        gy_start(0, WQ)
        for k in (WD, WU, WO, WQ):
            ga_start(1, k)
        gz_start(0, WD)

    backward(0, 12, [b0_0, b0_1, b0_2, b0_3])
    out_start(3, 0, ig0, ig_out)

    def small_copy(i, src, dst, device):
        return remote(src, dst, sm_s.at[i], sm_r.at[i], device)

    small_y = [small_copy(d - 1, sm, smy.at[d - 1], dev(x, yp(d), z, c)) for d in (1, 2, 3)]
    small_z = [
        small_copy(3 + j, sm2, smz.at[j], dev(x, y, zp(dz), lax.rem(c + dc, 2))) for j, (dz, dc) in enumerate(zc_peers)
    ]
    small_x = [small_copy(10 + d - 1, sm3, smx.at[d - 1], dev(xp(d), y, z, c)) for d in (1, 2, 3)]
    for copy in small_y:
        copy.start()
    gz_start(0, WU)
    for copy in small_y:
        copy.wait_recv()
    sm2[...] = sm[...] + smy[0] + smy[1] + smy[2]
    for copy in small_z:
        copy.start()
    gz_start(0, WO)
    gz_start(0, WQ)
    for copy in small_z:
        copy.wait_recv()
    total = sm2[...]
    for j in range(7):
        total = total + smz[j]
    sm3[...] = total
    for copy in small_x:
        copy.start()
    for k in (WD, WU, WO, WQ):
        ga_start(0, k)
    for copy in small_x:
        copy.wait_recv()
    shared = sm3[p] + smx[0, p] + smx[1, p] + smx[2, p]
    small_out[...] = shared
    up_out[...] = sm3[p, 6:7, ds(h_me * 512, 512)]
    qv_out[0:1, :] = sm3[p, 7:8, pl.ds(pl.multiple_of(h_me * 256, 128), 128)]
    qv_out[1:2, :] = sm3[p, 7:8, pl.ds(pl.multiple_of(h_me * 256 + 128, 128), 128)]

    for s in (0, 1):
        for k in range(4):
            ga_finish(s, k)
    out_finish(0, 0, xs_buf.at[1], so_out)
    out_finish(1, 1, xo, so_out)
    out_finish(2, 1, g_buf.at[0], ig_out)
    out_finish(3, 0, ig0, ig_out)
    for d in (1, 2, 3):
        send_prm(d).wait_send()
        for k in range(4):
            w_send(k, d).wait_send()
    for s in (0, 1):
        for k in range(4):
            @pl.when(p == s)
            def _():
                w_pass(k, 2).wait_send()
                for d in (1, 2, 3):
                    gz_copy(s, k, d).wait_send()
                for j in range(7):
                    ga_copy(s, k, j).wait_send()

            @pl.when(p != s)
            def _():
                for d in (1, 3):
                    w_pass(k, d).wait_send()

            for h in (0, 1):
                gc_copy(s, k, h).wait_send()

                @pl.when(y != 2 * h + s)
                def _():
                    gy_copy(s, k, h).wait_send()

    for k in range(0, 16, 2):
        for d in (1, 2, 3):
            rs_copy(k, d).wait_send()
    for k, ref in ((1, a2.at[0]), (3, xs_buf.at[1]), (5, a2.at[1]), (7, xo), (9, dyb.at[1]), (11, g_buf.at[0]),
                   (13, dyb.at[0]), (15, ig0)):
        for d in (1, 2, 3):
            ag_copy(k, ref, d).wait_send()
    for copy in small_y + small_z + small_x:
        copy.wait_send()


def run(x_in, seg, wq, qvb, wo, outb, wu, upb, wd, downb, gain, shift, og):
    any_spec = pl.BlockSpec(memory_space=pl.ANY)
    vmem = pl.BlockSpec(memory_space=pltpu.VMEM)
    V = pltpu.VMEM
    dma = pltpu.SemaphoreType.DMA
    tokens = x_in.shape[0]

    def kinds(lead, shrink):
        return [V(tuple(lead) + (ROWS[k] // shrink, COLS[k]), BF16) for k in range(4)]

    scratch = kinds((4,), 1)
    scratch += [
        V((4, 8, D), F32), V((SEQ, SEQ), F32),
        V((2, SEQ, D), BF16), V((2, SEQ, D), BF16), V((2, SEQ, D), BF16), V((2, SEQ, D), BF16), V((2, SEQ, D), BF16),
        V((SEQ, D), BF16), V((SEQ, D), BF16),
        V((2, 2, SEQ, 384), BF16), V((2, 2, 2, SEQ, SEQ), BF16), V((2, 2, SEQ, 128), BF16),
        V((2, 2, SEQ, 512), BF16), V((2, 2, SEQ, 512), F32),
        V((2, SEQ, 512), BF16), V((2, SEQ, 384), BF16), V((SEQ, D), F32),
        V((8, SEQ, D), BF16), V((8, 3, R, D), BF16),
        V((2, R, D), F32), V((2, R, D), F32), V((2, R, 128), F32), V((2, R, 128), F32), V((R, D), F32), V((R, D), F32),
    ]
    scratch += kinds((2, 2), 1) + kinds((2, 2), 2) + kinds((3,), 2) + kinds((3,), 8)
    scratch += [V((2, 8, D), F32)] * 3 + [V((3, 2, 8, D), F32), V((7, 2, 8, D), F32), V((3, 2, 8, D), F32)]
    scratch += [
        dma((48,)), dma((48,)), dma((12,)), dma((12,)), dma((12,)), dma((12,)), dma((3,)), dma((3,)), dma((6,)),
        dma((16,)), dma((16,)), dma((16,)), dma((12,)), dma((12,)), dma((12,)), dma((28,)), dma((28,)), dma((4,)),
        dma((13,)), dma((13,)), dma((12,)), dma((12,)), dma((4,)),
    ]
    return pl.pallas_call(
        kernel,
        out_shape=(
            jax.ShapeDtypeStruct((tokens, D), BF16),
            jax.ShapeDtypeStruct((tokens, D), BF16),
            *[jax.ShapeDtypeStruct((ROWS[k], COLS[k]), BF16) for k in range(4)],
            jax.ShapeDtypeStruct((8, D), F32),
            jax.ShapeDtypeStruct((1, 512), F32),
            jax.ShapeDtypeStruct((2, 128), F32),
        ),
        in_specs=[any_spec, vmem, any_spec, vmem, any_spec, vmem, any_spec, vmem, any_spec, vmem, vmem, vmem, any_spec],
        out_specs=(any_spec,) * 6 + (vmem,) * 3,
        scratch_shapes=scratch,
        compiler_params=pltpu.CompilerParams(collective_id=0, has_side_effects=True, vmem_limit_bytes=64 * 1024 * 1024),
    )(x_in, seg, wq, qvb, wo, outb, wu, upb, wd, downb, gain, shift, og)


def on_device(
    section_input, segment_ids, w_qkv, qv_bias, w_out, out_bias, w_up, up_bias, w_down, down_bias, norm_gains,
    norm_shifts, out_grad,
):
    so, ig, gq, go, gu, gd, small, up, qv = run(
        section_input, segment_ids.reshape(-1, SEQ), w_qkv.reshape(D, 384), qv_bias[0], w_out[0], out_bias, w_up[0],
        up_bias, w_down[0], down_bias, norm_gains[0], norm_shifts[0], out_grad,
    )
    return (
        so[None],
        ig[None],
        gq.astype(F32).reshape(1, D, 3, 128),
        qv[None],
        go.astype(F32)[None],
        small[0:1],
        gu.astype(F32)[None],
        up,
        gd.astype(F32)[None],
        small[1:2],
        small[None, 2:4],
        small[None, 4:6],
    )


def solution(mesh):
    placed = (
        P("dp", None),
        P("dp"),
        P("pipe", None, None, "tensor"),
        P("pipe", None, "tensor"),
        P("pipe", "tensor", None),
        P("pipe", None),
        P("pipe", None, "tensor"),
        P("pipe", "tensor"),
        P("pipe", "tensor", None),
        P("pipe", None),
        P("pipe", None, None),
        P("pipe", None, None),
        P("dp", None),
    )
    return jax.shard_map(
        on_device,
        mesh=mesh,
        in_specs=placed,
        out_specs=(
            P("pipe", "dp", None),
            P("pipe", "dp", None),
            P("pipe", None, None, "tensor"),
            P("pipe", None, "tensor"),
            P("pipe", "tensor", None),
            P("pipe", None),
            P("pipe", None, "tensor"),
            P("pipe", "tensor"),
            P("pipe", "tensor", None),
            P("pipe", None),
            P("pipe", None, None),
            P("pipe", None, None),
        ),
        check_vma=False,
    )
```

```python
import jax
import jax.numpy as jnp
from jax import lax
from jax.experimental import pallas as pl
from jax.experimental.pallas import tpu as pltpu
from jax.sharding import PartitionSpec as P

MESH = pl.DeviceIdType.MESH
F32 = jnp.float32
BF16 = jnp.bfloat16

SEQ = 256
D = 1024
R = 64
NORM_EPS = 1e-05
GELU_COEF = 0.7978845608028654
CUBIC_COEF = 0.044715
MASKED_SCORE = -1e30
SCALE = 0.125
WQ, WO, WU, WD = range(4)
ROWS = (1024, 128, 1024, 512)
COLS = (384, 1024, 512, 1024)


def dot_nn(a, b):
    return jnp.dot(a, b, preferred_element_type=F32)


def dot_nt(a, b):
    return lax.dot_general(a, b, (((1,), (1,)), ((), ())), preferred_element_type=F32)


def dot_tn(a, b):
    return lax.dot_general(a, b, (((0,), (0,)), ((), ())), preferred_element_type=F32)


def loop(n, body):
    lax.fori_loop(0, n, lambda i, c: (body(i), c)[1], 0)


def ds(start, size):
    return pl.ds(pl.multiple_of(start, size), size)


def norm(rows):
    centred = rows - jnp.mean(rows, axis=-1, keepdims=True)
    inv = lax.rsqrt(jnp.mean(centred * centred, axis=-1, keepdims=True) + NORM_EPS)
    return centred * inv, inv


def norm_back(grad, normed, inv, gain):
    e = grad * gain
    return inv * (
        e - jnp.mean(e, axis=-1, keepdims=True) - normed * jnp.mean(e * normed, axis=-1, keepdims=True)
    )


def kernel(
    x_in, seg_in, wq_in, qvb_in, wo_in, outb_in, wu_in, upb_in, wd_in, downb_in, gain_in, shift_in, og_in,
    so_out, ig_out, gq_out, go_out, gu_out, gd_out, small_out, up_out, qv_out,
    wq, wo, wu, wd, prm, mask, xs_buf, g_buf, a1, a2, dyb, xo, ig0, qkv, prob, mix, hid, slope, du, dqkv, acc,
    rs_out, rs_in, n1, n2, i1, i2, yrow, dyrow,
    gq, go, gu, gd, cq, co, cu, cd, yq, yo, yu, yd, zq, zo, zu, zd, fq, fo, fu, fd, sm, sm2, sm3, smy, smz, smx,
    x_s, x_r, wy_s, wy_r, wz_s, wz_r, wc_s, wc_r, pr_s, pr_r, loc, gc_s, gc_r, gy_s, gy_r, gz_s, gz_r, ga_s, ga_r, gf_s, gf_r, gl,
    sm_s, sm_r, o_s, o_r, o_l,
):
    p = lax.axis_index("pipe")
    t = lax.axis_index("tensor")
    dp = lax.axis_index("dp")
    h_me, x = lax.div(t, 4), lax.rem(t, 4)
    z, c = lax.div(dp, 2), lax.rem(dp, 2)
    y = h_me * 2 + p

    def dev(xx, yy, zz, cc):
        return {"pipe": lax.rem(yy, 2), "tensor": lax.div(yy, 2) * 4 + xx, "dp": zz * 2 + cc}

    def xp(d):
        return lax.rem(x + d, 4)

    def yp(d):
        return lax.rem(y + d, 4)

    def zp(d):
        return lax.rem(z + d, 4)

    core_peer = dev(x, y, z, 1 - c)

    def remote(src, dst, ss, rs, device):
        return pltpu.make_async_remote_copy(
            src_ref=src, dst_ref=dst, send_sem=ss, recv_sem=rs, device_id=device, device_id_type=MESH
        )

    own = ds(x * R, R)
    w_in = (wq_in, wo_in, wu_in, wd_in)
    w_all = (wq, wo, wu, wd)
    g_all = (gq, go, gu, gd)
    c_all = (cq, co, cu, cd)
    y_all = (yq, yo, yu, yd)
    z_all = (zq, zo, zu, zd)
    fin = (fq, fo, fu, fd)
    g_outs = (gq_out, go_out, gu_out, gd_out)

    zc_peers = [(dz, dc) for dz in range(4) for dc in range(2) if (dz, dc) != (0, 0)]

    barrier = pltpu.get_barrier_semaphore()
    peers = [dev(xp(d), y, z, c) for d in (1, 2, 3)]
    peers += [dev(x, yp(d), z, c) for d in (1, 2, 3)]
    peers += [dev(x, y, zp(dz), lax.rem(c + dc, 2)) for dz, dc in zc_peers]
    for peer in peers:
        pl.semaphore_signal(barrier, inc=1, device_id=peer, device_id_type=MESH)

    load_x = pltpu.make_async_copy(x_in.at[ds(y * SEQ, SEQ)], xs_buf.at[0], loc.at[0])
    load_g = pltpu.make_async_copy(og_in.at[ds(y * SEQ, SEQ)], g_buf.at[1], loc.at[1])
    load_x.start()
    load_g.start()
    load_w = [pltpu.make_async_copy(w_in[k], w_all[k].at[y], loc.at[2 + k]) for k in range(4)]
    for copy in load_w:
        copy.start()

    prm[y] = jnp.zeros((8, D), F32)
    prm[y, 0:1, :] = outb_in[...]
    prm[y, 1:2, :] = downb_in[...]
    prm[y, 2:4, :] = gain_in[...]
    prm[y, 4:6, :] = shift_in[...]
    prm[y, 6:7, 0:512] = upb_in[...]
    prm[y, 7:8, 0:128] = qvb_in[0:1, :]
    prm[y, 7:8, 128:256] = qvb_in[1:2, :]
    sm[...] = jnp.zeros_like(sm)

    pl.semaphore_wait(barrier, len(peers))

    def send_prm(d):
        return remote(prm.at[y], prm.at[y], pr_s.at[d - 1], pr_r.at[d - 1], dev(x, yp(d), z, c))

    for d in (1, 2, 3):
        send_prm(d).start()

    def half_rows(k, which):
        return ds(which * (ROWS[k] // 2), ROWS[k] // 2)

    even = lax.rem(z, 2)

    def quarter_rows(k, which):
        return ds(c * (ROWS[k] // 2) + which * (ROWS[k] // 4), ROWS[k] // 4)

    def eighth_rows(k, which, j):
        q = ROWS[k] // 8
        return ds(c * (ROWS[k] // 2) + which * (2 * q) + j * q, q)

    def w_send(k, d):
        rows = quarter_rows(k, even)
        i = k * 3 + d - 1
        return remote(w_in[k].at[rows], w_all[k].at[y, rows], wy_s.at[i], wy_r.at[i], dev(x, yp(d), z, c))

    def w_side(k, d, j):
        i = (k * 3 + d - 1) * 2 + j
        block = w_all[k].at[lax.rem(y - d + 4, 4), eighth_rows(k, even, j)]
        return remote(block, block, wz_s.at[i], wz_r.at[i], dev(x, y, zp(1 if j == 0 else 3), c))

    def w_pass(k, d, j):
        i = (k * 3 + d - 1) * 3 + j
        rows = quarter_rows(k, even) if j == 0 else eighth_rows(k, 1 - even, j - 1)
        block = w_all[k].at[lax.rem(y - d + 4, 4), rows]
        return remote(block, block, wc_s.at[i], wc_r.at[i], core_peer)

    def w_send_all(s):
        @pl.when(p == s)
        def _():
            for k in range(4):
                for d in (2, 1, 3):
                    w_send(k, d).start()

    def w_each(s, act):
        @pl.when(p == s)
        def _():
            act(2)

        @pl.when(p != s)
        def _():
            act(1)
            act(3)

    def w_spread(s, k):
        def act(d):
            w_send(k, d).wait_recv()
            for j in (0, 1):
                w_side(k, d, j).start()
            w_pass(k, d, 0).start()

        w_each(s, act)

    def w_hand_over(s, k):
        def act(d):
            for j in (0, 1):
                w_side(k, d, j).wait_recv()
                w_pass(k, d, 1 + j).start()

        w_each(s, act)

    def w_ready(s, k):
        @pl.when(p == s)
        def _():
            load_w[k].wait()

        def act(d):
            for j in (0, 1, 2):
                w_pass(k, d, j).wait_recv()

        w_each(s, act)

    def rs_copy(k, d):
        dest = xp(d)
        return remote(
            rs_out.at[k // 2, ds(dest * R, R)], rs_in.at[k // 2, d - 1], x_s.at[k * 3 + d - 1], x_r.at[k * 3 + d - 1],
            dev(dest, y, z, c),
        )

    def rs_start(k):
        for d in (2, 1, 3):
            rs_copy(k, d).start()

    def rs_finish(k):
        total = acc[own, :]
        for d in (1, 3, 2):
            rs_copy(k, d).wait_recv()
            total = total + rs_in[k // 2, d - 1].astype(F32)
        return total

    def ag_copy(k, ref, d):
        return remote(ref.at[own], ref.at[own], x_s.at[k * 3 + d - 1], x_r.at[k * 3 + d - 1], dev(xp(d), y, z, c))

    def ag_start(k, ref):
        for d in (2, 1, 3):
            ag_copy(k, ref, d).start()

    def ag_finish(k, ref):
        for d in (1, 3, 2):
            ag_copy(k, ref, d).wait_recv()

    def out_copy(i, ref, out, d):
        rows = ds(y * SEQ, SEQ)
        j = i * 3 + d - 1
        return remote(ref, out.at[rows], o_s.at[j], o_r.at[j], dev(x, yp(d), z, c))

    def out_local(i, ref, out):
        return pltpu.make_async_copy(ref, out.at[ds(y * SEQ, SEQ)], o_l.at[i])

    def out_start(i, s, ref, out):
        for d in (1, 2, 3):
            @pl.when(lax.rem(y + d, 2) == s)
            def _():
                out_copy(i, ref, out, d).start()

        @pl.when(p == s)
        def _():
            out_local(i, ref, out).start()

    def out_finish(i, s, ref, out):
        for d in (1, 2, 3):
            @pl.when(lax.rem(y + d, 2) == s)
            def _():
                out_copy(i, ref, out, d).wait_send()

        @pl.when(p == s)
        def _():
            out_local(i, ref, out).wait()
            for d in (1, 2, 3):
                out_copy(i, ref, out, d).wait_recv()

    def gc_copy(s, k, h):
        i = (s * 4 + k) * 2 + h
        return remote(g_all[k].at[s, h, half_rows(k, 1 - c)], c_all[k].at[s, h], gc_s.at[i], gc_r.at[i], core_peer)

    def gc_start(s, k):
        for h in (0, 1):
            gc_copy(s, k, h).start()

    def sum_rows(k, target, base, sources, rows):
        step = min(rows, 64)

        def body(r):
            here = pl.ds(pl.multiple_of(base + r * step, 16), step)
            there = pl.ds(pl.multiple_of(r * step, 16), step)
            total = target[here, :].astype(F32)
            for source in sources:
                total = total + source[there, :].astype(F32)
            target[here, :] = total.astype(BF16)

        loop(rows // step, body)

    def gy_copy(s, k, h):
        d = lax.rem(2 * h + s - y + 4, 4)
        i = (s * 4 + k) * 2 + h
        return remote(
            g_all[k].at[s, h, half_rows(k, c)], y_all[k].at[d - 1], gy_s.at[i], gy_r.at[k * 3 + d - 1],
            dev(x, 2 * h + s, z, c),
        )

    def gy_start(s, k):
        for h in (0, 1):
            gc_copy(s, k, h).wait_recv()
            sum_rows(k, g_all[k].at[s, h], c * (ROWS[k] // 2), [c_all[k].at[s, h]], ROWS[k] // 2)

            @pl.when(y != 2 * h + s)
            def _():
                gy_copy(s, k, h).start()

    def piece(k, zz):
        q = ROWS[k] // 8
        return pl.ds(pl.multiple_of(c * (ROWS[k] // 2) + zz * q, 16), q)

    def gz_copy(s, k, d):
        zz = zp(d)
        i = k * 3 + d - 1
        return remote(
            g_all[k].at[s, h_me, piece(k, zz)], z_all[k].at[d - 1], gz_s.at[i], gz_r.at[i], dev(x, y, zz, c)
        )

    def gz_start(s, k):
        @pl.when(p == s)
        def _():
            for d in (1, 2, 3):
                slot = y_all[k].at[d - 1]
                remote(slot, slot, gy_s.at[0], gy_r.at[k * 3 + d - 1], dev(x, yp(d), z, c)).wait_recv()
            sum_rows(
                k, g_all[k].at[s, h_me], c * (ROWS[k] // 2), [y_all[k].at[j] for j in range(3)], ROWS[k] // 2
            )
            for d in (2, 1, 3):
                gz_copy(s, k, d).start()

    def ga_copy(k, d):
        i = k * 3 + d - 1
        block = fin[k].at[piece(k, z)]
        return remote(block, block, ga_s.at[i], ga_r.at[i], dev(x, y, zp(d), c))

    def gf_copy(k):
        rows = half_rows(k, c)
        return remote(fin[k].at[rows], g_outs[k].at[rows], gf_s.at[k], gf_r.at[k], core_peer)

    def gf_local(k):
        rows = half_rows(k, c)
        return pltpu.make_async_copy(fin[k].at[rows], g_outs[k].at[rows], gl.at[k])

    def ga_start(s, k):
        @pl.when(p == s)
        def _():
            q = ROWS[k] // 8
            for d in (1, 3, 2):
                gz_copy(s, k, d).wait_recv()
            rows = piece(k, z)
            total = g_all[k][s, h_me, rows, :].astype(F32)
            for j in range(3):
                total = total + z_all[k][j].astype(F32)
            fin[k][rows, :] = total.astype(BF16)
            for d in (2, 1, 3):
                ga_copy(k, d).start()

    def gf_start(s, k):
        @pl.when(p == s)
        def _():
            for d in (1, 3, 2):
                ga_copy(k, d).wait_recv()
            gf_copy(k).start()
            gf_local(k).start()

    def gf_finish(k):
        gf_local(k).wait()
        gf_copy(k).wait()
        for d in (1, 2, 3):
            ga_copy(k, d).wait_send()

    w_send_all(0)

    seg = seg_in[pl.ds(y, 1), :].astype(F32)
    seg_b = jnp.broadcast_to(seg, (SEQ, SEQ))
    rows_i = lax.broadcasted_iota(jnp.int32, (SEQ, SEQ), 0)
    cols_i = lax.broadcasted_iota(jnp.int32, (SEQ, SEQ), 1)
    mask[...] = jnp.where((rows_i >= cols_i) & (seg_b == seg_b.T), 0.0, MASKED_SCORE)

    low_lanes = lax.broadcasted_iota(jnp.int32, (SEQ, 128), 1) < 64

    def pick_head(value, e):
        keep = low_lanes if e == 0 else jnp.logical_not(low_lanes)
        return jnp.where(keep, value, jnp.zeros_like(value))

    def first_norm(s):
        def body(r):
            rows = ds(r * R, R)
            normed, _ = norm(xs_buf[s, rows, :].astype(F32))
            a1[s, rows, :] = (normed * prm[s, 2:3, :] + prm[s, 4:5, :]).astype(BF16)

        loop(4, body)
        normed, inv = norm(xs_buf[s, own, :].astype(F32))
        n1[s] = normed
        i1[s] = jnp.broadcast_to(inv, (R, 128))

    def attention(s):
        def body(h):
            b = 2 * h + s
            bias = jnp.concatenate(
                [prm[b, 7:8, 0:128], jnp.zeros((1, 128), F32), prm[b, 7:8, 128:256]], axis=1
            )
            qkv[s, h] = (dot_nn(a1[s], wq[b]) + bias).astype(BF16)
            query, key, value = qkv[s, h, :, 0:128], qkv[s, h, :, 128:256], qkv[s, h, :, 256:384]
            parts = []
            for e in (0, 1):
                scores = dot_nt(pick_head(query, e), key) * SCALE + mask[...]
                weights = jnp.exp(scores - jnp.max(scores, axis=-1, keepdims=True))
                probs = (weights / jnp.sum(weights, axis=-1, keepdims=True)).astype(BF16)
                prob[s, h, e] = probs
                parts.append(dot_nn(probs, value))
            mix[s, h] = jnp.where(low_lanes, parts[0], parts[1]).astype(BF16)

        loop(2, body)

    def partial(k, tile):
        def body(n):
            cols = ds(n * 256, 256)
            value = tile(cols)
            acc[:, cols] = value
            rs_out[k // 2, :, cols] = value.astype(BF16)

        loop(4, body)

    def feed_up(s):
        def body(i):
            h, n = lax.div(i, 2), lax.rem(i, 2)
            b = 2 * h + s
            cols = ds(n * 256, 256)
            u = dot_nn(a2[s], wu[b, :, cols]) + prm[b, 6:7, cols]
            th = jnp.tanh(GELU_COEF * (u + CUBIC_COEF * u * u * u))
            hid[s, h, :, cols] = (0.5 * u * (1.0 + th)).astype(BF16)
            slope[s, h, :, cols] = 0.5 * (1.0 + th) + 0.5 * u * (1.0 - th * th) * GELU_COEF * (
                1.0 + 3.0 * CUBIC_COEF * u * u
            )

        loop(4, body)

    def forward(s, hooks):
        hooks[0]()
        first_norm(s)
        w_ready(s, WQ)
        attention(s)
        hooks[4]()
        w_ready(s, WO)
        partial(4 * s, lambda cols: dot_nn(mix[s, 0], wo[s, :, cols]) + dot_nn(mix[s, 1], wo[s + 2, :, cols]))
        k = 4 * s
        rs_start(k)
        hooks[1]()
        middle = xs_buf[s, own, :].astype(F32) + rs_finish(k) + prm[s, 0:1, :]
        yrow[...] = middle
        normed, inv = norm(middle)
        n2[s] = normed
        i2[s] = jnp.broadcast_to(inv, (R, 128))
        a2[s, own, :] = (normed * prm[s, 3:4, :] + prm[s, 5:6, :]).astype(BF16)
        ag_start(k + 1, a2.at[s])
        hooks[2]()
        w_ready(s, WU)
        ag_finish(k + 1, a2.at[s])
        feed_up(s)
        hooks[5]()
        w_ready(s, WD)
        partial(k + 2, lambda cols: dot_nn(hid[s, 0], wd[s, :, cols]) + dot_nn(hid[s, 1], wd[s + 2, :, cols]))
        rs_start(k + 2)
        hooks[3]()
        result = (yrow[...] + rs_finish(k + 2) + prm[s, 1:2, :]).astype(BF16)
        target = xs_buf.at[1] if s == 0 else xo
        target[own, :] = result
        ag_start(k + 3, target)

    load_x.wait()
    for d in (1, 2, 3):
        send_prm(d).wait_recv()

    def f0_0():
        w_spread(0, WQ)
        w_spread(0, WO)
        w_hand_over(0, WQ)

    def f0_1():
        w_send_all(1)
        w_spread(0, WU)

    def f0_2():
        w_hand_over(0, WU)
        w_spread(0, WD)

    def f0_2b():
        w_hand_over(0, WO)

    def f0_3():
        w_spread(1, WQ)
        w_spread(1, WO)

    def f1_0():
        pass

    def f1_1():
        w_hand_over(1, WU)
        w_spread(1, WD)

    def f1_2():
        w_hand_over(1, WD)

    forward(0, [f0_0, f0_1, f0_2, f0_3, f0_2b, lambda: w_hand_over(0, WD)])
    w_hand_over(1, WQ)
    w_hand_over(1, WO)
    w_spread(1, WU)
    ag_finish(3, xs_buf.at[1])
    out_start(0, 0, xs_buf.at[1], so_out)
    forward(1, [f1_0, f1_1, f1_2, f1_0, f1_0, f1_0])
    load_g.wait()

    def backward(s, k, hooks):
        def grad_up_tile(i):
            h, n = lax.div(i, 2), lax.rem(i, 2)
            b = 2 * h + s
            cols = ds(n * 256, 256)
            value = (dot_nt(g_buf[s], wd[b, cols, :]) * slope[s, h, :, cols]).astype(BF16)
            du[h, :, cols] = value

        loop(4, grad_up_tile)
        partial(k, lambda cols: dot_nt(du[0], wu[s, cols, :]) + dot_nt(du[1], wu[s + 2, cols, :]))
        rs_start(k)

        def grad_down(i):
            h, n = lax.div(i, 2), lax.rem(i, 2)
            rows = ds(n * 256, 256)
            gd[s, h, rows, :] = dot_tn(hid[s, h, :, rows], g_buf[s]).astype(BF16)

        loop(4, grad_down)
        gc_start(s, WD)

        def grad_up(i):
            h, n = lax.div(i, 4), lax.rem(i, 4)
            rows = ds(n * 256, 256)
            gu[s, h, rows, :] = dot_tn(a2[s, :, rows], du[h]).astype(BF16)

        loop(8, grad_up)
        gc_start(s, WU)
        for h in (0, 1):
            sm[s, 6:7, h * 512 : h * 512 + 512] = jnp.sum(du[h].astype(F32), axis=0, keepdims=True)
        hooks[0]()

        top = g_buf[s, own, :].astype(F32)
        sm[s, 1:2, :] = jnp.sum(top, axis=0, keepdims=True)
        g_second = rs_finish(k)
        normed = n2[s]
        sm[s, 3:4, :] = jnp.sum(g_second * normed, axis=0, keepdims=True)
        sm[s, 5:6, :] = jnp.sum(g_second, axis=0, keepdims=True)
        dy = top + norm_back(g_second, normed, i2[s, :, 0:1], prm[s, 3:4, :])
        dyrow[...] = dy
        sm[s, 0:1, :] = jnp.sum(dy, axis=0, keepdims=True)
        dyb[s, own, :] = dy.astype(BF16)
        ag_start(k + 1, dyb.at[s])
        hooks[1]()
        ag_finish(k + 1, dyb.at[s])

        def attention_back(h):
            b = 2 * h + s
            go[s, h] = dot_tn(mix[s, h], dyb[s]).astype(BF16)
            grad_mix = dot_nt(dyb[s], wo[b]).astype(BF16)
            query, key, value = qkv[s, h, :, 0:128], qkv[s, h, :, 128:256], qkv[s, h, :, 256:384]
            parts = []
            for e in (0, 1):
                probs = prob[s, h, e]
                wide = probs.astype(F32)
                grad_prob = dot_nt(pick_head(grad_mix, e), value)
                delta = jnp.sum(wide * grad_prob, axis=-1, keepdims=True)
                grad_scores = (wide * (grad_prob - delta) * SCALE).astype(BF16)
                parts.append((dot_nn(grad_scores, key), dot_tn(grad_scores, query), dot_tn(probs, grad_mix)))
            for j in range(3):
                both = jnp.where(low_lanes, parts[0][j], parts[1][j]).astype(BF16)
                dqkv[h, :, j * 128 : j * 128 + 128] = both

        loop(2, attention_back)
        partial(k + 2, lambda cols: dot_nt(dqkv[0], wq[s, cols, :]) + dot_nt(dqkv[1], wq[s + 2, cols, :]))
        rs_start(k + 2)
        gc_start(s, WO)

        def grad_qkv(i):
            h, n = lax.div(i, 4), lax.rem(i, 4)
            rows = ds(n * 256, 256)
            gq[s, h, rows, :] = dot_tn(a1[s, :, rows], dqkv[h]).astype(BF16)

        loop(8, grad_qkv)
        gc_start(s, WQ)
        for h in (0, 1):
            sums = jnp.sum(dqkv[h].astype(F32), axis=0, keepdims=True)
            sm[s, 7:8, h * 256 : h * 256 + 128] = sums[:, 0:128]
            sm[s, 7:8, h * 256 + 128 : h * 256 + 256] = sums[:, 256:384]
        hooks[2]()
        g_first = rs_finish(k + 2)
        normed = n1[s]
        sm[s, 2:3, :] = jnp.sum(g_first * normed, axis=0, keepdims=True)
        sm[s, 4:5, :] = jnp.sum(g_first, axis=0, keepdims=True)
        low = dyrow[...] + norm_back(g_first, normed, i1[s, :, 0:1], prm[s, 2:3, :])
        target = g_buf.at[0] if s == 1 else ig0
        target[own, :] = low.astype(BF16)
        ag_start(k + 3, target)
        hooks[3]()
        ag_finish(k + 3, target)

    def b1_0():
        ag_finish(7, xo)
        out_start(1, 1, xo, so_out)

    def b1_1():
        gy_start(1, WD)

    def b1_2():
        gy_start(1, WU)

    def b1_3():
        gy_start(1, WO)
        gy_start(1, WQ)

    backward(1, 8, [b1_0, b1_1, b1_2, b1_3])
    out_start(2, 1, g_buf.at[0], ig_out)

    def b0_0():
        gz_start(1, WD)

    def b0_1():
        gy_start(0, WD)
        gy_start(0, WU)
        gz_start(1, WU)

    def b0_2():
        gz_start(1, WO)
        gz_start(1, WQ)
        gy_start(0, WO)

    def b0_3():
        gy_start(0, WQ)
        for k in (WD, WU, WO, WQ):
            ga_start(1, k)
        gz_start(0, WD)
        gz_start(0, WU)

    backward(0, 12, [b0_0, b0_1, b0_2, b0_3])
    out_start(3, 0, ig0, ig_out)

    def small_copy(i, src, dst, device):
        return remote(src, dst, sm_s.at[i], sm_r.at[i], device)

    small_y = [small_copy(d - 1, sm, smy.at[d - 1], dev(x, yp(d), z, c)) for d in (1, 2, 3)]
    small_z = [
        small_copy(3 + j, sm2, smz.at[j], dev(x, y, zp(dz), lax.rem(c + dc, 2))) for j, (dz, dc) in enumerate(zc_peers)
    ]
    small_x = [small_copy(10 + d - 1, sm3, smx.at[d - 1], dev(xp(d), y, z, c)) for d in (1, 2, 3)]
    for copy in small_y:
        copy.start()
    for k in (WD, WU, WO, WQ):
        gf_start(1, k)
    for copy in small_y:
        copy.wait_recv()
    sm2[...] = sm[...] + smy[0] + smy[1] + smy[2]
    for copy in small_z:
        copy.start()
    gz_start(0, WO)
    gz_start(0, WQ)
    for copy in small_z:
        copy.wait_recv()
    total = sm2[...]
    for j in range(7):
        total = total + smz[j]
    sm3[...] = total
    for copy in small_x:
        copy.start()
    for k in (WD, WU, WO, WQ):
        ga_start(0, k)
    for copy in small_x:
        copy.wait_recv()
    shared = sm3[p] + smx[0, p] + smx[1, p] + smx[2, p]
    small_out[...] = shared
    up_out[...] = sm3[p, 6:7, ds(h_me * 512, 512)]
    qv_out[0:1, :] = sm3[p, 7:8, pl.ds(pl.multiple_of(h_me * 256, 128), 128)]
    qv_out[1:2, :] = sm3[p, 7:8, pl.ds(pl.multiple_of(h_me * 256 + 128, 128), 128)]

    for k in (WD, WU, WO, WQ):
        gf_start(0, k)
    for k in range(4):
        gf_finish(k)
    out_finish(0, 0, xs_buf.at[1], so_out)
    out_finish(1, 1, xo, so_out)
    out_finish(2, 1, g_buf.at[0], ig_out)
    out_finish(3, 0, ig0, ig_out)
    for d in (1, 2, 3):
        send_prm(d).wait_send()
        for k in range(4):
            w_send(k, d).wait_send()
    for s in (0, 1):
        for k in range(4):
            @pl.when(p == s)
            def _():
                for d in (1, 2, 3):
                    gz_copy(s, k, d).wait_send()

            def sent(d):
                for j in (0, 1):
                    w_side(k, d, j).wait_send()
                for j in (0, 1, 2):
                    w_pass(k, d, j).wait_send()

            w_each(s, sent)

            for h in (0, 1):
                gc_copy(s, k, h).wait_send()

                @pl.when(y != 2 * h + s)
                def _():
                    gy_copy(s, k, h).wait_send()

    for k in range(0, 16, 2):
        for d in (1, 2, 3):
            rs_copy(k, d).wait_send()
    for k, ref in ((1, a2.at[0]), (3, xs_buf.at[1]), (5, a2.at[1]), (7, xo), (9, dyb.at[1]), (11, g_buf.at[0]),
                   (13, dyb.at[0]), (15, ig0)):
        for d in (1, 2, 3):
            ag_copy(k, ref, d).wait_send()
    for copy in small_y + small_z + small_x:
        copy.wait_send()


def run(x_in, seg, wq, qvb, wo, outb, wu, upb, wd, downb, gain, shift, og):
    any_spec = pl.BlockSpec(memory_space=pl.ANY)
    vmem = pl.BlockSpec(memory_space=pltpu.VMEM)
    V = pltpu.VMEM
    dma = pltpu.SemaphoreType.DMA
    tokens = x_in.shape[0]

    def kinds(lead, shrink):
        return [V(tuple(lead) + (ROWS[k] // shrink, COLS[k]), BF16) for k in range(4)]

    scratch = kinds((4,), 1)
    scratch += [
        V((4, 8, D), F32), V((SEQ, SEQ), F32),
        V((2, SEQ, D), BF16), V((2, SEQ, D), BF16), V((2, SEQ, D), BF16), V((2, SEQ, D), BF16), V((2, SEQ, D), BF16),
        V((SEQ, D), BF16), V((SEQ, D), BF16),
        V((2, 2, SEQ, 384), BF16), V((2, 2, 2, SEQ, SEQ), BF16), V((2, 2, SEQ, 128), BF16),
        V((2, 2, SEQ, 512), BF16), V((2, 2, SEQ, 512), F32),
        V((2, SEQ, 512), BF16), V((2, SEQ, 384), BF16), V((SEQ, D), F32),
        V((8, SEQ, D), BF16), V((8, 3, R, D), BF16),
        V((2, R, D), F32), V((2, R, D), F32), V((2, R, 128), F32), V((2, R, 128), F32), V((R, D), F32), V((R, D), F32),
    ]
    scratch += kinds((2, 2), 1) + kinds((2, 2), 2) + kinds((3,), 2) + kinds((3,), 8) + kinds((), 1)
    scratch += [V((2, 8, D), F32)] * 3 + [V((3, 2, 8, D), F32), V((7, 2, 8, D), F32), V((3, 2, 8, D), F32)]
    scratch += [
        dma((48,)), dma((48,)), dma((12,)), dma((12,)), dma((24,)), dma((24,)), dma((36,)), dma((36,)), dma((3,)), dma((3,)), dma((6,)),
        dma((16,)), dma((16,)), dma((16,)), dma((12,)), dma((12,)), dma((12,)), dma((12,)), dma((12,)), dma((4,)), dma((4,)), dma((4,)),
        dma((13,)), dma((13,)), dma((12,)), dma((12,)), dma((4,)),
    ]
    return pl.pallas_call(
        kernel,
        out_shape=(
            jax.ShapeDtypeStruct((tokens, D), BF16),
            jax.ShapeDtypeStruct((tokens, D), BF16),
            *[jax.ShapeDtypeStruct((ROWS[k], COLS[k]), BF16) for k in range(4)],
            jax.ShapeDtypeStruct((8, D), F32),
            jax.ShapeDtypeStruct((1, 512), F32),
            jax.ShapeDtypeStruct((2, 128), F32),
        ),
        in_specs=[any_spec, vmem, any_spec, vmem, any_spec, vmem, any_spec, vmem, any_spec, vmem, vmem, vmem, any_spec],
        out_specs=(any_spec,) * 6 + (vmem,) * 3,
        scratch_shapes=scratch,
        compiler_params=pltpu.CompilerParams(collective_id=0, has_side_effects=True, vmem_limit_bytes=64 * 1024 * 1024),
    )(x_in, seg, wq, qvb, wo, outb, wu, upb, wd, downb, gain, shift, og)


def on_device(
    section_input, segment_ids, w_qkv, qv_bias, w_out, out_bias, w_up, up_bias, w_down, down_bias, norm_gains,
    norm_shifts, out_grad,
):
    so, ig, gq, go, gu, gd, small, up, qv = run(
        section_input, segment_ids.reshape(-1, SEQ), w_qkv.reshape(D, 384), qv_bias[0], w_out[0], out_bias, w_up[0],
        up_bias, w_down[0], down_bias, norm_gains[0], norm_shifts[0], out_grad,
    )
    return (
        so[None],
        ig[None],
        gq.astype(F32).reshape(1, D, 3, 128),
        qv[None],
        go.astype(F32)[None],
        small[0:1],
        gu.astype(F32)[None],
        up,
        gd.astype(F32)[None],
        small[1:2],
        small[None, 2:4],
        small[None, 4:6],
    )


def solution(mesh):
    placed = (
        P("dp", None),
        P("dp"),
        P("pipe", None, None, "tensor"),
        P("pipe", None, "tensor"),
        P("pipe", "tensor", None),
        P("pipe", None),
        P("pipe", None, "tensor"),
        P("pipe", "tensor"),
        P("pipe", "tensor", None),
        P("pipe", None),
        P("pipe", None, None),
        P("pipe", None, None),
        P("dp", None),
    )
    return jax.shard_map(
        on_device,
        mesh=mesh,
        in_specs=placed,
        out_specs=(
            P("pipe", "dp", None),
            P("pipe", "dp", None),
            P("pipe", None, None, "tensor"),
            P("pipe", None, "tensor"),
            P("pipe", "tensor", None),
            P("pipe", None),
            P("pipe", None, "tensor"),
            P("pipe", "tensor"),
            P("pipe", "tensor", None),
            P("pipe", None),
            P("pipe", None, None),
            P("pipe", None, None),
        ),
        check_vma=False,
    )
```

```python
import jax
import jax.numpy as jnp
from jax import lax
from jax.experimental import pallas as pl
from jax.experimental.pallas import tpu as pltpu
from jax.sharding import PartitionSpec as P

MESH = pl.DeviceIdType.MESH
F32 = jnp.float32
BF16 = jnp.bfloat16

SEQ = 256
D = 1024
HALF = 128
R = 32
NORM_EPS = 1e-05
GELU_COEF = 0.7978845608028654
CUBIC_COEF = 0.044715
MASKED_SCORE = -1e30
SCALE = 0.125
WQ, WO, WU, WD = range(4)
ROWS = (1024, 128, 1024, 512)
COLS = (128, 1024, 512, 1024)
Z_FIRST = (WQ, WU)


def dot_nn(a, b):
    return jnp.dot(a, b, preferred_element_type=F32)


def dot_nt(a, b):
    return lax.dot_general(a, b, (((1,), (1,)), ((), ())), preferred_element_type=F32)


def dot_tn(a, b):
    return lax.dot_general(a, b, (((0,), (0,)), ((), ())), preferred_element_type=F32)


def loop(n, body):
    lax.fori_loop(0, n, lambda i, c: (body(i), c)[1], 0)


def ds(start, size):
    return pl.ds(pl.multiple_of(start, size), size)


def norm(rows):
    centred = rows - jnp.mean(rows, axis=-1, keepdims=True)
    inv = lax.rsqrt(jnp.mean(centred * centred, axis=-1, keepdims=True) + NORM_EPS)
    return centred * inv, inv


def norm_back(grad, normed, inv, gain):
    e = grad * gain
    return inv * (
        e - jnp.mean(e, axis=-1, keepdims=True) - normed * jnp.mean(e * normed, axis=-1, keepdims=True)
    )


def shape_of(k, rows):
    return (3, rows, 128) if k == WQ else (rows, COLS[k])


def at(k, rows):
    return (slice(None), rows) if k == WQ else (rows,)


def kernel(
    x_in, seg_in, wq_in, qvb_in, wo_in, outb_in, wu_in, upb_in, wd_in, downb_in, gain_in, shift_in, og_in,
    so_out, ig_out, gq_out, go_out, gu_out, gd_out, small_out,
    wq, wo, wu, wd, prm, mask, xs_buf, g_buf, a1, a2, dyb, xo, ig0, qkv, prob, mix, hid, slope, du, dqkv, dkv, acc,
    rs_out, rs_in, n1, n2, i1, i2, yrow, dyrow,
    gq, go, gu, gd, cq, co, cu, cd, yq, yo, yu, yd, zq, zo, zu, zd, fq, fo, fu, fd,
    sm, sm1, sm2, sm3, smc, smz, smy, smx,
    x_s, x_r, wy_s, wy_r, wz_s, wz_r, wc_s, wc_r, pr_s, pr_r, loc, gc_s, gc_r, gy_s, gy_r, gz_s, gz_r, ga_s, ga_r,
    gf_s, gf_r, gl, sm_s, sm_r, o_s, o_r, o_l, d_s, d_r, d_l,
):
    p = lax.axis_index("pipe")
    t = lax.axis_index("tensor")
    dp = lax.axis_index("dp")
    h_me, x = lax.div(t, 4), lax.rem(t, 4)
    z, c = lax.div(dp, 2), lax.rem(dp, 2)
    y = h_me * 2 + p

    def dev(xx, yy, zz, cc):
        return {"pipe": lax.rem(yy, 2), "tensor": lax.div(yy, 2) * 4 + xx, "dp": zz * 2 + cc}

    def xp(d):
        return lax.rem(x + d, 4)

    def yp(d):
        return lax.rem(y + d, 4)

    def zp(d):
        return lax.rem(z + d, 4)

    core_peer = dev(x, y, z, 1 - c)

    def remote(src, dst, ss, rs, device):
        return pltpu.make_async_remote_copy(
            src_ref=src, dst_ref=dst, send_sem=ss, recv_sem=rs, device_id=device, device_id_type=MESH
        )

    def stream(u):
        return pl.ds(u * HALF, HALF)

    def own(u):
        return ds(u * HALF + x * R, R)

    w_in = (wq_in, wo_in, wu_in, wd_in)
    w_all = (wq, wo, wu, wd)
    g_all = (gq, go, gu, gd)
    c_all = (cq, co, cu, cd)
    y_all = (yq, yo, yu, yd)
    z_all = (zq, zo, zu, zd)
    fin = (fq, fo, fu, fd)
    g_outs = (gq_out, go_out, gu_out, gd_out)
    grid_peers = [(dx, dy) for dx in range(4) for dy in range(4) if (dx, dy) != (0, 0)]

    barrier = pltpu.get_barrier_semaphore()
    peers = [dev(xp(dx), yp(dy), z, c) for dx, dy in grid_peers]
    peers += [dev(x, y, zp(d), c) for d in (1, 2, 3)] + [core_peer]
    for peer in peers:
        pl.semaphore_signal(barrier, inc=1, device_id=peer, device_id_type=MESH)

    load_x = pltpu.make_async_copy(x_in.at[ds(y * SEQ, SEQ)], xs_buf.at[0], loc.at[0])
    load_g = pltpu.make_async_copy(og_in.at[ds(y * SEQ, SEQ)], g_buf.at[1], loc.at[1])
    load_x.start()
    load_w = [pltpu.make_async_copy(w_in[k], w_all[k].at[y], loc.at[2 + k]) for k in range(4)]
    for copy in load_w:
        copy.start()
    load_g.start()

    prm[y] = jnp.zeros((8, D), F32)
    prm[y, 0:1, :] = outb_in[...]
    prm[y, 1:2, :] = downb_in[...]
    prm[y, 2:4, :] = gain_in[...]
    prm[y, 4:6, :] = shift_in[...]
    prm[y, 6:7, 0:512] = upb_in[...]
    prm[y, 7:8, 0:128] = qvb_in[0:1, :]
    prm[y, 7:8, 128:256] = qvb_in[1:2, :]
    sm[...] = jnp.zeros_like(sm)

    pl.semaphore_wait(barrier, len(peers))

    def send_prm(d):
        return remote(prm.at[y], prm.at[y], pr_s.at[d - 1], pr_r.at[d - 1], dev(x, yp(d), z, c))

    even = lax.rem(z, 2)

    def half_rows(k, which):
        return ds(which * (ROWS[k] // 2), ROWS[k] // 2)

    def quarter_rows(k, which):
        q = ROWS[k] // 4
        return pl.ds(pl.multiple_of(c * (2 * q) + which * q, q), q)

    def eighth_rows(k, which, j):
        q = ROWS[k] // 8
        return pl.ds(pl.multiple_of(c * (4 * q) + which * (2 * q) + j * q, q), q)

    def w_send(k, d):
        rows = at(k, quarter_rows(k, even))
        i = k * 3 + d - 1
        return remote(
            w_in[k].at[rows], w_all[k].at[(y,) + rows], wy_s.at[i], wy_r.at[i], dev(x, yp(d), z, c)
        )

    def w_block(k, d, rows):
        return w_all[k].at[(lax.rem(y - d + 4, 4),) + at(k, rows)]

    def w_side(k, d, j):
        i = (k * 3 + d - 1) * 2 + j
        block = w_block(k, d, eighth_rows(k, even, j))
        return remote(block, block, wz_s.at[i], wz_r.at[i], dev(x, y, zp(1 if j == 0 else 3), c))

    def w_pass(k, d, j):
        i = (k * 3 + d - 1) * 3 + j
        block = w_block(k, d, quarter_rows(k, even) if j == 0 else eighth_rows(k, 1 - even, j - 1))
        return remote(block, block, wc_s.at[i], wc_r.at[i], core_peer)

    def w_send_all(s):
        @pl.when(p == s)
        def _():
            for k in range(4):
                for d in (2, 1, 3):
                    w_send(k, d).start()

    def w_each(s, act):
        @pl.when(p == s)
        def _():
            act(2)

        @pl.when(p != s)
        def _():
            act(1)
            act(3)

    def w_spread(s, k):
        def act(d):
            w_send(k, d).wait_recv()
            for j in (0, 1):
                w_side(k, d, j).start()
            w_pass(k, d, 0).start()

        w_each(s, act)

    def w_hand_over(s, k):
        def act(d):
            for j in (0, 1):
                w_side(k, d, j).wait_recv()
                w_pass(k, d, 1 + j).start()

        w_each(s, act)

    def w_ready(s, k):
        @pl.when(p == s)
        def _():
            load_w[k].wait()

        def act(d):
            for j in (0, 1, 2):
                w_pass(k, d, j).wait_recv()

        w_each(s, act)

    def x_sem(k, u, d):
        return (k * 2 + u) * 3 + d - 1

    def rs_copy(k, u, d):
        dest = xp(d)
        i = x_sem(k, u, d)
        return remote(
            rs_out.at[k // 2, ds(u * HALF + dest * R, R)], rs_in.at[k // 2, u, d - 1], x_s.at[i], x_r.at[i],
            dev(dest, y, z, c),
        )

    def rs_start(k, u):
        for d in (2, 1, 3):
            rs_copy(k, u, d).start()

    def rs_finish(k, u):
        total = acc[own(u), :]
        for d in (1, 3, 2):
            rs_copy(k, u, d).wait_recv()
            total = total + rs_in[k // 2, u, d - 1].astype(F32)
        return total

    def ag_copy(k, u, ref, d):
        i = x_sem(k, u, d)
        block = ref.at[own(u)]
        return remote(block, block, x_s.at[i], x_r.at[i], dev(xp(d), y, z, c))

    def ag_start(k, u, ref):
        for d in (2, 1, 3):
            ag_copy(k, u, ref, d).start()

    def ag_finish(k, u, ref):
        for d in (1, 3, 2):
            ag_copy(k, u, ref, d).wait_recv()

    def out_copy(i, ref, out, d):
        j = i * 3 + d - 1
        return remote(ref, out.at[ds(y * SEQ, SEQ)], o_s.at[j], o_r.at[j], dev(x, yp(d), z, c))

    def out_local(i, ref, out):
        return pltpu.make_async_copy(ref, out.at[ds(y * SEQ, SEQ)], o_l.at[i])

    def out_start(i, s, ref, out):
        for d in (1, 2, 3):
            @pl.when(lax.rem(y + d, 2) == s)
            def _():
                out_copy(i, ref, out, d).start()

        @pl.when(p == s)
        def _():
            out_local(i, ref, out).start()

    def out_finish(i, s, ref, out):
        for d in (1, 2, 3):
            @pl.when(lax.rem(y + d, 2) == s)
            def _():
                out_copy(i, ref, out, d).wait_send()

        @pl.when(p == s)
        def _():
            out_local(i, ref, out).wait()
            for d in (1, 2, 3):
                out_copy(i, ref, out, d).wait_recv()

    def low_rows(u):
        return ds(y * SEQ + u * HALF + x * R, R)

    def low_copy(u, j):
        dx, dy = grid_peers[j]
        i = u * 15 + j
        return remote(ig0.at[own(u)], ig_out.at[low_rows(u)], d_s.at[i], d_r.at[i], dev(xp(dx), yp(dy), z, c))

    def low_local(u):
        return pltpu.make_async_copy(ig0.at[own(u)], ig_out.at[low_rows(u)], d_l.at[u])

    def low_start(u):
        for j, (dx, dy) in enumerate(grid_peers):
            @pl.when(lax.rem(y + dy, 2) == 0)
            def _():
                low_copy(u, j).start()

        @pl.when(p == 0)
        def _():
            low_local(u).start()

    def low_finish(u):
        for j, (dx, dy) in enumerate(grid_peers):
            @pl.when(lax.rem(y + dy, 2) == 0)
            def _():
                low_copy(u, j).wait_send()

        @pl.when(p == 0)
        def _():
            low_local(u).wait()
            for j in range(15):
                low_copy(u, j).wait_recv()

    def gc_copy(s, k, h):
        i = (s * 4 + k) * 2 + h
        return remote(
            g_all[k].at[(s, h) + at(k, half_rows(k, 1 - c))], c_all[k].at[s, h], gc_s.at[i], gc_r.at[i], core_peer
        )

    def gc_start(s, k):
        for h in (0, 1):
            gc_copy(s, k, h).start()

    def sum_rows(k, target, base, sources, rows, result=None):
        step = min(rows, 64)
        result = target if result is None else result

        def body(r):
            here = at(k, pl.ds(pl.multiple_of(base + r * step, 16), step))
            there = at(k, pl.ds(pl.multiple_of(r * step, 16), step))
            total = target[here].astype(F32)
            for source in sources:
                total = total + source[there].astype(F32)
            result[here] = total.astype(BF16)

        loop(rows // step, body)

    def piece_base(k, zz):
        return c * (ROWS[k] // 2) + zz * (ROWS[k] // 8)

    def piece(k, zz):
        return at(k, pl.ds(pl.multiple_of(piece_base(k, zz), 16), ROWS[k] // 8))

    def gy_copy(s, k, h):
        d = lax.rem(2 * h + s - y + 4, 4)
        i = (s * 4 + k) * 2 + h
        rows = piece(k, z) if k in Z_FIRST else at(k, half_rows(k, c))
        return remote(
            g_all[k].at[(s, h) + rows], y_all[k].at[d - 1], gy_s.at[i], gy_r.at[k * 3 + d - 1],
            dev(x, 2 * h + s, z, c),
        )

    def gy_arrived(k):
        for d in (1, 3, 2):
            slot = y_all[k].at[d - 1]
            remote(slot, slot, gy_s.at[0], gy_r.at[k * 3 + d - 1], dev(x, yp(d), z, c)).wait_recv()

    def gy_start(s, k, h):
        @pl.when(y != 2 * h + s)
        def _():
            gy_copy(s, k, h).start()

    def gz_copy(s, k, h, d):
        zz = zp(d)
        i = ((s * 4 + k) * 2 + h) * 3 + d - 1 if k in Z_FIRST else 48 + k * 3 + d - 1
        block = h if k in Z_FIRST else h_me
        slot = z_all[k].at[s, h, d - 1] if k in Z_FIRST else z_all[k].at[d - 1]
        return remote(g_all[k].at[(s, block) + piece(k, zz)], slot, gz_s.at[i], gz_r.at[i], dev(x, y, zz, c))

    def ga_copy(k, d):
        i = k * 3 + d - 1
        block = fin[k].at[piece(k, z)]
        return remote(block, block, ga_s.at[i], ga_r.at[i], dev(x, y, zp(d), c))

    def gf_copy(k):
        rows = at(k, half_rows(k, c))
        return remote(fin[k].at[rows], g_outs[k].at[rows], gf_s.at[k], gf_r.at[k], core_peer)

    def gf_local(k):
        rows = at(k, half_rows(k, c))
        return pltpu.make_async_copy(fin[k].at[rows], g_outs[k].at[rows], gl.at[k])

    def stage1(s, k):
        for h in (0, 1):
            gc_copy(s, k, h).wait_recv()
            sum_rows(k, g_all[k].at[s, h], c * (ROWS[k] // 2), [c_all[k].at[s, h]], ROWS[k] // 2)
            if k in Z_FIRST:
                for d in (2, 1, 3):
                    gz_copy(s, k, h, d).start()
            else:
                gy_start(s, k, h)

    def stage2(s, k):
        q = ROWS[k] // 8
        if k in Z_FIRST:
            for h in (0, 1):
                for d in (1, 3, 2):
                    gz_copy(s, k, h, d).wait_recv()
                sum_rows(k, g_all[k].at[s, h], piece_base(k, z), [z_all[k].at[s, h, j] for j in range(3)], q)
                gy_start(s, k, h)
        else:
            @pl.when(p == s)
            def _():
                gy_arrived(k)
                sum_rows(
                    k, g_all[k].at[s, h_me], c * (4 * q), [y_all[k].at[j] for j in range(3)], 4 * q
                )
                for d in (2, 1, 3):
                    gz_copy(s, k, 0, d).start()

    def stage3(s, k):
        @pl.when(p == s)
        def _():
            if k in Z_FIRST:
                gy_arrived(k)
                slots = [y_all[k].at[j] for j in range(3)]
            else:
                for d in (1, 3, 2):
                    gz_copy(s, k, 0, d).wait_recv()
                slots = [z_all[k].at[j] for j in range(3)]
            sum_rows(k, g_all[k].at[s, h_me], piece_base(k, z), slots, ROWS[k] // 8, fin[k])
            for d in (2, 1, 3):
                ga_copy(k, d).start()

    def stage4(s, k):
        @pl.when(p == s)
        def _():
            for d in (1, 3, 2):
                ga_copy(k, d).wait_recv()
            gf_copy(k).start()
            gf_local(k).start()

    def gf_finish(k):
        gf_local(k).wait()
        gf_copy(k).wait()
        for d in (1, 2, 3):
            ga_copy(k, d).wait_send()

    w_send_all(0)
    for d in (1, 2, 3):
        send_prm(d).start()

    seg = jnp.concatenate([seg_in[pl.ds(2 * y, 1), :], seg_in[pl.ds(2 * y + 1, 1), :]], axis=1).astype(F32)
    seg_b = jnp.broadcast_to(seg, (SEQ, SEQ))
    rows_i = lax.broadcasted_iota(jnp.int32, (SEQ, SEQ), 0)
    cols_i = lax.broadcasted_iota(jnp.int32, (SEQ, SEQ), 1)
    mask[...] = jnp.where((rows_i >= cols_i) & (seg_b == seg_b.T), 0.0, MASKED_SCORE)

    def low_lanes(rows):
        return lax.broadcasted_iota(jnp.int32, (rows, 128), 1) < 64

    def pick_head(value, e):
        keep = low_lanes(value.shape[0])
        keep = keep if e == 0 else jnp.logical_not(keep)
        return jnp.where(keep, value, jnp.zeros_like(value))

    def planes(b, rows):
        return jnp.concatenate([wq[b, 0, rows, :], wq[b, 1, rows, :], wq[b, 2, rows, :]], axis=1)

    def first_norm(s, u):
        def body(r):
            rows = ds(u * HALF + r * 64, 64)
            normed, _ = norm(xs_buf[s, rows, :].astype(F32))
            a1[s, rows, :] = (normed * prm[s, 2:3, :] + prm[s, 4:5, :]).astype(BF16)

        loop(2, body)

    def first_own(s, u):
        normed, inv = norm(xs_buf[s, own(u), :].astype(F32))
        n1[s, u] = normed
        i1[s, u] = jnp.broadcast_to(inv, (R, 128))

    def attention(s, u):
        keys = (u + 1) * HALF
        rows = stream(u)

        def body(h):
            b = 2 * h + s
            bias = jnp.concatenate(
                [prm[b, 7:8, 0:128], jnp.zeros((1, 128), F32), prm[b, 7:8, 128:256]], axis=1
            )
            qkv[s, h, rows, :] = (dot_nn(a1[s, rows, :], planes(b, slice(None))) + bias).astype(BF16)
            query = qkv[s, h, rows, 0:128]
            key, value = qkv[s, h, 0:keys, 128:256], qkv[s, h, 0:keys, 256:384]
            parts = []
            for e in (0, 1):
                scores = dot_nt(pick_head(query, e), key) * SCALE + mask[rows, 0:keys]
                weights = jnp.exp(scores - jnp.max(scores, axis=-1, keepdims=True))
                probs = (weights / jnp.sum(weights, axis=-1, keepdims=True)).astype(BF16)
                prob[s, h, e, rows, 0:keys] = probs
                parts.append(dot_nn(probs, value))
            mix[s, h, rows, :] = jnp.where(low_lanes(HALF), parts[0], parts[1]).astype(BF16)

        loop(2, body)

    def partial(k, u, tile):
        rows = stream(u)

        def body(n):
            cols = ds(n * 256, 256)
            value = tile(rows, cols)
            acc[rows, cols] = value
            rs_out[k // 2, rows, cols] = value.astype(BF16)

        loop(4, body)
        rs_start(k, u)

    def feed_up(s, u):
        rows = stream(u)

        def body(i):
            h, n = lax.div(i, 2), lax.rem(i, 2)
            b = 2 * h + s
            cols = ds(n * 256, 256)
            v = dot_nn(a2[s, rows, :], wu[b, :, cols]) + prm[b, 6:7, cols]
            th = jnp.tanh(GELU_COEF * (v + CUBIC_COEF * v * v * v))
            hid[s, h, rows, cols] = (0.5 * v * (1.0 + th)).astype(BF16)
            slope[s, h, rows, cols] = 0.5 * (1.0 + th) + 0.5 * v * (1.0 - th * th) * GELU_COEF * (
                1.0 + 3.0 * CUBIC_COEF * v * v
            )

        loop(4, body)

    def forward(s, hooks):
        k = 4 * s
        target = xs_buf.at[1] if s == 0 else xo
        for u in (0, 1):
            if s == 1:
                ag_finish(3, u, xs_buf.at[1])
            first_norm(s, u)
            if u == 0:
                hooks[0]()
                w_ready(s, WQ)
            attention(s, u)
            if u == 0:
                hooks[1]()
                w_ready(s, WO)
            partial(
                k, u,
                lambda rows, cols: dot_nn(mix[s, 0, rows, :], wo[s, :, cols])
                + dot_nn(mix[s, 1, rows, :], wo[s + 2, :, cols]),
            )
        hooks[2]()
        for u in (0, 1):
            first_own(s, u)
            middle = xs_buf[s, own(u), :].astype(F32) + rs_finish(k, u) + prm[s, 0:1, :]
            yrow[u] = middle
            normed, inv = norm(middle)
            a2[s, own(u), :] = (normed * prm[s, 3:4, :] + prm[s, 5:6, :]).astype(BF16)
            ag_start(k + 1, u, a2.at[s])
            n2[s, u] = normed
            i2[s, u] = jnp.broadcast_to(inv, (R, 128))
        hooks[3]()
        w_ready(s, WU)
        for u in (0, 1):
            ag_finish(k + 1, u, a2.at[s])
            feed_up(s, u)
            if u == 0:
                hooks[4]()
                w_ready(s, WD)
            partial(
                k + 2, u,
                lambda rows, cols: dot_nn(hid[s, 0, rows, :], wd[s, :, cols])
                + dot_nn(hid[s, 1, rows, :], wd[s + 2, :, cols]),
            )
        hooks[5]()
        for u in (0, 1):
            target[own(u), :] = (yrow[u] + rs_finish(k + 2, u) + prm[s, 1:2, :]).astype(BF16)
            ag_start(k + 3, u, target)

    load_x.wait()
    for d in (1, 2, 3):
        send_prm(d).wait_recv()

    def f0_0():
        w_spread(0, WQ)
        w_spread(0, WO)
        w_hand_over(0, WQ)

    def f0_1():
        w_hand_over(0, WO)

    def f0_2():
        w_send_all(1)
        w_spread(0, WU)

    def f0_3():
        w_hand_over(0, WU)
        w_spread(0, WD)

    def f0_4():
        w_hand_over(0, WD)

    def f0_5():
        w_spread(1, WQ)
        w_spread(1, WO)

    def f1_0():
        w_hand_over(1, WQ)
        w_hand_over(1, WO)

    def f1_2():
        out_start(0, 0, xs_buf.at[1], so_out)
        w_spread(1, WU)

    def f1_3():
        w_hand_over(1, WU)
        w_spread(1, WD)

    def f1_4():
        w_hand_over(1, WD)

    def nothing():
        pass

    forward(0, [f0_0, f0_1, f0_2, f0_3, f0_4, f0_5])
    forward(1, [f1_0, nothing, f1_2, f1_3, f1_4, nothing])
    load_g.wait()

    def attention_back(s, u):
        rows = stream(u)
        keys = (u + 1) * HALF

        def body(h):
            grad_mix = dot_nt(dyb[s, rows, :], wo[2 * h + s]).astype(BF16)
            query = qkv[s, h, rows, 0:128]
            key, value = qkv[s, h, 0:keys, 128:256], qkv[s, h, 0:keys, 256:384]
            parts = []
            for e in (0, 1):
                probs = prob[s, h, e, rows, 0:keys]
                wide = probs.astype(F32)
                grad_prob = dot_nt(pick_head(grad_mix, e), value)
                delta = jnp.sum(wide * grad_prob, axis=-1, keepdims=True)
                grad_scores = (wide * (grad_prob - delta) * SCALE).astype(BF16)
                parts.append((dot_nn(grad_scores, key), dot_tn(grad_scores, query), dot_tn(probs, grad_mix)))
            dqkv[h, rows, 0:128] = jnp.where(low_lanes(HALF), parts[0][0], parts[1][0]).astype(BF16)
            for j in (1, 2):
                both = jnp.where(low_lanes(keys), parts[0][j], parts[1][j])
                cols = slice(j * 128, j * 128 + 128)
                if u == 1:
                    dqkv[h, rows, cols] = both[HALF:, :].astype(BF16)
                    dkv[h, :, (j - 1) * 128 : j * 128] = both[:HALF, :]
                else:
                    dqkv[h, rows, cols] = (both + dkv[h, :, (j - 1) * 128 : j * 128]).astype(BF16)

        loop(2, body)

    def add_row(s, i, value):
        sm[s, i : i + 1, :] = sm[s, i : i + 1, :] + jnp.sum(value, axis=0, keepdims=True)

    def backward(s, k, hooks):
        for u in (1, 0):
            rows = stream(u)
            if s == 0:
                ag_finish(11, u, g_buf.at[0])

            def grad_up_tile(i):
                h, n = lax.div(i, 2), lax.rem(i, 2)
                cols = ds(n * 256, 256)
                value = dot_nt(g_buf[s, rows, :], wd[2 * h + s, cols, :]) * slope[s, h, rows, cols]
                du[h, rows, cols] = value.astype(BF16)

            loop(4, grad_up_tile)
            partial(
                k, u,
                lambda rows, cols: dot_nt(du[0, rows, :], wu[s, cols, :]) + dot_nt(du[1, rows, :], wu[s + 2, cols, :]),
            )

        def grad_down(i):
            h, n = lax.div(i, 2), lax.rem(i, 2)
            rows = ds(n * 256, 256)
            gd[s, h, rows, :] = dot_tn(hid[s, h, :, rows], g_buf[s]).astype(BF16)

        loop(4, grad_down)
        gc_start(s, WD)
        hooks[0]()
        for u in (1, 0):
            top = g_buf[s, own(u), :].astype(F32)
            g_second = rs_finish(k, u)
            normed = n2[s, u]
            dy = top + norm_back(g_second, normed, i2[s, u, :, 0:1], prm[s, 3:4, :])
            dyb[s, own(u), :] = dy.astype(BF16)
            ag_start(k + 1, u, dyb.at[s])
            dyrow[u] = dy
            add_row(s, 1, top)
            add_row(s, 3, g_second * normed)
            add_row(s, 5, g_second)
            add_row(s, 0, dy)

        def grad_up(i):
            h, n = lax.div(i, 4), lax.rem(i, 4)
            rows = ds(n * 256, 256)
            gu[s, h, rows, :] = dot_tn(a2[s, :, rows], du[h]).astype(BF16)

        loop(8, grad_up)
        gc_start(s, WU)
        for h in (0, 1):
            sm[s, 6:7, h * 512 : h * 512 + 512] = jnp.sum(du[h].astype(F32), axis=0, keepdims=True)
        hooks[1]()
        for u in (1, 0):
            ag_finish(k + 1, u, dyb.at[s])
            attention_back(s, u)
            partial(
                k + 2, u,
                lambda rows, cols: dot_nt(dqkv[0, rows, :], planes(s, cols)) + dot_nt(dqkv[1, rows, :], planes(s + 2, cols)),
            )

        def grad_qkv(i):
            h, n = lax.div(i, 4), lax.rem(i, 4)
            rows = ds(n * 256, 256)
            value = dot_tn(a1[s, :, rows], dqkv[h]).astype(BF16)
            for j in range(3):
                gq[s, h, j, rows, :] = value[:, j * 128 : j * 128 + 128]

        loop(8, grad_qkv)
        gc_start(s, WQ)
        for h in (0, 1):
            go[s, h] = dot_tn(mix[s, h], dyb[s]).astype(BF16)
        gc_start(s, WO)
        for h in (0, 1):
            sums = jnp.sum(dqkv[h].astype(F32), axis=0, keepdims=True)
            sm[s, 7:8, h * 256 : h * 256 + 128] = sums[:, 0:128]
            sm[s, 7:8, h * 256 + 128 : h * 256 + 256] = sums[:, 256:384]
        hooks[2]()
        target = g_buf.at[0] if s == 1 else ig0
        for u in (1, 0):
            g_first = rs_finish(k + 2, u)
            normed = n1[s, u]
            low = dyrow[u] + norm_back(g_first, normed, i1[s, u, :, 0:1], prm[s, 2:3, :])
            target[own(u), :] = low.astype(BF16)
            if s == 1:
                ag_start(k + 3, u, target)
            else:
                low_start(u)
            add_row(s, 2, g_first * normed)
            add_row(s, 4, g_first)
        hooks[3]()

    def b1_0():
        for u in (0, 1):
            ag_finish(7, u, xo)
        out_start(1, 1, xo, so_out)

    def b1_1():
        stage1(1, WD)

    def b1_2():
        stage1(1, WU)

    def b1_3():
        stage1(1, WQ)
        stage1(1, WO)

    backward(1, 8, [b1_0, b1_1, b1_2, b1_3])

    def b0_0():
        out_start(2, 1, g_buf.at[0], ig_out)
        stage2(1, WU)

    def b0_1():
        stage1(0, WD)
        stage2(1, WD)

    def b0_2():
        stage1(0, WU)
        stage1(0, WQ)
        stage1(0, WO)
        stage3(1, WU)
        stage2(1, WQ)
        stage2(1, WO)

    def b0_3():
        pass

    backward(0, 12, [b0_0, b0_1, b0_2, b0_3])

    def small_copy(i, src, dst, device):
        return remote(src, dst, sm_s.at[i], sm_r.at[i], device)

    small_c = [small_copy(0, sm, smc, core_peer)]
    small_z = [small_copy(d, sm1, smz.at[d - 1], dev(x, y, zp(d), c)) for d in (1, 2, 3)]
    small_y = [small_copy(3 + d, sm2, smy.at[d - 1], dev(x, yp(d), z, c)) for d in (1, 2, 3)]
    small_x = [small_copy(6 + d, sm3, smx.at[d - 1], dev(xp(d), y, z, c)) for d in (1, 2, 3)]

    def start_all(copies):
        for copy in copies:
            copy.start()

    def arrived(copies):
        for copy in copies:
            copy.wait_recv()

    start_all(small_c)
    stage3(1, WD)
    stage3(1, WQ)
    arrived(small_c)
    sm1[...] = sm[...] + smc[...]
    start_all(small_z)
    stage3(1, WO)
    stage2(0, WU)
    stage2(0, WQ)
    arrived(small_z)
    sm2[...] = sm1[...] + smz[0] + smz[1] + smz[2]
    start_all(small_y)
    stage2(0, WD)
    stage2(0, WO)
    for k in range(4):
        stage4(1, k)
    arrived(small_y)
    sm3[...] = sm2[...] + smy[0] + smy[1] + smy[2]
    start_all(small_x)
    stage3(0, WU)
    stage3(0, WQ)
    arrived(small_x)
    mine = sm3[p]
    shared = mine + smx[0, p] + smx[1, p] + smx[2, p]
    row = lax.broadcasted_iota(jnp.int32, (8, D), 0)
    small_out[...] = jnp.where(row < 6, shared, mine)
    stage3(0, WD)
    stage3(0, WO)
    for k in (WU, WQ, WD, WO):
        stage4(0, k)
    for k in (WU, WQ, WD, WO):
        gf_finish(k)

    out_finish(0, 0, xs_buf.at[1], so_out)
    out_finish(1, 1, xo, so_out)
    out_finish(2, 1, g_buf.at[0], ig_out)
    for u in (1, 0):
        low_finish(u)
    for d in (1, 2, 3):
        send_prm(d).wait_send()
        for k in range(4):
            w_send(k, d).wait_send()
    for s in (0, 1):
        for k in range(4):
            if k not in Z_FIRST:
                @pl.when(p == s)
                def _():
                    for d in (1, 2, 3):
                        gz_copy(s, k, 0, d).wait_send()

            def sent(d):
                for j in (0, 1):
                    w_side(k, d, j).wait_send()
                for j in (0, 1, 2):
                    w_pass(k, d, j).wait_send()

            w_each(s, sent)

            for h in (0, 1):
                gc_copy(s, k, h).wait_send()
                if k in Z_FIRST:
                    for d in (1, 2, 3):
                        gz_copy(s, k, h, d).wait_send()

                @pl.when(y != 2 * h + s)
                def _():
                    gy_copy(s, k, h).wait_send()

    gathered = {
        1: a2.at[0], 3: xs_buf.at[1], 5: a2.at[1], 7: xo, 9: dyb.at[1], 11: g_buf.at[0], 13: dyb.at[0],
    }
    for u in (0, 1):
        for d in (1, 2, 3):
            for k in range(0, 16, 2):
                rs_copy(k, u, d).wait_send()
            for k, ref in gathered.items():
                ag_copy(k, u, ref, d).wait_send()
    for copy in small_c + small_z + small_y + small_x:
        copy.wait_send()


def finish_kernel(
    so_in, ig_in, gq_in, go_in, gu_in, gd_in, small_in,
    so_out, ig_out, gq_out, go_out, gu_out, gd_out, outb, downb, gains, shifts, upb, qvb,
    so_buf, ig_buf, gq_buf, go_buf, gu_buf, gd_buf, gq_f, go_f, gu_f, gd_f, l_sem, s_sem,
):
    ins = (gu_in, gd_in, so_in, ig_in, gq_in, go_in)
    bufs = (gu_buf, gd_buf, so_buf, ig_buf, gq_buf, go_buf)
    wide = (gu_f, gd_f, None, None, gq_f, go_f)
    outs = (gu_out, gd_out, so_out, ig_out, gq_out, go_out)
    loads = [pltpu.make_async_copy(ins[i], bufs[i], l_sem.at[i]) for i in range(6)]
    for copy in loads:
        copy.start()
    h = lax.div(lax.axis_index("tensor"), 4)
    outb[...] = small_in[0:1, :]
    downb[...] = small_in[1:2, :]
    gains[...] = small_in[2:4, :]
    shifts[...] = small_in[4:6, :]
    upb[...] = jnp.where(h == 0, small_in[6:7, 0:512], small_in[6:7, 512:1024])
    qvb[0:1, :] = jnp.where(h == 0, small_in[7:8, 0:128], small_in[7:8, 256:384])
    qvb[1:2, :] = jnp.where(h == 0, small_in[7:8, 128:256], small_in[7:8, 384:512])
    stores = []
    for i in range(6):
        loads[i].wait()
        source = bufs[i]
        if wide[i] is not None:
            source = wide[i]
            lead = source.shape[0]
            step = lead if len(source.shape) == 3 else 64

            def body(r):
                if len(source.shape) == 3:
                    rows = ds(r * 128, 128)
                    wide[i][:, rows, :] = bufs[i][:, rows, :].astype(F32)
                else:
                    rows = ds(r * 64, 64)
                    wide[i][rows, :] = bufs[i][rows, :].astype(F32)

            loop(8 if len(source.shape) == 3 else lead // step, body)
        stores.append(pltpu.make_async_copy(source, outs[i], s_sem.at[i]))
        stores[-1].start()
    for copy in stores:
        copy.wait()


def run(x_in, seg, wq, qvb, wo, outb, wu, upb, wd, downb, gain, shift, og):
    any_spec = pl.BlockSpec(memory_space=pl.ANY)
    vmem = pl.BlockSpec(memory_space=pltpu.VMEM)
    V = pltpu.VMEM
    dma = pltpu.SemaphoreType.DMA
    tokens = x_in.shape[0]

    def kinds(lead, shrink):
        return [V(tuple(lead) + shape_of(k, ROWS[k] // shrink), BF16) for k in range(4)]

    scratch = kinds((4,), 1)
    scratch += [
        V((4, 8, D), F32), V((SEQ, SEQ), F32),
        V((2, SEQ, D), BF16), V((2, SEQ, D), BF16), V((2, SEQ, D), BF16), V((2, SEQ, D), BF16), V((2, SEQ, D), BF16),
        V((SEQ, D), BF16), V((SEQ, D), BF16),
        V((2, 2, SEQ, 384), BF16), V((2, 2, 2, SEQ, SEQ), BF16), V((2, 2, SEQ, 128), BF16),
        V((2, 2, SEQ, 512), BF16), V((2, 2, SEQ, 512), F32),
        V((2, SEQ, 512), BF16), V((2, SEQ, 384), BF16), V((2, HALF, 256), F32), V((SEQ, D), F32),
        V((8, SEQ, D), BF16), V((8, 2, 3, R, D), BF16),
        V((2, 2, R, D), F32), V((2, 2, R, D), F32), V((2, 2, R, 128), F32), V((2, 2, R, 128), F32),
        V((2, R, D), F32), V((2, R, D), F32),
    ]
    scratch += kinds((2, 2), 1) + kinds((2, 2), 2)
    scratch += [V((3,) + shape_of(k, ROWS[k] // (8 if k in Z_FIRST else 2)), BF16) for k in range(4)]
    scratch += [V(((2, 2, 3) if k in Z_FIRST else (3,)) + shape_of(k, ROWS[k] // 8), BF16) for k in range(4)]
    scratch += kinds((), 1)
    scratch += [V((2, 8, D), F32)] * 5 + [V((3, 2, 8, D), F32)] * 3
    sems = (96, 96, 12, 12, 24, 24, 36, 36, 3, 3, 6, 16, 16, 16, 12, 60, 60, 12, 12, 4, 4, 4, 10, 10, 9, 9, 3, 30, 30, 2)
    scratch += [dma((n,)) for n in sems]
    grads = [jax.ShapeDtypeStruct(shape_of(k, ROWS[k]), BF16) for k in range(4)]
    rows = jax.ShapeDtypeStruct((tokens, D), BF16)
    parts = pl.pallas_call(
        kernel,
        out_shape=(rows, rows, *grads, jax.ShapeDtypeStruct((8, D), F32)),
        in_specs=[any_spec, vmem, any_spec, vmem, any_spec, vmem, any_spec, vmem, any_spec, vmem, vmem, vmem, any_spec],
        out_specs=(any_spec,) * 6 + (vmem,),
        scratch_shapes=scratch,
        compiler_params=pltpu.CompilerParams(collective_id=0, has_side_effects=True, vmem_limit_bytes=64 * 1024 * 1024),
    )(x_in, seg, wq, qvb, wo, outb, wu, upb, wd, downb, gain, shift, og)

    def f32(*shape):
        return jax.ShapeDtypeStruct(shape, F32)

    return pl.pallas_call(
        finish_kernel,
        out_shape=(
            rows, rows, *[f32(*shape_of(k, ROWS[k])) for k in range(4)],
            f32(1, D), f32(1, D), f32(2, D), f32(2, D), f32(1, 512), f32(2, 128),
        ),
        in_specs=[any_spec] * 6 + [vmem],
        out_specs=(any_spec,) * 6 + (vmem,) * 6,
        scratch_shapes=[
            V((tokens, D), BF16), V((tokens, D), BF16), *kinds((), 1),
            *[V(shape_of(k, ROWS[k]), F32) for k in range(4)], dma((6,)), dma((6,)),
        ],
        compiler_params=pltpu.CompilerParams(vmem_limit_bytes=48 * 1024 * 1024),
    )(*parts)


def on_device(
    section_input, segment_ids, w_qkv, qv_bias, w_out, out_bias, w_up, up_bias, w_down, down_bias, norm_gains,
    norm_shifts, out_grad,
):
    so, ig, gq, go, gu, gd, outb, downb, gains, shifts, upb, qvb = run(
        section_input, segment_ids.reshape(8, 128), w_qkv[0].transpose(1, 0, 2), qv_bias[0], w_out[0], out_bias,
        w_up[0], up_bias, w_down[0], down_bias, norm_gains[0], norm_shifts[0], out_grad,
    )
    return (
        so[None], ig[None], gq.transpose(1, 0, 2)[None], qvb[None], go[None], outb, gu[None], upb, gd[None], downb,
        gains[None], shifts[None],
    )


def solution(mesh):
    placed = (
        P("dp", None),
        P("dp"),
        P("pipe", None, None, "tensor"),
        P("pipe", None, "tensor"),
        P("pipe", "tensor", None),
        P("pipe", None),
        P("pipe", None, "tensor"),
        P("pipe", "tensor"),
        P("pipe", "tensor", None),
        P("pipe", None),
        P("pipe", None, None),
        P("pipe", None, None),
        P("dp", None),
    )
    return jax.shard_map(
        on_device,
        mesh=mesh,
        in_specs=placed,
        out_specs=(
            P("pipe", "dp", None),
            P("pipe", "dp", None),
            P("pipe", None, None, "tensor"),
            P("pipe", None, "tensor"),
            P("pipe", "tensor", None),
            P("pipe", None),
            P("pipe", None, "tensor"),
            P("pipe", "tensor"),
            P("pipe", "tensor", None),
            P("pipe", None),
            P("pipe", None, None),
            P("pipe", None, None),
        ),
        check_vma=False,
    )
```

```python
import jax
import jax.numpy as jnp
from jax import lax
from jax.experimental import pallas as pl
from jax.experimental.pallas import tpu as pltpu
from jax.sharding import PartitionSpec as P

MESH = pl.DeviceIdType.MESH
F32 = jnp.float32
BF16 = jnp.bfloat16

SEQ = 256
D = 1024
HALF = 128
R = 32
NORM_EPS = 1e-05
GELU_COEF = 0.7978845608028654
CUBIC_COEF = 0.044715
MASKED_SCORE = -1e30
SCALE = 0.125
WQ, WO, WU, WD = range(4)
ROWS = (1024, 128, 1024, 512)
COLS = (128, 1024, 512, 1024)
Z_FIRST = (WQ, WU)


def dot_nn(a, b):
    return jnp.dot(a, b, preferred_element_type=F32)


def dot_nt(a, b):
    return lax.dot_general(a, b, (((1,), (1,)), ((), ())), preferred_element_type=F32)


def dot_tn(a, b):
    return lax.dot_general(a, b, (((0,), (0,)), ((), ())), preferred_element_type=F32)


def loop(n, body):
    lax.fori_loop(0, n, lambda i, c: (body(i), c)[1], 0)


def ds(start, size):
    return pl.ds(pl.multiple_of(start, size), size)


def norm(rows):
    centred = rows - jnp.mean(rows, axis=-1, keepdims=True)
    inv = lax.rsqrt(jnp.mean(centred * centred, axis=-1, keepdims=True) + NORM_EPS)
    return centred * inv, inv


def norm_back(grad, normed, inv, gain):
    e = grad * gain
    return inv * (
        e - jnp.mean(e, axis=-1, keepdims=True) - normed * jnp.mean(e * normed, axis=-1, keepdims=True)
    )


def shape_of(k, rows):
    return (3, rows, 128) if k == WQ else (rows, COLS[k])


def at(k, rows):
    return (slice(None), rows) if k == WQ else (rows,)


def kernel(
    x_in, seg_in, wq_in, qvb_in, wo_in, outb_in, wu_in, upb_in, wd_in, downb_in, gain_in, shift_in, og_in,
    so_out, ig_out, gq_out, go_out, gu_out, gd_out, small_out,
    wq, wo, wu, wd, prm, mask, xs_buf, g_buf, a1, a2, dyb, xo, ig0, qkv, prob, mix, hid, slope, du, dqkv, dkv, acc,
    rs_out, rs_in, n1, n2, i1, i2, yrow, dyrow,
    gq, go, gu, gd, cq, co, cu, cd, yq, yo, yu, yd, rq, ro, ru, rd, zq, zo, zu, zd, fq, fo, fu, fd,
    sm, sm1, sm2, sm3, smc, smz, smy, smx,
    x_s, x_r, wy_s, wy_r, wz_s, wz_r, wc_s, wc_r, wr_s, wr_r, pr_s, pr_r, loc, gc_s, gc_r, gy_s, gy_r, ry_s, ry_r, gz_s, gz_r, ga_s, ga_r,
    gf_s, gf_r, gl, sm_s, sm_r, o_s, o_r, o_l, d_s, d_r, d_l,
):
    p = lax.axis_index("pipe")
    t = lax.axis_index("tensor")
    dp = lax.axis_index("dp")
    h_me, x = lax.div(t, 4), lax.rem(t, 4)
    z, c = lax.div(dp, 2), lax.rem(dp, 2)
    y = h_me * 2 + p

    def dev(xx, yy, zz, cc):
        return {"pipe": lax.rem(yy, 2), "tensor": lax.div(yy, 2) * 4 + xx, "dp": zz * 2 + cc}

    def xp(d):
        return lax.rem(x + d, 4)

    def yp(d):
        return lax.rem(y + d, 4)

    def zp(d):
        return lax.rem(z + d, 4)

    core_peer = dev(x, y, z, 1 - c)

    def remote(src, dst, ss, rs, device):
        return pltpu.make_async_remote_copy(
            src_ref=src, dst_ref=dst, send_sem=ss, recv_sem=rs, device_id=device, device_id_type=MESH
        )

    def stream(u):
        return pl.ds(u * HALF, HALF)

    def own(u):
        return ds(u * HALF + x * R, R)

    w_in = (wq_in, wo_in, wu_in, wd_in)
    w_all = (wq, wo, wu, wd)
    g_all = (gq, go, gu, gd)
    c_all = (cq, co, cu, cd)
    y_all = (yq, yo, yu, yd)
    z_all = (zq, zo, zu, zd)
    r_all = (rq, ro, ru, rd)
    fin = (fq, fo, fu, fd)
    g_outs = (gq_out, go_out, gu_out, gd_out)
    grid_peers = [(dx, dy) for dx in range(4) for dy in range(4) if (dx, dy) != (0, 0)]

    barrier = pltpu.get_barrier_semaphore()
    peers = [dev(xp(dx), yp(dy), z, c) for dx, dy in grid_peers]
    peers += [dev(x, y, zp(d), c) for d in (1, 2, 3)] + [core_peer]
    for peer in peers:
        pl.semaphore_signal(barrier, inc=1, device_id=peer, device_id_type=MESH)

    load_x = pltpu.make_async_copy(x_in.at[ds(y * SEQ, SEQ)], xs_buf.at[0], loc.at[0])
    load_g = pltpu.make_async_copy(og_in.at[ds(y * SEQ, SEQ)], g_buf.at[1], loc.at[1])
    load_x.start()
    load_w = [pltpu.make_async_copy(w_in[k], w_all[k].at[y], loc.at[2 + k]) for k in range(4)]
    for copy in load_w:
        copy.start()
    load_g.start()

    prm[y] = jnp.zeros((8, D), F32)
    prm[y, 0:1, :] = outb_in[...]
    prm[y, 1:2, :] = downb_in[...]
    prm[y, 2:4, :] = gain_in[...]
    prm[y, 4:6, :] = shift_in[...]
    prm[y, 6:7, 0:512] = upb_in[...]
    prm[y, 7:8, 0:128] = qvb_in[0:1, :]
    prm[y, 7:8, 128:256] = qvb_in[1:2, :]
    sm[...] = jnp.zeros_like(sm)

    pl.semaphore_wait(barrier, len(peers))

    def send_prm(d):
        return remote(prm.at[y], prm.at[y], pr_s.at[d - 1], pr_r.at[d - 1], dev(x, yp(d), z, c))

    even = lax.rem(z, 2)

    def half_rows(k, which):
        return ds(which * (ROWS[k] // 2), ROWS[k] // 2)

    def quarter_rows(k, which):
        q = ROWS[k] // 4
        return pl.ds(pl.multiple_of(c * (2 * q) + which * q, q), q)

    def eighth_rows(k, which, j):
        q = ROWS[k] // 8
        return pl.ds(pl.multiple_of(c * (4 * q) + which * (2 * q) + j * q, q), q)

    def w_send(k, d):
        rows = at(k, quarter_rows(k, even))
        i = k * 3 + d - 1
        return remote(
            w_in[k].at[rows], w_all[k].at[(y,) + rows], wy_s.at[i], wy_r.at[i], dev(x, yp(d), z, c)
        )

    def w_block(k, d, rows):
        return w_all[k].at[(lax.rem(y - d + 4, 4),) + at(k, rows)]

    def w_side(k, d, j):
        i = (k * 3 + d - 1) * 2 + j
        block = w_block(k, d, eighth_rows(k, even, j))
        return remote(block, block, wz_s.at[i], wz_r.at[i], dev(x, y, zp(1 if j == 0 else 3), c))

    def w_pass(k, d, j):
        i = (k * 3 + d - 1) * 3 + j
        block = w_block(k, d, quarter_rows(k, even) if j == 0 else eighth_rows(k, 1 - even, j - 1))
        return remote(block, block, wc_s.at[i], wc_r.at[i], core_peer)

    def w_relay(k, j):
        block = w_block(k, 1 if j == 0 else 3, eighth_rows(k, even, j))
        i = k * 2 + j
        return remote(block, block, wr_s.at[i], wr_r.at[i], dev(x, yp(1 if j == 0 else 3), z, c))

    def w_relayed(k, j):
        block = w_block(k, 2, eighth_rows(k, even, j))
        i = k * 2 + j
        return remote(block, block, wr_s.at[i], wr_r.at[i], dev(x, yp(1 if j == 0 else 3), z, c))

    def w_send_all(s):
        @pl.when(p == s)
        def _():
            for k in range(4):
                for d in (1, 3):
                    w_send(k, d).start()

    def w_each(s, act):
        @pl.when(p == s)
        def _():
            act(2)

        @pl.when(p != s)
        def _():
            act(1)
            act(3)

    def w_spread(s, k):
        def act(d):
            if d == 2:
                w_relayed(k, 0).wait_recv()
                w_side(k, d, 0).start()
                w_relayed(k, 1).wait_recv()
                w_side(k, d, 1).start()
            else:
                w_send(k, d).wait_recv()
                w_relay(k, 0 if d == 1 else 1).start()
                for j in (0, 1):
                    w_side(k, d, j).start()
            w_pass(k, d, 0).start()

        w_each(s, act)

    def w_hand_over(s, k):
        def act(d):
            for j in (0, 1):
                w_side(k, d, j).wait_recv()
                w_pass(k, d, 1 + j).start()

        w_each(s, act)

    def w_ready(s, k):
        @pl.when(p == s)
        def _():
            load_w[k].wait()

        def act(d):
            for j in (0, 1, 2):
                w_pass(k, d, j).wait_recv()

        w_each(s, act)

    def x_sem(k, u, d):
        return (k * 2 + u) * 3 + d - 1

    def rs_copy(k, u, d):
        dest = xp(d)
        i = x_sem(k, u, d)
        return remote(
            rs_out.at[k // 2, ds(u * HALF + dest * R, R)], rs_in.at[k // 2, u, d - 1], x_s.at[i], x_r.at[i],
            dev(dest, y, z, c),
        )

    def rs_start(k, u):
        for d in (2, 1, 3):
            rs_copy(k, u, d).start()

    def rs_finish(k, u):
        total = acc[own(u), :]
        for d in (1, 3, 2):
            rs_copy(k, u, d).wait_recv()
            total = total + rs_in[k // 2, u, d - 1].astype(F32)
        return total

    def ag_copy(k, u, ref, d):
        i = x_sem(k, u, d)
        block = ref.at[own(u)]
        return remote(block, block, x_s.at[i], x_r.at[i], dev(xp(d), y, z, c))

    def ag_start(k, u, ref):
        for d in (2, 1, 3):
            ag_copy(k, u, ref, d).start()

    def ag_finish(k, u, ref):
        for d in (1, 3, 2):
            ag_copy(k, u, ref, d).wait_recv()

    def out_copy(i, ref, out, d):
        j = i * 3 + d - 1
        return remote(ref, out.at[ds(y * SEQ, SEQ)], o_s.at[j], o_r.at[j], dev(x, yp(d), z, c))

    def out_local(i, ref, out):
        return pltpu.make_async_copy(ref, out.at[ds(y * SEQ, SEQ)], o_l.at[i])

    def out_start(i, s, ref, out):
        for d in (1, 2, 3):
            @pl.when(lax.rem(y + d, 2) == s)
            def _():
                out_copy(i, ref, out, d).start()

        @pl.when(p == s)
        def _():
            out_local(i, ref, out).start()

    def out_finish(i, s, ref, out):
        for d in (1, 2, 3):
            @pl.when(lax.rem(y + d, 2) == s)
            def _():
                out_copy(i, ref, out, d).wait_send()

        @pl.when(p == s)
        def _():
            out_local(i, ref, out).wait()
            for d in (1, 2, 3):
                out_copy(i, ref, out, d).wait_recv()

    def low_rows(u):
        return ds(y * SEQ + u * HALF + x * R, R)

    def low_copy(u, j):
        dx, dy = grid_peers[j]
        i = u * 15 + j
        return remote(ig0.at[own(u)], ig_out.at[low_rows(u)], d_s.at[i], d_r.at[i], dev(xp(dx), yp(dy), z, c))

    def low_local(u):
        return pltpu.make_async_copy(ig0.at[own(u)], ig_out.at[low_rows(u)], d_l.at[u])

    def low_start(u):
        for j, (dx, dy) in enumerate(grid_peers):
            @pl.when(lax.rem(y + dy, 2) == 0)
            def _():
                low_copy(u, j).start()

        @pl.when(p == 0)
        def _():
            low_local(u).start()

    def low_finish(u):
        for j, (dx, dy) in enumerate(grid_peers):
            @pl.when(lax.rem(y + dy, 2) == 0)
            def _():
                low_copy(u, j).wait_send()

        @pl.when(p == 0)
        def _():
            low_local(u).wait()
            for j in range(15):
                low_copy(u, j).wait_recv()

    def gc_copy(s, k, h):
        i = (s * 4 + k) * 2 + h
        return remote(
            g_all[k].at[(s, h) + at(k, half_rows(k, 1 - c))], c_all[k].at[s, h], gc_s.at[i], gc_r.at[i], core_peer
        )

    def gc_start(s, k):
        for h in (0, 1):
            gc_copy(s, k, h).start()

    def sum_rows(k, target, base, sources, rows, result=None):
        step = min(rows, 64)
        result = target if result is None else result

        def body(r):
            here = at(k, pl.ds(pl.multiple_of(base + r * step, 16), step))
            there = at(k, pl.ds(pl.multiple_of(r * step, 16), step))
            total = target[here].astype(F32)
            for source in sources:
                total = total + source[there].astype(F32)
            result[here] = total.astype(BF16)

        loop(rows // step, body)

    def piece_base(k, zz):
        return c * (ROWS[k] // 2) + zz * (ROWS[k] // 8)

    def piece(k, zz):
        return at(k, pl.ds(pl.multiple_of(piece_base(k, zz), 16), ROWS[k] // 8))

    def region(k):
        return (piece_base(k, z), ROWS[k] // 8) if k in Z_FIRST else (c * (ROWS[k] // 2), ROWS[k] // 2)

    def y_side(j):
        return yp(1 if j == 0 else 3)

    def relay_copy(s, k, j):
        base, n = region(k)
        rows = at(k, pl.ds(pl.multiple_of(base + j * (n // 2), 16), n // 2))
        i = k * 2 + j
        return remote(
            g_all[k].at[(s, 1 - h_me) + rows], r_all[k].at[j], ry_s.at[i], ry_r.at[i], dev(x, y_side(j), z, c)
        )

    def main_copy(s, k, j):
        base, n = region(k)
        rows = at(k, pl.ds(pl.multiple_of(base, 16), n))
        i = k * 2 + j
        block = lax.div(y_side(j), 2)
        return remote(
            g_all[k].at[(s, block) + rows], y_all[k].at[j], gy_s.at[i], gy_r.at[i], dev(x, y_side(j), z, c)
        )

    def relay_start(s, k):
        @pl.when(p == s)
        def _():
            for j in (0, 1):
                relay_copy(s, k, j).start()

    def main_start(s, k):
        @pl.when(p != s)
        def _():
            base, n = region(k)
            for j in (0, 1):
                relay_copy(s, k, j).wait_recv()
                sum_rows(
                    k, g_all[k].at[s, lax.div(y_side(j), 2)], base + j * (n // 2), [r_all[k].at[j]], n // 2
                )
                main_copy(s, k, j).start()

    def main_arrived(s, k):
        for j in (0, 1):
            main_copy(s, k, j).wait_recv()
        return [y_all[k].at[j] for j in (0, 1)]

    def gz_copy(s, k, h, d):
        zz = zp(d)
        i = ((s * 4 + k) * 2 + h) * 3 + d - 1 if k in Z_FIRST else 48 + k * 3 + d - 1
        block = h if k in Z_FIRST else h_me
        slot = z_all[k].at[s, h, d - 1] if k in Z_FIRST else z_all[k].at[d - 1]
        return remote(g_all[k].at[(s, block) + piece(k, zz)], slot, gz_s.at[i], gz_r.at[i], dev(x, y, zz, c))

    def ga_copy(k, d):
        i = k * 3 + d - 1
        block = fin[k].at[piece(k, z)]
        return remote(block, block, ga_s.at[i], ga_r.at[i], dev(x, y, zp(d), c))

    def gf_copy(k):
        rows = at(k, half_rows(k, c))
        return remote(fin[k].at[rows], g_outs[k].at[rows], gf_s.at[k], gf_r.at[k], core_peer)

    def gf_local(k):
        rows = at(k, half_rows(k, c))
        return pltpu.make_async_copy(fin[k].at[rows], g_outs[k].at[rows], gl.at[k])

    def stage1(s, k):
        for h in (0, 1):
            gc_copy(s, k, h).wait_recv()
            sum_rows(k, g_all[k].at[s, h], c * (ROWS[k] // 2), [c_all[k].at[s, h]], ROWS[k] // 2)
            if k in Z_FIRST:
                for d in (2, 1, 3):
                    gz_copy(s, k, h, d).start()
        if k not in Z_FIRST:
            relay_start(s, k)

    def stage2(s, k):
        if k in Z_FIRST:
            for h in (0, 1):
                for d in (1, 3, 2):
                    gz_copy(s, k, h, d).wait_recv()
                slots = [z_all[k].at[s, h, j] for j in range(3)]
                sum_rows(k, g_all[k].at[s, h], piece_base(k, z), slots, ROWS[k] // 8)
            relay_start(s, k)
        else:
            main_start(s, k)

    def stage3(s, k):
        if k in Z_FIRST:
            main_start(s, k)
        else:
            @pl.when(p == s)
            def _():
                slots = main_arrived(s, k)
                sum_rows(k, g_all[k].at[s, h_me], c * (ROWS[k] // 2), slots, ROWS[k] // 2)
                for d in (2, 1, 3):
                    gz_copy(s, k, 0, d).start()

    def stage4(s, k):
        @pl.when(p == s)
        def _():
            if k in Z_FIRST:
                slots = main_arrived(s, k)
            else:
                for d in (1, 3, 2):
                    gz_copy(s, k, 0, d).wait_recv()
                slots = [z_all[k].at[j] for j in range(3)]
            sum_rows(k, g_all[k].at[s, h_me], piece_base(k, z), slots, ROWS[k] // 8, fin[k])
            for d in (2, 1, 3):
                ga_copy(k, d).start()

    def stage5(s, k):
        @pl.when(p == s)
        def _():
            for d in (1, 3, 2):
                ga_copy(k, d).wait_recv()
            gf_copy(k).start()
            gf_local(k).start()

    def gf_finish(k):
        gf_local(k).wait()
        gf_copy(k).wait()
        for d in (1, 2, 3):
            ga_copy(k, d).wait_send()

    w_send_all(0)
    for d in (1, 2, 3):
        send_prm(d).start()

    seg = jnp.concatenate([seg_in[pl.ds(2 * y, 1), :], seg_in[pl.ds(2 * y + 1, 1), :]], axis=1).astype(F32)
    seg_b = jnp.broadcast_to(seg, (SEQ, SEQ))
    rows_i = lax.broadcasted_iota(jnp.int32, (SEQ, SEQ), 0)
    cols_i = lax.broadcasted_iota(jnp.int32, (SEQ, SEQ), 1)
    mask[...] = jnp.where((rows_i >= cols_i) & (seg_b == seg_b.T), 0.0, MASKED_SCORE)

    def low_lanes(rows):
        return lax.broadcasted_iota(jnp.int32, (rows, 128), 1) < 64

    def pick_head(value, e):
        keep = low_lanes(value.shape[0])
        keep = keep if e == 0 else jnp.logical_not(keep)
        return jnp.where(keep, value, jnp.zeros_like(value))

    def planes(b, rows):
        return jnp.concatenate([wq[b, 0, rows, :], wq[b, 1, rows, :], wq[b, 2, rows, :]], axis=1)

    def first_norm(s, u):
        def body(r):
            rows = ds(u * HALF + r * 64, 64)
            normed, _ = norm(xs_buf[s, rows, :].astype(F32))
            a1[s, rows, :] = (normed * prm[s, 2:3, :] + prm[s, 4:5, :]).astype(BF16)

        loop(2, body)

    def first_own(s, u):
        normed, inv = norm(xs_buf[s, own(u), :].astype(F32))
        n1[s, u] = normed
        i1[s, u] = jnp.broadcast_to(inv, (R, 128))

    def attention(s, u):
        keys = (u + 1) * HALF
        rows = stream(u)

        def body(h):
            b = 2 * h + s
            bias = jnp.concatenate(
                [prm[b, 7:8, 0:128], jnp.zeros((1, 128), F32), prm[b, 7:8, 128:256]], axis=1
            )
            qkv[s, h, rows, :] = (dot_nn(a1[s, rows, :], planes(b, slice(None))) + bias).astype(BF16)
            query = qkv[s, h, rows, 0:128]
            key, value = qkv[s, h, 0:keys, 128:256], qkv[s, h, 0:keys, 256:384]
            parts = []
            for e in (0, 1):
                scores = dot_nt(pick_head(query, e), key) * SCALE + mask[rows, 0:keys]
                weights = jnp.exp(scores - jnp.max(scores, axis=-1, keepdims=True))
                probs = (weights / jnp.sum(weights, axis=-1, keepdims=True)).astype(BF16)
                prob[s, h, e, rows, 0:keys] = probs
                parts.append(dot_nn(probs, value))
            mix[s, h, rows, :] = jnp.where(low_lanes(HALF), parts[0], parts[1]).astype(BF16)

        loop(2, body)

    def partial(k, u, tile):
        rows = stream(u)

        def body(n):
            cols = ds(n * 256, 256)
            value = tile(rows, cols)
            acc[rows, cols] = value
            rs_out[k // 2, rows, cols] = value.astype(BF16)

        loop(4, body)
        rs_start(k, u)

    def feed_up(s, u):
        rows = stream(u)

        def body(i):
            h, n = lax.div(i, 2), lax.rem(i, 2)
            b = 2 * h + s
            cols = ds(n * 256, 256)
            v = dot_nn(a2[s, rows, :], wu[b, :, cols]) + prm[b, 6:7, cols]
            th = jnp.tanh(GELU_COEF * (v + CUBIC_COEF * v * v * v))
            hid[s, h, rows, cols] = (0.5 * v * (1.0 + th)).astype(BF16)
            slope[s, h, rows, cols] = 0.5 * (1.0 + th) + 0.5 * v * (1.0 - th * th) * GELU_COEF * (
                1.0 + 3.0 * CUBIC_COEF * v * v
            )

        loop(4, body)

    def forward(s, hooks):
        k = 4 * s
        target = xs_buf.at[1] if s == 0 else xo
        for u in (0, 1):
            if s == 1:
                ag_finish(3, u, xs_buf.at[1])
            first_norm(s, u)
            if u == 0:
                hooks[0]()
                w_ready(s, WQ)
            attention(s, u)
            if u == 0:
                hooks[1]()
                w_ready(s, WO)
            partial(
                k, u,
                lambda rows, cols: dot_nn(mix[s, 0, rows, :], wo[s, :, cols])
                + dot_nn(mix[s, 1, rows, :], wo[s + 2, :, cols]),
            )
        hooks[2]()
        for u in (0, 1):
            first_own(s, u)
            middle = xs_buf[s, own(u), :].astype(F32) + rs_finish(k, u) + prm[s, 0:1, :]
            yrow[u] = middle
            normed, inv = norm(middle)
            a2[s, own(u), :] = (normed * prm[s, 3:4, :] + prm[s, 5:6, :]).astype(BF16)
            ag_start(k + 1, u, a2.at[s])
            n2[s, u] = normed
            i2[s, u] = jnp.broadcast_to(inv, (R, 128))
        hooks[3]()
        w_ready(s, WU)
        for u in (0, 1):
            ag_finish(k + 1, u, a2.at[s])
            feed_up(s, u)
            if u == 0:
                hooks[4]()
                w_ready(s, WD)
            partial(
                k + 2, u,
                lambda rows, cols: dot_nn(hid[s, 0, rows, :], wd[s, :, cols])
                + dot_nn(hid[s, 1, rows, :], wd[s + 2, :, cols]),
            )
        hooks[5]()
        for u in (0, 1):
            target[own(u), :] = (yrow[u] + rs_finish(k + 2, u) + prm[s, 1:2, :]).astype(BF16)
            ag_start(k + 3, u, target)

    load_x.wait()
    for d in (1, 2, 3):
        send_prm(d).wait_recv()

    def f0_0():
        w_spread(0, WQ)
        w_spread(0, WO)
        w_hand_over(0, WQ)

    def f0_1():
        w_hand_over(0, WO)

    def f0_2():
        w_send_all(1)
        w_spread(0, WU)

    def f0_3():
        w_hand_over(0, WU)
        w_spread(0, WD)

    def f0_4():
        w_hand_over(0, WD)

    def f0_5():
        w_spread(1, WQ)
        w_spread(1, WO)

    def f1_0():
        w_hand_over(1, WQ)
        w_hand_over(1, WO)

    def f1_2():
        out_start(0, 0, xs_buf.at[1], so_out)
        w_spread(1, WU)

    def f1_3():
        w_hand_over(1, WU)
        w_spread(1, WD)

    def f1_4():
        w_hand_over(1, WD)

    def nothing():
        pass

    forward(0, [f0_0, f0_1, f0_2, f0_3, f0_4, f0_5])
    forward(1, [f1_0, nothing, f1_2, f1_3, f1_4, nothing])
    load_g.wait()

    def attention_back(s, u):
        rows = stream(u)
        keys = (u + 1) * HALF

        def body(h):
            grad_mix = dot_nt(dyb[s, rows, :], wo[2 * h + s]).astype(BF16)
            query = qkv[s, h, rows, 0:128]
            key, value = qkv[s, h, 0:keys, 128:256], qkv[s, h, 0:keys, 256:384]
            parts = []
            for e in (0, 1):
                probs = prob[s, h, e, rows, 0:keys]
                wide = probs.astype(F32)
                grad_prob = dot_nt(pick_head(grad_mix, e), value)
                delta = jnp.sum(wide * grad_prob, axis=-1, keepdims=True)
                grad_scores = (wide * (grad_prob - delta) * SCALE).astype(BF16)
                parts.append((dot_nn(grad_scores, key), dot_tn(grad_scores, query), dot_tn(probs, grad_mix)))
            dqkv[h, rows, 0:128] = jnp.where(low_lanes(HALF), parts[0][0], parts[1][0]).astype(BF16)
            for j in (1, 2):
                both = jnp.where(low_lanes(keys), parts[0][j], parts[1][j])
                cols = slice(j * 128, j * 128 + 128)
                if u == 1:
                    dqkv[h, rows, cols] = both[HALF:, :].astype(BF16)
                    dkv[h, :, (j - 1) * 128 : j * 128] = both[:HALF, :]
                else:
                    dqkv[h, rows, cols] = (both + dkv[h, :, (j - 1) * 128 : j * 128]).astype(BF16)

        loop(2, body)

    def add_row(s, i, value):
        sm[s, i : i + 1, :] = sm[s, i : i + 1, :] + jnp.sum(value, axis=0, keepdims=True)

    def backward(s, k, hooks):
        for u in (1, 0):
            rows = stream(u)
            if s == 0:
                ag_finish(11, u, g_buf.at[0])

            def grad_up_tile(i):
                h, n = lax.div(i, 2), lax.rem(i, 2)
                cols = ds(n * 256, 256)
                value = dot_nt(g_buf[s, rows, :], wd[2 * h + s, cols, :]) * slope[s, h, rows, cols]
                du[h, rows, cols] = value.astype(BF16)

            loop(4, grad_up_tile)
            partial(
                k, u,
                lambda rows, cols: dot_nt(du[0, rows, :], wu[s, cols, :]) + dot_nt(du[1, rows, :], wu[s + 2, cols, :]),
            )

        def grad_down(i):
            h, n = lax.div(i, 2), lax.rem(i, 2)
            rows = ds(n * 256, 256)
            gd[s, h, rows, :] = dot_tn(hid[s, h, :, rows], g_buf[s]).astype(BF16)

        loop(4, grad_down)
        gc_start(s, WD)
        hooks[0]()
        for u in (1, 0):
            top = g_buf[s, own(u), :].astype(F32)
            g_second = rs_finish(k, u)
            normed = n2[s, u]
            dy = top + norm_back(g_second, normed, i2[s, u, :, 0:1], prm[s, 3:4, :])
            dyb[s, own(u), :] = dy.astype(BF16)
            ag_start(k + 1, u, dyb.at[s])
            dyrow[u] = dy
            add_row(s, 1, top)
            add_row(s, 3, g_second * normed)
            add_row(s, 5, g_second)
            add_row(s, 0, dy)

        def grad_up(i):
            h, n = lax.div(i, 4), lax.rem(i, 4)
            rows = ds(n * 256, 256)
            gu[s, h, rows, :] = dot_tn(a2[s, :, rows], du[h]).astype(BF16)

        loop(8, grad_up)
        gc_start(s, WU)
        for h in (0, 1):
            sm[s, 6:7, h * 512 : h * 512 + 512] = jnp.sum(du[h].astype(F32), axis=0, keepdims=True)
        hooks[1]()
        for u in (1, 0):
            ag_finish(k + 1, u, dyb.at[s])
            attention_back(s, u)
            partial(
                k + 2, u,
                lambda rows, cols: dot_nt(dqkv[0, rows, :], planes(s, cols)) + dot_nt(dqkv[1, rows, :], planes(s + 2, cols)),
            )

        def grad_qkv(i):
            h, n = lax.div(i, 4), lax.rem(i, 4)
            rows = ds(n * 256, 256)
            value = dot_tn(a1[s, :, rows], dqkv[h]).astype(BF16)
            for j in range(3):
                gq[s, h, j, rows, :] = value[:, j * 128 : j * 128 + 128]

        loop(8, grad_qkv)
        gc_start(s, WQ)
        for h in (0, 1):
            go[s, h] = dot_tn(mix[s, h], dyb[s]).astype(BF16)
        gc_start(s, WO)
        for h in (0, 1):
            sums = jnp.sum(dqkv[h].astype(F32), axis=0, keepdims=True)
            sm[s, 7:8, h * 256 : h * 256 + 128] = sums[:, 0:128]
            sm[s, 7:8, h * 256 + 128 : h * 256 + 256] = sums[:, 256:384]
        hooks[2]()
        target = g_buf.at[0] if s == 1 else ig0
        for u in (1, 0):
            g_first = rs_finish(k + 2, u)
            normed = n1[s, u]
            low = dyrow[u] + norm_back(g_first, normed, i1[s, u, :, 0:1], prm[s, 2:3, :])
            target[own(u), :] = low.astype(BF16)
            if s == 1:
                ag_start(k + 3, u, target)
            else:
                low_start(u)
            add_row(s, 2, g_first * normed)
            add_row(s, 4, g_first)
        hooks[3]()

    def b1_0():
        for u in (0, 1):
            ag_finish(7, u, xo)
        out_start(1, 1, xo, so_out)

    def b1_1():
        stage1(1, WD)

    def b1_2():
        stage1(1, WU)
        stage2(1, WD)

    def b1_3():
        stage1(1, WQ)
        stage1(1, WO)

    backward(1, 8, [b1_0, b1_1, b1_2, b1_3])

    def b0_0():
        out_start(2, 1, g_buf.at[0], ig_out)
        stage2(1, WU)
        stage3(1, WD)
        stage2(1, WO)

    def b0_1():
        stage1(0, WD)
        stage3(1, WU)
        stage2(1, WQ)

    def b0_2():
        stage1(0, WU)
        stage2(0, WD)
        stage1(0, WQ)
        stage1(0, WO)
        stage3(1, WO)
        stage3(1, WQ)
        stage4(1, WD)

    def b0_3():
        stage2(0, WU)
        stage4(1, WU)
        stage2(0, WO)

    backward(0, 12, [b0_0, b0_1, b0_2, b0_3])

    def small_copy(i, src, dst, device):
        return remote(src, dst, sm_s.at[i], sm_r.at[i], device)

    small_c = [small_copy(0, sm, smc, core_peer)]
    small_z = [small_copy(d, sm1, smz.at[d - 1], dev(x, y, zp(d), c)) for d in (1, 2, 3)]
    small_y = [small_copy(3 + d, sm2, smy.at[d - 1], dev(x, yp(d), z, c)) for d in (1, 2, 3)]
    small_x = [small_copy(6 + d, sm3, smx.at[d - 1], dev(xp(d), y, z, c)) for d in (1, 2, 3)]

    def start_all(copies):
        for copy in copies:
            copy.start()

    def arrived(copies):
        for copy in copies:
            copy.wait_recv()

    start_all(small_c)
    stage2(0, WQ)
    stage3(0, WU)
    arrived(small_c)
    sm1[...] = sm[...] + smc[...]
    start_all(small_z)
    stage4(1, WO)
    stage4(1, WQ)
    stage3(0, WD)
    stage3(0, WQ)
    stage3(0, WO)
    arrived(small_z)
    sm2[...] = sm1[...] + smz[0] + smz[1] + smz[2]
    start_all(small_y)
    for k in range(4):
        stage5(1, k)
    stage4(0, WU)
    arrived(small_y)
    sm3[...] = sm2[...] + smy[0] + smy[1] + smy[2]
    start_all(small_x)
    stage4(0, WD)
    stage4(0, WO)
    stage4(0, WQ)
    arrived(small_x)
    mine = sm3[p]
    shared = mine + smx[0, p] + smx[1, p] + smx[2, p]
    row = lax.broadcasted_iota(jnp.int32, (8, D), 0)
    small_out[...] = jnp.where(row < 6, shared, mine)
    for k in (WU, WD, WO, WQ):
        stage5(0, k)
    for k in (WU, WD, WO, WQ):
        gf_finish(k)

    out_finish(0, 0, xs_buf.at[1], so_out)
    out_finish(1, 1, xo, so_out)
    out_finish(2, 1, g_buf.at[0], ig_out)
    for u in (1, 0):
        low_finish(u)
    for d in (1, 2, 3):
        send_prm(d).wait_send()
    for s in (0, 1):
        for k in range(4):
            if k not in Z_FIRST:
                @pl.when(p == s)
                def _():
                    for d in (1, 2, 3):
                        gz_copy(s, k, 0, d).wait_send()

            def sent(d):
                if d == 2:
                    for e in (1, 3):
                        w_send(k, e).wait_send()
                else:
                    w_relay(k, 0 if d == 1 else 1).wait_send()
                for j in (0, 1):
                    w_side(k, d, j).wait_send()
                for j in (0, 1, 2):
                    w_pass(k, d, j).wait_send()

            w_each(s, sent)

            for h in (0, 1):
                gc_copy(s, k, h).wait_send()
                if k in Z_FIRST:
                    for d in (1, 2, 3):
                        gz_copy(s, k, h, d).wait_send()

            for j in (0, 1):
                @pl.when(p == s)
                def _():
                    relay_copy(s, k, j).wait_send()

                @pl.when(p != s)
                def _():
                    main_copy(s, k, j).wait_send()

    gathered = {
        1: a2.at[0], 3: xs_buf.at[1], 5: a2.at[1], 7: xo, 9: dyb.at[1], 11: g_buf.at[0], 13: dyb.at[0],
    }
    for u in (0, 1):
        for d in (1, 2, 3):
            for k in range(0, 16, 2):
                rs_copy(k, u, d).wait_send()
            for k, ref in gathered.items():
                ag_copy(k, u, ref, d).wait_send()
    for copy in small_c + small_z + small_y + small_x:
        copy.wait_send()


def finish_kernel(
    so_in, ig_in, gq_in, go_in, gu_in, gd_in, small_in,
    so_out, ig_out, gq_out, go_out, gu_out, gd_out, outb, downb, gains, shifts, upb, qvb,
    so_buf, ig_buf, gq_buf, go_buf, gu_buf, gd_buf, gq_f, go_f, gu_f, gd_f, l_sem, s_sem,
):
    ins = (gu_in, gd_in, so_in, ig_in, gq_in, go_in)
    bufs = (gu_buf, gd_buf, so_buf, ig_buf, gq_buf, go_buf)
    wide = (gu_f, gd_f, None, None, gq_f, go_f)
    outs = (gu_out, gd_out, so_out, ig_out, gq_out, go_out)
    loads = [pltpu.make_async_copy(ins[i], bufs[i], l_sem.at[i]) for i in range(6)]
    for copy in loads:
        copy.start()
    h = lax.div(lax.axis_index("tensor"), 4)
    outb[...] = small_in[0:1, :]
    downb[...] = small_in[1:2, :]
    gains[...] = small_in[2:4, :]
    shifts[...] = small_in[4:6, :]
    upb[...] = jnp.where(h == 0, small_in[6:7, 0:512], small_in[6:7, 512:1024])
    qvb[0:1, :] = jnp.where(h == 0, small_in[7:8, 0:128], small_in[7:8, 256:384])
    qvb[1:2, :] = jnp.where(h == 0, small_in[7:8, 128:256], small_in[7:8, 384:512])
    stores = []
    for i in range(6):
        loads[i].wait()
        source = bufs[i]
        if wide[i] is not None:
            source = wide[i]
            lead = source.shape[0]
            step = lead if len(source.shape) == 3 else 64

            def body(r):
                if len(source.shape) == 3:
                    rows = ds(r * 128, 128)
                    wide[i][:, rows, :] = bufs[i][:, rows, :].astype(F32)
                else:
                    rows = ds(r * 64, 64)
                    wide[i][rows, :] = bufs[i][rows, :].astype(F32)

            loop(8 if len(source.shape) == 3 else lead // step, body)
        stores.append(pltpu.make_async_copy(source, outs[i], s_sem.at[i]))
        stores[-1].start()
    for copy in stores:
        copy.wait()


def run(x_in, seg, wq, qvb, wo, outb, wu, upb, wd, downb, gain, shift, og):
    any_spec = pl.BlockSpec(memory_space=pl.ANY)
    vmem = pl.BlockSpec(memory_space=pltpu.VMEM)
    V = pltpu.VMEM
    dma = pltpu.SemaphoreType.DMA
    tokens = x_in.shape[0]

    def kinds(lead, shrink):
        return [V(tuple(lead) + shape_of(k, ROWS[k] // shrink), BF16) for k in range(4)]

    scratch = kinds((4,), 1)
    scratch += [
        V((4, 8, D), F32), V((SEQ, SEQ), F32),
        V((2, SEQ, D), BF16), V((2, SEQ, D), BF16), V((2, SEQ, D), BF16), V((2, SEQ, D), BF16), V((2, SEQ, D), BF16),
        V((SEQ, D), BF16), V((SEQ, D), BF16),
        V((2, 2, SEQ, 384), BF16), V((2, 2, 2, SEQ, SEQ), BF16), V((2, 2, SEQ, 128), BF16),
        V((2, 2, SEQ, 512), BF16), V((2, 2, SEQ, 512), F32),
        V((2, SEQ, 512), BF16), V((2, SEQ, 384), BF16), V((2, HALF, 256), F32), V((SEQ, D), F32),
        V((8, SEQ, D), BF16), V((8, 2, 3, R, D), BF16),
        V((2, 2, R, D), F32), V((2, 2, R, D), F32), V((2, 2, R, 128), F32), V((2, 2, R, 128), F32),
        V((2, R, D), F32), V((2, R, D), F32),
    ]
    scratch += kinds((2, 2), 1) + kinds((2, 2), 2)
    scratch += [V((2,) + shape_of(k, ROWS[k] // (8 if k in Z_FIRST else 2)), BF16) for k in range(4)]
    scratch += [V((2,) + shape_of(k, ROWS[k] // (16 if k in Z_FIRST else 4)), BF16) for k in range(4)]
    scratch += [V(((2, 2, 3) if k in Z_FIRST else (3,)) + shape_of(k, ROWS[k] // 8), BF16) for k in range(4)]
    scratch += kinds((), 1)
    scratch += [V((2, 8, D), F32)] * 5 + [V((3, 2, 8, D), F32)] * 3
    sems = (96, 96, 12, 12, 24, 24, 36, 36, 8, 8, 3, 3, 6, 16, 16, 8, 8, 8, 8, 60, 60, 12, 12, 4, 4, 4, 10, 10, 9, 9, 3, 30, 30, 2)
    scratch += [dma((n,)) for n in sems]
    grads = [jax.ShapeDtypeStruct(shape_of(k, ROWS[k]), BF16) for k in range(4)]
    rows = jax.ShapeDtypeStruct((tokens, D), BF16)
    parts = pl.pallas_call(
        kernel,
        out_shape=(rows, rows, *grads, jax.ShapeDtypeStruct((8, D), F32)),
        in_specs=[any_spec, vmem, any_spec, vmem, any_spec, vmem, any_spec, vmem, any_spec, vmem, vmem, vmem, any_spec],
        out_specs=(any_spec,) * 6 + (vmem,),
        scratch_shapes=scratch,
        compiler_params=pltpu.CompilerParams(collective_id=0, has_side_effects=True, vmem_limit_bytes=64 * 1024 * 1024),
    )(x_in, seg, wq, qvb, wo, outb, wu, upb, wd, downb, gain, shift, og)

    def f32(*shape):
        return jax.ShapeDtypeStruct(shape, F32)

    return pl.pallas_call(
        finish_kernel,
        out_shape=(
            rows, rows, *[f32(*shape_of(k, ROWS[k])) for k in range(4)],
            f32(1, D), f32(1, D), f32(2, D), f32(2, D), f32(1, 512), f32(2, 128),
        ),
        in_specs=[any_spec] * 6 + [vmem],
        out_specs=(any_spec,) * 6 + (vmem,) * 6,
        scratch_shapes=[
            V((tokens, D), BF16), V((tokens, D), BF16), *kinds((), 1),
            *[V(shape_of(k, ROWS[k]), F32) for k in range(4)], dma((6,)), dma((6,)),
        ],
        compiler_params=pltpu.CompilerParams(vmem_limit_bytes=62 * 1024 * 1024),
    )(*parts)


def on_device(
    section_input, segment_ids, w_qkv, qv_bias, w_out, out_bias, w_up, up_bias, w_down, down_bias, norm_gains,
    norm_shifts, out_grad,
):
    so, ig, gq, go, gu, gd, outb, downb, gains, shifts, upb, qvb = run(
        section_input, segment_ids.reshape(8, 128), w_qkv[0].transpose(1, 0, 2), qv_bias[0], w_out[0], out_bias,
        w_up[0], up_bias, w_down[0], down_bias, norm_gains[0], norm_shifts[0], out_grad,
    )
    return (
        so[None], ig[None], gq.transpose(1, 0, 2)[None], qvb[None], go[None], outb, gu[None], upb, gd[None], downb,
        gains[None], shifts[None],
    )


def solution(mesh):
    placed = (
        P("dp", None),
        P("dp"),
        P("pipe", None, None, "tensor"),
        P("pipe", None, "tensor"),
        P("pipe", "tensor", None),
        P("pipe", None),
        P("pipe", None, "tensor"),
        P("pipe", "tensor"),
        P("pipe", "tensor", None),
        P("pipe", None),
        P("pipe", None, None),
        P("pipe", None, None),
        P("dp", None),
    )
    return jax.shard_map(
        on_device,
        mesh=mesh,
        in_specs=placed,
        out_specs=(
            P("pipe", "dp", None),
            P("pipe", "dp", None),
            P("pipe", None, None, "tensor"),
            P("pipe", None, "tensor"),
            P("pipe", "tensor", None),
            P("pipe", None),
            P("pipe", None, "tensor"),
            P("pipe", "tensor"),
            P("pipe", "tensor", None),
            P("pipe", None),
            P("pipe", None, None),
            P("pipe", None, None),
        ),
        check_vma=False,
    )
```

```python
import jax
import jax.numpy as jnp
from jax import lax
from jax.experimental import pallas as pl
from jax.experimental.pallas import tpu as pltpu
from jax.sharding import PartitionSpec as P

MESH = pl.DeviceIdType.MESH
F32 = jnp.float32
BF16 = jnp.bfloat16

SEQ = 256
D = 1024
HALF = 128
R = 32
NORM_EPS = 1e-05
GELU_COEF = 0.7978845608028654
CUBIC_COEF = 0.044715
MASKED_SCORE = -1e30
SCALE = 0.125
WQ, WO, WU, WD = range(4)
ROWS = (1024, 128, 1024, 512)
COLS = (128, 1024, 512, 1024)
Z_FIRST = (WQ, WU)


def dot_nn(a, b):
    return jnp.dot(a, b, preferred_element_type=F32)


def dot_nt(a, b):
    return lax.dot_general(a, b, (((1,), (1,)), ((), ())), preferred_element_type=F32)


def dot_tn(a, b):
    return lax.dot_general(a, b, (((0,), (0,)), ((), ())), preferred_element_type=F32)


def loop(n, body):
    lax.fori_loop(0, n, lambda i, c: (body(i), c)[1], 0)


def ds(start, size):
    return pl.ds(pl.multiple_of(start, size), size)


def norm(rows):
    centred = rows - jnp.mean(rows, axis=-1, keepdims=True)
    inv = lax.rsqrt(jnp.mean(centred * centred, axis=-1, keepdims=True) + NORM_EPS)
    return centred * inv, inv


def norm_back(grad, normed, inv, gain):
    e = grad * gain
    return inv * (
        e - jnp.mean(e, axis=-1, keepdims=True) - normed * jnp.mean(e * normed, axis=-1, keepdims=True)
    )


def shape_of(k, rows):
    return (3, rows, 128) if k == WQ else (rows, COLS[k])


def at(k, rows):
    return (slice(None), rows) if k == WQ else (rows,)


def kernel(
    x_in, seg_in, wq_in, qvb_in, wo_in, outb_in, wu_in, upb_in, wd_in, downb_in, gain_in, shift_in, og_in,
    so_out, ig_out, gq_out, go_out, gu_out, gd_out, small_out,
    wq, wo, wu, wd, prm, mask, xs_buf, g_buf, a1, a2, dyb, xo, ig0, qkv, prob, mix, hid, slope, du, dqkv, dkv, acc,
    rs_out, rs_in, n1, n2, i1, i2, yrow, dyrow,
    gq, go, gu, gd, cq, co, cu, cd, yq, yo, yu, yd, rq, ro, ru, rd, zq, zo, zu, zd, fq, fo, fu, fd,
    sm, sm1, sm2, sm3, smc, smz, smy, smx,
    x_s, x_r, wy_s, wy_r, wz_s, wz_r, wc_s, wc_r, wr_s, wr_r, pr_s, pr_r, loc, gc_s, gc_r, gy_s, gy_r, ry_s, ry_r, gz_s, gz_r, ga_s, ga_r,
    gf_s, gf_r, gl, sm_s, sm_r, o_s, o_r, o_l, d_s, d_r, d_l,
):
    p = lax.axis_index("pipe")
    t = lax.axis_index("tensor")
    dp = lax.axis_index("dp")
    h_me, x = lax.div(t, 4), lax.rem(t, 4)
    z, c = lax.div(dp, 2), lax.rem(dp, 2)
    y = h_me * 2 + p

    def dev(xx, yy, zz, cc):
        return {"pipe": lax.rem(yy, 2), "tensor": lax.div(yy, 2) * 4 + xx, "dp": zz * 2 + cc}

    def xp(d):
        return lax.rem(x + d, 4)

    def yp(d):
        return lax.rem(y + d, 4)

    def zp(d):
        return lax.rem(z + d, 4)

    core_peer = dev(x, y, z, 1 - c)

    def remote(src, dst, ss, rs, device):
        return pltpu.make_async_remote_copy(
            src_ref=src, dst_ref=dst, send_sem=ss, recv_sem=rs, device_id=device, device_id_type=MESH
        )

    def stream(u):
        return pl.ds(u * HALF, HALF)

    def own(u):
        return ds(u * HALF + x * R, R)

    w_in = (wq_in, wo_in, wu_in, wd_in)
    w_all = (wq, wo, wu, wd)
    g_all = (gq, go, gu, gd)
    c_all = (cq, co, cu, cd)
    y_all = (yq, yo, yu, yd)
    z_all = (zq, zo, zu, zd)
    r_all = (rq, ro, ru, rd)
    fin = (fq, fo, fu, fd)
    g_outs = (gq_out, go_out, gu_out, gd_out)
    grid_peers = [(dx, dy) for dx in range(4) for dy in range(4) if (dx, dy) != (0, 0)]

    barrier = pltpu.get_barrier_semaphore()
    peers = [dev(xp(dx), yp(dy), z, c) for dx, dy in grid_peers]
    peers += [dev(x, y, zp(d), c) for d in (1, 2, 3)] + [core_peer]
    for peer in peers:
        pl.semaphore_signal(barrier, inc=1, device_id=peer, device_id_type=MESH)

    load_x = pltpu.make_async_copy(x_in.at[ds(y * SEQ, SEQ)], xs_buf.at[0], loc.at[0])
    load_g = pltpu.make_async_copy(og_in.at[ds(y * SEQ, SEQ)], g_buf.at[1], loc.at[1])
    load_x.start()
    load_w = [pltpu.make_async_copy(w_in[k], w_all[k].at[y], loc.at[2 + k]) for k in range(4)]
    for copy in load_w:
        copy.start()
    load_g.start()

    prm[y] = jnp.zeros((8, D), F32)
    prm[y, 0:1, :] = outb_in[...]
    prm[y, 1:2, :] = downb_in[...]
    prm[y, 2:4, :] = gain_in[...]
    prm[y, 4:6, :] = shift_in[...]
    prm[y, 6:7, 0:512] = upb_in[...]
    prm[y, 7:8, 0:128] = qvb_in[0:1, :]
    prm[y, 7:8, 128:256] = qvb_in[1:2, :]
    sm[...] = jnp.zeros_like(sm)

    pl.semaphore_wait(barrier, len(peers))

    def send_prm(d):
        return remote(prm.at[y], prm.at[y], pr_s.at[d - 1], pr_r.at[d - 1], dev(x, yp(d), z, c))

    even = lax.rem(z, 2)

    def half_rows(k, which):
        return ds(which * (ROWS[k] // 2), ROWS[k] // 2)

    def quarter_rows(k, which):
        q = ROWS[k] // 4
        return pl.ds(pl.multiple_of(c * (2 * q) + which * q, q), q)

    def eighth_rows(k, which, j):
        q = ROWS[k] // 8
        return pl.ds(pl.multiple_of(c * (4 * q) + which * (2 * q) + j * q, q), q)

    def w_send(k, d):
        rows = at(k, quarter_rows(k, even))
        i = k * 3 + d - 1
        return remote(
            w_in[k].at[rows], w_all[k].at[(y,) + rows], wy_s.at[i], wy_r.at[i], dev(x, yp(d), z, c)
        )

    def w_block(k, d, rows):
        return w_all[k].at[(lax.rem(y - d + 4, 4),) + at(k, rows)]

    def w_side(k, d, j):
        i = (k * 3 + d - 1) * 2 + j
        block = w_block(k, d, eighth_rows(k, even, j))
        return remote(block, block, wz_s.at[i], wz_r.at[i], dev(x, y, zp(1 if j == 0 else 3), c))

    def w_pass(k, d, j):
        i = (k * 3 + d - 1) * 3 + j
        block = w_block(k, d, quarter_rows(k, even) if j == 0 else eighth_rows(k, 1 - even, j - 1))
        return remote(block, block, wc_s.at[i], wc_r.at[i], core_peer)

    def w_relay(k, j):
        block = w_block(k, 1 if j == 0 else 3, eighth_rows(k, even, j))
        i = k * 2 + j
        return remote(block, block, wr_s.at[i], wr_r.at[i], dev(x, yp(1 if j == 0 else 3), z, c))

    def w_relayed(k, j):
        block = w_block(k, 2, eighth_rows(k, even, j))
        i = k * 2 + j
        return remote(block, block, wr_s.at[i], wr_r.at[i], dev(x, yp(1 if j == 0 else 3), z, c))

    def w_send_kind(s, k):
        @pl.when(p == s)
        def _():
            for d in (1, 3):
                w_send(k, d).start()

    def w_each(s, act):
        @pl.when(p == s)
        def _():
            act(2)

        @pl.when(p != s)
        def _():
            act(1)
            act(3)

    def w_spread(s, k):
        def act(d):
            if d == 2:
                w_relayed(k, 0).wait_recv()
                w_side(k, d, 0).start()
                w_relayed(k, 1).wait_recv()
                w_side(k, d, 1).start()
            else:
                w_send(k, d).wait_recv()
                w_relay(k, 0 if d == 1 else 1).start()
                for j in (0, 1):
                    w_side(k, d, j).start()
            w_pass(k, d, 0).start()

        w_each(s, act)

    def w_hand_over(s, k):
        def act(d):
            for j in (0, 1):
                w_side(k, d, j).wait_recv()
                w_pass(k, d, 1 + j).start()

        w_each(s, act)

    def w_ready(s, k):
        @pl.when(p == s)
        def _():
            load_w[k].wait()

        def act(d):
            for j in (0, 1, 2):
                w_pass(k, d, j).wait_recv()

        w_each(s, act)

    def x_sem(k, u, d):
        return (k * 2 + u) * 3 + d - 1

    def rs_copy(k, u, d):
        dest = xp(d)
        i = x_sem(k, u, d)
        return remote(
            rs_out.at[k // 2, ds(u * HALF + dest * R, R)], rs_in.at[k // 2, u, d - 1], x_s.at[i], x_r.at[i],
            dev(dest, y, z, c),
        )

    def rs_start(k, u):
        for d in (2, 1, 3):
            rs_copy(k, u, d).start()

    def rs_finish(k, u):
        total = acc[own(u), :]
        for d in (1, 3, 2):
            rs_copy(k, u, d).wait_recv()
            total = total + rs_in[k // 2, u, d - 1].astype(F32)
        return total

    def ag_copy(k, u, ref, d):
        i = x_sem(k, u, d)
        block = ref.at[own(u)]
        return remote(block, block, x_s.at[i], x_r.at[i], dev(xp(d), y, z, c))

    def ag_start(k, u, ref):
        for d in (2, 1, 3):
            ag_copy(k, u, ref, d).start()

    def ag_finish(k, u, ref):
        for d in (1, 3, 2):
            ag_copy(k, u, ref, d).wait_recv()

    def out_copy(i, ref, out, d):
        j = i * 3 + d - 1
        return remote(ref, out.at[ds(y * SEQ, SEQ)], o_s.at[j], o_r.at[j], dev(x, yp(d), z, c))

    def out_local(i, ref, out):
        return pltpu.make_async_copy(ref, out.at[ds(y * SEQ, SEQ)], o_l.at[i])

    def out_start(i, s, ref, out):
        for d in (1, 2, 3):
            @pl.when(lax.rem(y + d, 2) == s)
            def _():
                out_copy(i, ref, out, d).start()

        @pl.when(p == s)
        def _():
            out_local(i, ref, out).start()

    def out_finish(i, s, ref, out):
        for d in (1, 2, 3):
            @pl.when(lax.rem(y + d, 2) == s)
            def _():
                out_copy(i, ref, out, d).wait_send()

        @pl.when(p == s)
        def _():
            out_local(i, ref, out).wait()
            for d in (1, 2, 3):
                out_copy(i, ref, out, d).wait_recv()

    def low_rows(u):
        return ds(y * SEQ + u * HALF + x * R, R)

    def low_copy(u, j):
        dx, dy = grid_peers[j]
        i = u * 15 + j
        return remote(ig0.at[own(u)], ig_out.at[low_rows(u)], d_s.at[i], d_r.at[i], dev(xp(dx), yp(dy), z, c))

    def low_local(u):
        return pltpu.make_async_copy(ig0.at[own(u)], ig_out.at[low_rows(u)], d_l.at[u])

    def low_start(u):
        for j, (dx, dy) in enumerate(grid_peers):
            @pl.when(lax.rem(y + dy, 2) == 0)
            def _():
                low_copy(u, j).start()

        @pl.when(p == 0)
        def _():
            low_local(u).start()

    def low_finish(u):
        for j, (dx, dy) in enumerate(grid_peers):
            @pl.when(lax.rem(y + dy, 2) == 0)
            def _():
                low_copy(u, j).wait_send()

        @pl.when(p == 0)
        def _():
            low_local(u).wait()
            for j in range(15):
                low_copy(u, j).wait_recv()

    def gc_copy(s, k, h):
        i = (s * 4 + k) * 2 + h
        return remote(
            g_all[k].at[(s, h) + at(k, half_rows(k, 1 - c))], c_all[k].at[s, h], gc_s.at[i], gc_r.at[i], core_peer
        )

    def gc_start(s, k):
        for h in (0, 1):
            gc_copy(s, k, h).start()

    def sum_rows(k, target, base, sources, rows, result=None):
        step = min(rows, 64)
        result = target if result is None else result

        def body(r):
            here = at(k, pl.ds(pl.multiple_of(base + r * step, 16), step))
            there = at(k, pl.ds(pl.multiple_of(r * step, 16), step))
            if len(sources) == 1:
                result[here] = target[here] + sources[0][there]
                return
            total = target[here].astype(F32)
            for source in sources:
                total = total + source[there].astype(F32)
            result[here] = total.astype(BF16)

        loop(rows // step, body)

    def piece_base(k, zz):
        return c * (ROWS[k] // 2) + zz * (ROWS[k] // 8)

    def piece(k, zz):
        return at(k, pl.ds(pl.multiple_of(piece_base(k, zz), 16), ROWS[k] // 8))

    def region(k):
        return (piece_base(k, z), ROWS[k] // 8) if k in Z_FIRST else (c * (ROWS[k] // 2), ROWS[k] // 2)

    def y_side(j):
        return yp(1 if j == 0 else 3)

    def relay_copy(s, k, j):
        base, n = region(k)
        rows = at(k, pl.ds(pl.multiple_of(base + j * (n // 2), 16), n // 2))
        i = k * 2 + j
        return remote(
            g_all[k].at[(s, 1 - h_me) + rows], r_all[k].at[j], ry_s.at[i], ry_r.at[i], dev(x, y_side(j), z, c)
        )

    def main_copy(s, k, j):
        base, n = region(k)
        rows = at(k, pl.ds(pl.multiple_of(base, 16), n))
        i = k * 2 + j
        block = lax.div(y_side(j), 2)
        return remote(
            g_all[k].at[(s, block) + rows], y_all[k].at[j], gy_s.at[i], gy_r.at[i], dev(x, y_side(j), z, c)
        )

    def relay_start(s, k):
        @pl.when(p == s)
        def _():
            for j in (0, 1):
                relay_copy(s, k, j).start()

    def main_start(s, k):
        @pl.when(p != s)
        def _():
            base, n = region(k)
            for j in (0, 1):
                relay_copy(s, k, j).wait_recv()
                sum_rows(
                    k, g_all[k].at[s, lax.div(y_side(j), 2)], base + j * (n // 2), [r_all[k].at[j]], n // 2
                )
                main_copy(s, k, j).start()

    def main_arrived(s, k):
        for j in (0, 1):
            main_copy(s, k, j).wait_recv()
        return [y_all[k].at[j] for j in (0, 1)]

    def gz_copy(s, k, h, d):
        zz = zp(d)
        i = ((s * 4 + k) * 2 + h) * 3 + d - 1 if k in Z_FIRST else 48 + k * 3 + d - 1
        block = h if k in Z_FIRST else h_me
        slot = z_all[k].at[s, h, d - 1] if k in Z_FIRST else z_all[k].at[d - 1]
        return remote(g_all[k].at[(s, block) + piece(k, zz)], slot, gz_s.at[i], gz_r.at[i], dev(x, y, zz, c))

    def ga_copy(k, d):
        i = k * 3 + d - 1
        block = fin[k].at[piece(k, z)]
        return remote(block, block, ga_s.at[i], ga_r.at[i], dev(x, y, zp(d), c))

    def gf_copy(k):
        rows = at(k, half_rows(k, c))
        return remote(fin[k].at[rows], g_outs[k].at[rows], gf_s.at[k], gf_r.at[k], core_peer)

    def gf_local(k):
        rows = at(k, half_rows(k, c))
        return pltpu.make_async_copy(fin[k].at[rows], g_outs[k].at[rows], gl.at[k])

    def stage1(s, k):
        for h in (0, 1):
            gc_copy(s, k, h).wait_recv()
            sum_rows(k, g_all[k].at[s, h], c * (ROWS[k] // 2), [c_all[k].at[s, h]], ROWS[k] // 2)
            if k in Z_FIRST:
                for d in (2, 1, 3):
                    gz_copy(s, k, h, d).start()
        if k not in Z_FIRST:
            relay_start(s, k)

    def stage2(s, k):
        if k in Z_FIRST:
            for h in (0, 1):
                for d in (1, 3, 2):
                    gz_copy(s, k, h, d).wait_recv()
                slots = [z_all[k].at[s, h, j] for j in range(3)]
                sum_rows(k, g_all[k].at[s, h], piece_base(k, z), slots, ROWS[k] // 8)
            relay_start(s, k)
        else:
            main_start(s, k)

    def stage3(s, k):
        if k in Z_FIRST:
            main_start(s, k)
        else:
            @pl.when(p == s)
            def _():
                slots = main_arrived(s, k)
                sum_rows(k, g_all[k].at[s, h_me], c * (ROWS[k] // 2), slots, ROWS[k] // 2)
                for d in (2, 1, 3):
                    gz_copy(s, k, 0, d).start()

    def stage4(s, k):
        @pl.when(p == s)
        def _():
            if k in Z_FIRST:
                slots = main_arrived(s, k)
            else:
                for d in (1, 3, 2):
                    gz_copy(s, k, 0, d).wait_recv()
                slots = [z_all[k].at[j] for j in range(3)]
            sum_rows(k, g_all[k].at[s, h_me], piece_base(k, z), slots, ROWS[k] // 8, fin[k])
            for d in (2, 1, 3):
                ga_copy(k, d).start()

    def stage5(s, k):
        @pl.when(p == s)
        def _():
            for d in (1, 3, 2):
                ga_copy(k, d).wait_recv()
            gf_copy(k).start()
            gf_local(k).start()

    def gf_finish(k):
        gf_local(k).wait()
        gf_copy(k).wait()
        for d in (1, 2, 3):
            ga_copy(k, d).wait_send()

    for d in (1, 3, 2):
        send_prm(d).start()
    for k in range(4):
        w_send_kind(0, k)

    seg = jnp.concatenate([seg_in[pl.ds(2 * y, 1), :], seg_in[pl.ds(2 * y + 1, 1), :]], axis=1).astype(F32)
    seg_b = jnp.broadcast_to(seg, (SEQ, SEQ))
    rows_i = lax.broadcasted_iota(jnp.int32, (SEQ, SEQ), 0)
    cols_i = lax.broadcasted_iota(jnp.int32, (SEQ, SEQ), 1)
    mask[...] = jnp.where((rows_i >= cols_i) & (seg_b == seg_b.T), 0.0, MASKED_SCORE)

    def low_lanes(rows):
        return lax.broadcasted_iota(jnp.int32, (rows, 128), 1) < 64

    def pick_head(value, e):
        keep = low_lanes(value.shape[0])
        keep = keep if e == 0 else jnp.logical_not(keep)
        return jnp.where(keep, value, jnp.zeros_like(value))

    def planes(b, rows):
        return jnp.concatenate([wq[b, 0, rows, :], wq[b, 1, rows, :], wq[b, 2, rows, :]], axis=1)

    def first_norm(s, u):
        def body(r):
            rows = ds(u * HALF + r * 64, 64)
            normed, _ = norm(xs_buf[s, rows, :].astype(F32))
            a1[s, rows, :] = (normed * prm[s, 2:3, :] + prm[s, 4:5, :]).astype(BF16)

        loop(2, body)

    def first_own(s, u):
        normed, inv = norm(xs_buf[s, own(u), :].astype(F32))
        n1[s, u] = normed
        i1[s, u] = jnp.broadcast_to(inv, (R, 128))

    def attention(s, u):
        keys = (u + 1) * HALF
        rows = stream(u)

        def body(h):
            b = 2 * h + s
            bias = jnp.concatenate(
                [prm[b, 7:8, 0:128], jnp.zeros((1, 128), F32), prm[b, 7:8, 128:256]], axis=1
            )
            qkv[s, h, rows, :] = (dot_nn(a1[s, rows, :], planes(b, slice(None))) + bias).astype(BF16)
            query = qkv[s, h, rows, 0:128]
            key, value = qkv[s, h, 0:keys, 128:256], qkv[s, h, 0:keys, 256:384]
            parts = []
            for e in (0, 1):
                scores = dot_nt(pick_head(query, e), key) * SCALE + mask[rows, 0:keys]
                weights = jnp.exp(scores - jnp.max(scores, axis=-1, keepdims=True))
                probs = (weights / jnp.sum(weights, axis=-1, keepdims=True)).astype(BF16)
                prob[s, h, e, rows, 0:keys] = probs
                parts.append(dot_nn(probs, value))
            mix[s, h, rows, :] = jnp.where(low_lanes(HALF), parts[0], parts[1]).astype(BF16)

        loop(2, body)

    def partial(k, u, tile):
        rows = stream(u)

        def body(n):
            cols = ds(n * 256, 256)
            value = tile(rows, cols)
            acc[rows, cols] = value
            rs_out[k // 2, rows, cols] = value.astype(BF16)

        loop(4, body)
        rs_start(k, u)

    def feed_up(s, u):
        rows = stream(u)

        def body(i):
            h, n = lax.div(i, 2), lax.rem(i, 2)
            b = 2 * h + s
            cols = ds(n * 256, 256)
            v = dot_nn(a2[s, rows, :], wu[b, :, cols]) + prm[b, 6:7, cols]
            th = jnp.tanh(GELU_COEF * (v + CUBIC_COEF * v * v * v))
            hid[s, h, rows, cols] = (0.5 * v * (1.0 + th)).astype(BF16)
            slope[s, h, rows, cols] = 0.5 * (1.0 + th) + 0.5 * v * (1.0 - th * th) * GELU_COEF * (
                1.0 + 3.0 * CUBIC_COEF * v * v
            )

        loop(4, body)

    def forward(s, hooks):
        k = 4 * s
        target = xs_buf.at[1] if s == 0 else xo
        for u in (0, 1):
            if s == 1:
                ag_finish(3, u, xs_buf.at[1])
            first_norm(s, u)
            if u == 0:
                hooks[0]()
                w_ready(s, WQ)
            attention(s, u)
            if u == 0:
                hooks[1]()
                w_ready(s, WO)
            partial(
                k, u,
                lambda rows, cols: dot_nn(mix[s, 0, rows, :], wo[s, :, cols])
                + dot_nn(mix[s, 1, rows, :], wo[s + 2, :, cols]),
            )
        hooks[2]()
        for u in (0, 1):
            first_own(s, u)
            middle = xs_buf[s, own(u), :].astype(F32) + rs_finish(k, u) + prm[s, 0:1, :]
            yrow[u] = middle
            normed, inv = norm(middle)
            a2[s, own(u), :] = (normed * prm[s, 3:4, :] + prm[s, 5:6, :]).astype(BF16)
            ag_start(k + 1, u, a2.at[s])
            n2[s, u] = normed
            i2[s, u] = jnp.broadcast_to(inv, (R, 128))
        hooks[3]()
        w_ready(s, WU)
        for u in (0, 1):
            ag_finish(k + 1, u, a2.at[s])
            feed_up(s, u)
            if u == 0:
                hooks[4]()
                w_ready(s, WD)
            partial(
                k + 2, u,
                lambda rows, cols: dot_nn(hid[s, 0, rows, :], wd[s, :, cols])
                + dot_nn(hid[s, 1, rows, :], wd[s + 2, :, cols]),
            )
        hooks[5]()
        for u in (0, 1):
            target[own(u), :] = (yrow[u] + rs_finish(k + 2, u) + prm[s, 1:2, :]).astype(BF16)
            ag_start(k + 3, u, target)

    load_x.wait()
    for d in (1, 2, 3):
        send_prm(d).wait_recv()

    def f0_0():
        w_spread(0, WQ)
        w_send_kind(1, WQ)
        w_spread(0, WO)
        w_send_kind(1, WO)
        w_hand_over(0, WQ)

    def f0_1():
        w_hand_over(0, WO)

    def f0_2():
        w_spread(0, WU)
        w_send_kind(1, WU)

    def f0_3():
        w_spread(0, WD)
        w_send_kind(1, WD)
        w_hand_over(0, WU)

    def f0_4():
        w_hand_over(0, WD)

    def f0_5():
        w_spread(1, WQ)
        w_spread(1, WO)
        w_spread(1, WU)

    def f1_0():
        w_hand_over(1, WQ)
        w_hand_over(1, WO)

    def f1_2():
        out_start(0, 0, xs_buf.at[1], so_out)
        w_spread(1, WD)

    def f1_3():
        w_hand_over(1, WU)

    def f1_4():
        w_hand_over(1, WD)

    def nothing():
        pass

    forward(0, [f0_0, f0_1, f0_2, f0_3, f0_4, f0_5])
    forward(1, [f1_0, nothing, f1_2, f1_3, f1_4, nothing])
    load_g.wait()

    def attention_back(s, u):
        rows = stream(u)
        keys = (u + 1) * HALF

        def body(h):
            grad_mix = dot_nt(dyb[s, rows, :], wo[2 * h + s]).astype(BF16)
            query = qkv[s, h, rows, 0:128]
            key, value = qkv[s, h, 0:keys, 128:256], qkv[s, h, 0:keys, 256:384]
            parts = []
            for e in (0, 1):
                probs = prob[s, h, e, rows, 0:keys]
                wide = probs.astype(F32)
                grad_prob = dot_nt(pick_head(grad_mix, e), value)
                delta = jnp.sum(wide * grad_prob, axis=-1, keepdims=True)
                grad_scores = (wide * (grad_prob - delta) * SCALE).astype(BF16)
                parts.append((dot_nn(grad_scores, key), dot_tn(grad_scores, query), dot_tn(probs, grad_mix)))
            dqkv[h, rows, 0:128] = jnp.where(low_lanes(HALF), parts[0][0], parts[1][0]).astype(BF16)
            for j in (1, 2):
                both = jnp.where(low_lanes(keys), parts[0][j], parts[1][j])
                cols = slice(j * 128, j * 128 + 128)
                if u == 1:
                    dqkv[h, rows, cols] = both[HALF:, :].astype(BF16)
                    dkv[h, :, (j - 1) * 128 : j * 128] = both[:HALF, :]
                else:
                    dqkv[h, rows, cols] = (both + dkv[h, :, (j - 1) * 128 : j * 128]).astype(BF16)

        loop(2, body)

    def add_row(s, i, value):
        sm[s, i : i + 1, :] = sm[s, i : i + 1, :] + jnp.sum(value, axis=0, keepdims=True)

    def backward(s, k, hooks):
        for u in (1, 0):
            rows = stream(u)
            if s == 0:
                ag_finish(11, u, g_buf.at[0])

            def grad_up_tile(i):
                h, n = lax.div(i, 2), lax.rem(i, 2)
                cols = ds(n * 256, 256)
                value = dot_nt(g_buf[s, rows, :], wd[2 * h + s, cols, :]) * slope[s, h, rows, cols]
                du[h, rows, cols] = value.astype(BF16)

            loop(4, grad_up_tile)
            partial(
                k, u,
                lambda rows, cols: dot_nt(du[0, rows, :], wu[s, cols, :]) + dot_nt(du[1, rows, :], wu[s + 2, cols, :]),
            )

        def grad_down(i):
            h, n = lax.div(i, 2), lax.rem(i, 2)
            rows = ds(n * 256, 256)
            gd[s, h, rows, :] = dot_tn(hid[s, h, :, rows], g_buf[s]).astype(BF16)

        loop(4, grad_down)
        gc_start(s, WD)
        hooks[0]()
        for u in (1, 0):
            top = g_buf[s, own(u), :].astype(F32)
            g_second = rs_finish(k, u)
            normed = n2[s, u]
            dy = top + norm_back(g_second, normed, i2[s, u, :, 0:1], prm[s, 3:4, :])
            dyb[s, own(u), :] = dy.astype(BF16)
            ag_start(k + 1, u, dyb.at[s])
            dyrow[u] = dy
            add_row(s, 1, top)
            add_row(s, 3, g_second * normed)
            add_row(s, 5, g_second)
            add_row(s, 0, dy)

        def grad_up(i):
            h, n = lax.div(i, 4), lax.rem(i, 4)
            rows = ds(n * 256, 256)
            gu[s, h, rows, :] = dot_tn(a2[s, :, rows], du[h]).astype(BF16)

        loop(8, grad_up)
        gc_start(s, WU)
        for h in (0, 1):
            sm[s, 6:7, h * 512 : h * 512 + 512] = jnp.sum(du[h].astype(F32), axis=0, keepdims=True)
        hooks[1]()
        for u in (1, 0):
            ag_finish(k + 1, u, dyb.at[s])
            attention_back(s, u)
            partial(
                k + 2, u,
                lambda rows, cols: dot_nt(dqkv[0, rows, :], planes(s, cols)) + dot_nt(dqkv[1, rows, :], planes(s + 2, cols)),
            )

        def grad_qkv(i):
            h, n = lax.div(i, 4), lax.rem(i, 4)
            rows = ds(n * 256, 256)
            value = dot_tn(a1[s, :, rows], dqkv[h]).astype(BF16)
            for j in range(3):
                gq[s, h, j, rows, :] = value[:, j * 128 : j * 128 + 128]

        loop(8, grad_qkv)
        gc_start(s, WQ)
        for h in (0, 1):
            go[s, h] = dot_tn(mix[s, h], dyb[s]).astype(BF16)
        gc_start(s, WO)
        for h in (0, 1):
            sums = jnp.sum(dqkv[h].astype(F32), axis=0, keepdims=True)
            sm[s, 7:8, h * 256 : h * 256 + 128] = sums[:, 0:128]
            sm[s, 7:8, h * 256 + 128 : h * 256 + 256] = sums[:, 256:384]
        hooks[2]()
        target = g_buf.at[0] if s == 1 else ig0
        for u in (1, 0):
            g_first = rs_finish(k + 2, u)
            normed = n1[s, u]
            low = dyrow[u] + norm_back(g_first, normed, i1[s, u, :, 0:1], prm[s, 2:3, :])
            target[own(u), :] = low.astype(BF16)
            if s == 1:
                ag_start(k + 3, u, target)
            else:
                low_start(u)
            add_row(s, 2, g_first * normed)
            add_row(s, 4, g_first)
        hooks[3]()

    def b1_0():
        for u in (0, 1):
            ag_finish(7, u, xo)
        out_start(1, 1, xo, so_out)

    def b1_1():
        stage1(1, WD)

    def b1_2():
        stage1(1, WU)
        stage2(1, WD)

    def b1_3():
        stage1(1, WQ)
        stage1(1, WO)

    backward(1, 8, [b1_0, b1_1, b1_2, b1_3])

    def b0_0():
        out_start(2, 1, g_buf.at[0], ig_out)
        stage2(1, WU)
        stage3(1, WD)
        stage2(1, WO)

    def b0_1():
        stage1(0, WD)
        stage3(1, WU)
        stage2(1, WQ)

    def b0_2():
        stage1(0, WU)
        stage2(0, WD)
        stage1(0, WQ)
        stage1(0, WO)
        stage3(1, WO)
        stage3(1, WQ)
        stage4(1, WD)

    def b0_3():
        stage2(0, WU)
        stage4(1, WU)
        stage2(0, WO)

    backward(0, 12, [b0_0, b0_1, b0_2, b0_3])

    def small_copy(i, src, dst, device):
        return remote(src, dst, sm_s.at[i], sm_r.at[i], device)

    small_c = [small_copy(0, sm, smc, core_peer)]
    small_z = [small_copy(d, sm1, smz.at[d - 1], dev(x, y, zp(d), c)) for d in (1, 2, 3)]
    small_y = [small_copy(3 + d, sm2, smy.at[d - 1], dev(x, yp(d), z, c)) for d in (1, 2, 3)]
    small_x = [small_copy(6 + d, sm3, smx.at[d - 1], dev(xp(d), y, z, c)) for d in (1, 2, 3)]

    def start_all(copies):
        for copy in copies:
            copy.start()

    def arrived(copies):
        for copy in copies:
            copy.wait_recv()

    start_all(small_c)
    stage2(0, WQ)
    stage3(0, WU)
    arrived(small_c)
    sm1[...] = sm[...] + smc[...]
    start_all(small_z)
    stage4(1, WO)
    stage4(1, WQ)
    stage3(0, WD)
    stage3(0, WQ)
    stage3(0, WO)
    arrived(small_z)
    sm2[...] = sm1[...] + smz[0] + smz[1] + smz[2]
    start_all(small_y)
    for k in range(4):
        stage5(1, k)
    stage4(0, WU)
    arrived(small_y)
    sm3[...] = sm2[...] + smy[0] + smy[1] + smy[2]
    start_all(small_x)
    stage4(0, WD)
    stage4(0, WO)
    stage4(0, WQ)
    arrived(small_x)
    mine = sm3[p]
    shared = mine + smx[0, p] + smx[1, p] + smx[2, p]
    row = lax.broadcasted_iota(jnp.int32, (8, D), 0)
    small_out[...] = jnp.where(row < 6, shared, mine)
    for k in (WU, WD, WO, WQ):
        stage5(0, k)
    for k in (WU, WD, WO, WQ):
        gf_finish(k)

    out_finish(0, 0, xs_buf.at[1], so_out)
    out_finish(1, 1, xo, so_out)
    out_finish(2, 1, g_buf.at[0], ig_out)
    for u in (1, 0):
        low_finish(u)
    for d in (1, 2, 3):
        send_prm(d).wait_send()
    for s in (0, 1):
        for k in range(4):
            if k not in Z_FIRST:
                @pl.when(p == s)
                def _():
                    for d in (1, 2, 3):
                        gz_copy(s, k, 0, d).wait_send()

            def sent(d):
                if d == 2:
                    for e in (1, 3):
                        w_send(k, e).wait_send()
                else:
                    w_relay(k, 0 if d == 1 else 1).wait_send()
                for j in (0, 1):
                    w_side(k, d, j).wait_send()
                for j in (0, 1, 2):
                    w_pass(k, d, j).wait_send()

            w_each(s, sent)

            for h in (0, 1):
                gc_copy(s, k, h).wait_send()
                if k in Z_FIRST:
                    for d in (1, 2, 3):
                        gz_copy(s, k, h, d).wait_send()

            for j in (0, 1):
                @pl.when(p == s)
                def _():
                    relay_copy(s, k, j).wait_send()

                @pl.when(p != s)
                def _():
                    main_copy(s, k, j).wait_send()

    gathered = {
        1: a2.at[0], 3: xs_buf.at[1], 5: a2.at[1], 7: xo, 9: dyb.at[1], 11: g_buf.at[0], 13: dyb.at[0],
    }
    for u in (0, 1):
        for d in (1, 2, 3):
            for k in range(0, 16, 2):
                rs_copy(k, u, d).wait_send()
            for k, ref in gathered.items():
                ag_copy(k, u, ref, d).wait_send()
    for copy in small_c + small_z + small_y + small_x:
        copy.wait_send()


def finish_kernel(
    so_in, ig_in, gq_in, go_in, gu_in, gd_in, small_in,
    so_out, ig_out, gq_out, go_out, gu_out, gd_out, outb, downb, gains, shifts, upb, qvb,
    so_buf, ig_buf, gq_buf, go_buf, gu_buf, gd_buf, gq_f, go_f, gu_f, gd_f, l_sem, s_sem,
):
    ins = (gu_in, gd_in, so_in, ig_in, gq_in, go_in)
    bufs = (gu_buf, gd_buf, so_buf, ig_buf, gq_buf, go_buf)
    wide = (gu_f, gd_f, None, None, gq_f, go_f)
    outs = (gu_out, gd_out, so_out, ig_out, gq_out, go_out)
    loads = [pltpu.make_async_copy(ins[i], bufs[i], l_sem.at[i]) for i in range(6)]
    for copy in loads:
        copy.start()
    h = lax.div(lax.axis_index("tensor"), 4)
    outb[...] = small_in[0:1, :]
    downb[...] = small_in[1:2, :]
    gains[...] = small_in[2:4, :]
    shifts[...] = small_in[4:6, :]
    upb[...] = jnp.where(h == 0, small_in[6:7, 0:512], small_in[6:7, 512:1024])
    qvb[0:1, :] = jnp.where(h == 0, small_in[7:8, 0:128], small_in[7:8, 256:384])
    qvb[1:2, :] = jnp.where(h == 0, small_in[7:8, 128:256], small_in[7:8, 384:512])
    stores = []
    for i in range(6):
        loads[i].wait()
        source = bufs[i]
        if wide[i] is not None:
            source = wide[i]
            lead = source.shape[0]
            step = lead if len(source.shape) == 3 else 64

            def body(r):
                if len(source.shape) == 3:
                    rows = ds(r * 128, 128)
                    wide[i][:, rows, :] = bufs[i][:, rows, :].astype(F32)
                else:
                    rows = ds(r * 64, 64)
                    wide[i][rows, :] = bufs[i][rows, :].astype(F32)

            loop(8 if len(source.shape) == 3 else lead // step, body)
        stores.append(pltpu.make_async_copy(source, outs[i], s_sem.at[i]))
        stores[-1].start()
    for copy in stores:
        copy.wait()


def run(x_in, seg, wq, qvb, wo, outb, wu, upb, wd, downb, gain, shift, og):
    any_spec = pl.BlockSpec(memory_space=pl.ANY)
    vmem = pl.BlockSpec(memory_space=pltpu.VMEM)
    V = pltpu.VMEM
    dma = pltpu.SemaphoreType.DMA
    tokens = x_in.shape[0]

    def kinds(lead, shrink):
        return [V(tuple(lead) + shape_of(k, ROWS[k] // shrink), BF16) for k in range(4)]

    scratch = kinds((4,), 1)
    scratch += [
        V((4, 8, D), F32), V((SEQ, SEQ), F32),
        V((2, SEQ, D), BF16), V((2, SEQ, D), BF16), V((2, SEQ, D), BF16), V((2, SEQ, D), BF16), V((2, SEQ, D), BF16),
        V((SEQ, D), BF16), V((SEQ, D), BF16),
        V((2, 2, SEQ, 384), BF16), V((2, 2, 2, SEQ, SEQ), BF16), V((2, 2, SEQ, 128), BF16),
        V((2, 2, SEQ, 512), BF16), V((2, 2, SEQ, 512), F32),
        V((2, SEQ, 512), BF16), V((2, SEQ, 384), BF16), V((2, HALF, 256), F32), V((SEQ, D), F32),
        V((8, SEQ, D), BF16), V((8, 2, 3, R, D), BF16),
        V((2, 2, R, D), F32), V((2, 2, R, D), F32), V((2, 2, R, 128), F32), V((2, 2, R, 128), F32),
        V((2, R, D), F32), V((2, R, D), F32),
    ]
    scratch += kinds((2, 2), 1) + kinds((2, 2), 2)
    scratch += [V((2,) + shape_of(k, ROWS[k] // (8 if k in Z_FIRST else 2)), BF16) for k in range(4)]
    scratch += [V((2,) + shape_of(k, ROWS[k] // (16 if k in Z_FIRST else 4)), BF16) for k in range(4)]
    scratch += [V(((2, 2, 3) if k in Z_FIRST else (3,)) + shape_of(k, ROWS[k] // 8), BF16) for k in range(4)]
    scratch += kinds((), 1)
    scratch += [V((2, 8, D), F32)] * 5 + [V((3, 2, 8, D), F32)] * 3
    sems = (96, 96, 12, 12, 24, 24, 36, 36, 8, 8, 3, 3, 6, 16, 16, 8, 8, 8, 8, 60, 60, 12, 12, 4, 4, 4, 10, 10, 9, 9, 3, 30, 30, 2)
    scratch += [dma((n,)) for n in sems]
    grads = [jax.ShapeDtypeStruct(shape_of(k, ROWS[k]), BF16) for k in range(4)]
    rows = jax.ShapeDtypeStruct((tokens, D), BF16)
    parts = pl.pallas_call(
        kernel,
        out_shape=(rows, rows, *grads, jax.ShapeDtypeStruct((8, D), F32)),
        in_specs=[any_spec, vmem, any_spec, vmem, any_spec, vmem, any_spec, vmem, any_spec, vmem, vmem, vmem, any_spec],
        out_specs=(any_spec,) * 6 + (vmem,),
        scratch_shapes=scratch,
        compiler_params=pltpu.CompilerParams(collective_id=0, has_side_effects=True, vmem_limit_bytes=64 * 1024 * 1024),
    )(x_in, seg, wq, qvb, wo, outb, wu, upb, wd, downb, gain, shift, og)

    def f32(*shape):
        return jax.ShapeDtypeStruct(shape, F32)

    return pl.pallas_call(
        finish_kernel,
        out_shape=(
            rows, rows, *[f32(*shape_of(k, ROWS[k])) for k in range(4)],
            f32(1, D), f32(1, D), f32(2, D), f32(2, D), f32(1, 512), f32(2, 128),
        ),
        in_specs=[any_spec] * 6 + [vmem],
        out_specs=(any_spec,) * 6 + (vmem,) * 6,
        scratch_shapes=[
            V((tokens, D), BF16), V((tokens, D), BF16), *kinds((), 1),
            *[V(shape_of(k, ROWS[k]), F32) for k in range(4)], dma((6,)), dma((6,)),
        ],
        compiler_params=pltpu.CompilerParams(vmem_limit_bytes=62 * 1024 * 1024),
    )(*parts)


def on_device(
    section_input, segment_ids, w_qkv, qv_bias, w_out, out_bias, w_up, up_bias, w_down, down_bias, norm_gains,
    norm_shifts, out_grad,
):
    so, ig, gq, go, gu, gd, outb, downb, gains, shifts, upb, qvb = run(
        section_input, segment_ids.reshape(8, 128), w_qkv[0].transpose(1, 0, 2), qv_bias[0], w_out[0], out_bias,
        w_up[0], up_bias, w_down[0], down_bias, norm_gains[0], norm_shifts[0], out_grad,
    )
    return (
        so[None], ig[None], gq.transpose(1, 0, 2)[None], qvb[None], go[None], outb, gu[None], upb, gd[None], downb,
        gains[None], shifts[None],
    )


def solution(mesh):
    placed = (
        P("dp", None),
        P("dp"),
        P("pipe", None, None, "tensor"),
        P("pipe", None, "tensor"),
        P("pipe", "tensor", None),
        P("pipe", None),
        P("pipe", None, "tensor"),
        P("pipe", "tensor"),
        P("pipe", "tensor", None),
        P("pipe", None),
        P("pipe", None, None),
        P("pipe", None, None),
        P("dp", None),
    )
    return jax.shard_map(
        on_device,
        mesh=mesh,
        in_specs=placed,
        out_specs=(
            P("pipe", "dp", None),
            P("pipe", "dp", None),
            P("pipe", None, None, "tensor"),
            P("pipe", None, "tensor"),
            P("pipe", "tensor", None),
            P("pipe", None),
            P("pipe", None, "tensor"),
            P("pipe", "tensor"),
            P("pipe", "tensor", None),
            P("pipe", None),
            P("pipe", None, None),
            P("pipe", None, None),
        ),
        check_vma=False,
    )
```

```python
import jax
import jax.numpy as jnp
from jax import lax
from jax.experimental import pallas as pl
from jax.experimental.pallas import tpu as pltpu
from jax.sharding import PartitionSpec as P

MESH = pl.DeviceIdType.MESH
F32 = jnp.float32
BF16 = jnp.bfloat16

SEQ = 256
D = 1024
HALF = 128
R = 32
NORM_EPS = 1e-05
GELU_COEF = 0.7978845608028654
CUBIC_COEF = 0.044715
MASKED_SCORE = -1e30
SCALE = 0.125
WQ, WO, WU, WD = range(4)
ROWS = (1024, 128, 1024, 512)
COLS = (128, 1024, 512, 1024)
Z_FIRST = (WQ, WU)


def dot_nn(a, b):
    return jnp.dot(a, b, preferred_element_type=F32)


def dot_nt(a, b):
    return lax.dot_general(a, b, (((1,), (1,)), ((), ())), preferred_element_type=F32)


def dot_tn(a, b):
    return lax.dot_general(a, b, (((0,), (0,)), ((), ())), preferred_element_type=F32)


def loop(n, body):
    lax.fori_loop(0, n, lambda i, c: (body(i), c)[1], 0)


def unrolled(n, body):
    for i in range(n):
        body(i)


def div(a, b):
    return a // b if isinstance(a, int) else lax.div(a, b)


def rem(a, b):
    return a % b if isinstance(a, int) else lax.rem(a, b)


def ds(start, size):
    if isinstance(start, int):
        return pl.ds(start, size)
    return pl.ds(pl.multiple_of(start, size), size)


def norm(rows):
    centred = rows - jnp.mean(rows, axis=-1, keepdims=True)
    inv = lax.rsqrt(jnp.mean(centred * centred, axis=-1, keepdims=True) + NORM_EPS)
    return centred * inv, inv


def norm_back(grad, normed, inv, gain):
    e = grad * gain
    return inv * (
        e - jnp.mean(e, axis=-1, keepdims=True) - normed * jnp.mean(e * normed, axis=-1, keepdims=True)
    )


def shape_of(k, rows):
    return (3, rows, 128) if k == WQ else (rows, COLS[k])


def at(k, rows):
    return (slice(None), rows) if k == WQ else (rows,)


def kernel(
    x_in, seg_in, wq_in, qvb_in, wo_in, outb_in, wu_in, upb_in, wd_in, downb_in, gain_in, shift_in, og_in,
    so_out, ig_out, gq_out, go_out, gu_out, gd_out, small_out,
    wq, wo, wu, wd, prm, mask, xs_buf, g_buf, a1, a2, dyb, xo, ig0, qkv, prob, mix, hid, slope, du, dqkv, dkv, acc,
    rs_out, rs_in, n1, n2, i1, i2, yrow, dyrow,
    gq, go, gu, gd, cq, co, cu, cd, yq, yo, yu, yd, rq, ro, ru, rd, zq, zo, zu, zd, fq, fo, fu, fd,
    sm, sm1, sm2, sm3, smc, smz, smy, smx,
    x_s, x_r, wy_s, wy_r, wz_s, wz_r, wc_s, wc_r, wr_s, wr_r, pr_s, pr_r, loc, gc_s, gc_r, gy_s, gy_r, ry_s, ry_r, gz_s, gz_r, ga_s, ga_r,
    gf_s, gf_r, gl, sm_s, sm_r, o_s, o_r, o_l, d_s, d_r, d_l,
):
    p = lax.axis_index("pipe")
    t = lax.axis_index("tensor")
    dp = lax.axis_index("dp")
    h_me, x = lax.div(t, 4), lax.rem(t, 4)
    z, c = lax.div(dp, 2), lax.rem(dp, 2)
    y = h_me * 2 + p

    def dev(xx, yy, zz, cc):
        return {"pipe": lax.rem(yy, 2), "tensor": lax.div(yy, 2) * 4 + xx, "dp": zz * 2 + cc}

    def xp(d):
        return lax.rem(x + d, 4)

    def yp(d):
        return lax.rem(y + d, 4)

    def zp(d):
        return lax.rem(z + d, 4)

    core_peer = dev(x, y, z, 1 - c)

    def remote(src, dst, ss, rs, device):
        return pltpu.make_async_remote_copy(
            src_ref=src, dst_ref=dst, send_sem=ss, recv_sem=rs, device_id=device, device_id_type=MESH
        )

    def stream(u):
        return pl.ds(u * HALF, HALF)

    def own(u):
        return ds(u * HALF + x * R, R)

    w_in = (wq_in, wo_in, wu_in, wd_in)
    w_all = (wq, wo, wu, wd)
    g_all = (gq, go, gu, gd)
    c_all = (cq, co, cu, cd)
    y_all = (yq, yo, yu, yd)
    z_all = (zq, zo, zu, zd)
    r_all = (rq, ro, ru, rd)
    fin = (fq, fo, fu, fd)
    g_outs = (gq_out, go_out, gu_out, gd_out)
    grid_peers = [(dx, dy) for dx in range(4) for dy in range(4) if (dx, dy) != (0, 0)]

    barrier = pltpu.get_barrier_semaphore()
    peers = [dev(xp(dx), yp(dy), z, c) for dx, dy in grid_peers]
    peers += [dev(x, y, zp(d), c) for d in (1, 2, 3)] + [core_peer]
    for peer in peers:
        pl.semaphore_signal(barrier, inc=1, device_id=peer, device_id_type=MESH)

    load_x = pltpu.make_async_copy(x_in.at[ds(y * SEQ, SEQ)], xs_buf.at[0], loc.at[0])
    load_g = pltpu.make_async_copy(og_in.at[ds(y * SEQ, SEQ)], g_buf.at[1], loc.at[1])
    load_x.start()
    load_w = [pltpu.make_async_copy(w_in[k], w_all[k].at[y], loc.at[2 + k]) for k in range(4)]
    for copy in load_w:
        copy.start()
    load_g.start()

    prm[y] = jnp.zeros((8, D), F32)
    prm[y, 0:1, :] = outb_in[...]
    prm[y, 1:2, :] = downb_in[...]
    prm[y, 2:4, :] = gain_in[...]
    prm[y, 4:6, :] = shift_in[...]
    prm[y, 6:7, 0:512] = upb_in[...]
    prm[y, 7:8, 0:128] = qvb_in[0:1, :]
    prm[y, 7:8, 128:256] = qvb_in[1:2, :]
    sm[...] = jnp.zeros_like(sm)

    pl.semaphore_wait(barrier, len(peers))

    def send_prm(d):
        return remote(prm.at[y], prm.at[y], pr_s.at[d - 1], pr_r.at[d - 1], dev(x, yp(d), z, c))

    even = lax.rem(z, 2)

    def half_rows(k, which):
        return ds(which * (ROWS[k] // 2), ROWS[k] // 2)

    def quarter_rows(k, which):
        q = ROWS[k] // 4
        return pl.ds(pl.multiple_of(c * (2 * q) + which * q, q), q)

    def eighth_rows(k, which, j):
        q = ROWS[k] // 8
        return pl.ds(pl.multiple_of(c * (4 * q) + which * (2 * q) + j * q, q), q)

    def w_send(k, d):
        rows = at(k, quarter_rows(k, even))
        i = k * 3 + d - 1
        return remote(
            w_in[k].at[rows], w_all[k].at[(y,) + rows], wy_s.at[i], wy_r.at[i], dev(x, yp(d), z, c)
        )

    def w_block(k, d, rows):
        return w_all[k].at[(lax.rem(y - d + 4, 4),) + at(k, rows)]

    def w_side(k, d, j):
        i = (k * 3 + d - 1) * 2 + j
        block = w_block(k, d, eighth_rows(k, even, j))
        return remote(block, block, wz_s.at[i], wz_r.at[i], dev(x, y, zp(1 if j == 0 else 3), c))

    def w_pass(k, d, j):
        i = (k * 3 + d - 1) * 3 + j
        block = w_block(k, d, quarter_rows(k, even) if j == 0 else eighth_rows(k, 1 - even, j - 1))
        return remote(block, block, wc_s.at[i], wc_r.at[i], core_peer)

    def w_relay(k, j):
        block = w_block(k, 1 if j == 0 else 3, eighth_rows(k, even, j))
        i = k * 2 + j
        return remote(block, block, wr_s.at[i], wr_r.at[i], dev(x, yp(1 if j == 0 else 3), z, c))

    def w_relayed(k, j):
        block = w_block(k, 2, eighth_rows(k, even, j))
        i = k * 2 + j
        return remote(block, block, wr_s.at[i], wr_r.at[i], dev(x, yp(1 if j == 0 else 3), z, c))

    def w_send_kind(s, k):
        @pl.when(p == s)
        def _():
            for d in (1, 3):
                w_send(k, d).start()

    def w_each(s, act):
        @pl.when(p == s)
        def _():
            act(2)

        @pl.when(p != s)
        def _():
            act(1)
            act(3)

    def w_spread(s, k):
        def act(d):
            if d == 2:
                w_relayed(k, 0).wait_recv()
                w_side(k, d, 0).start()
                w_relayed(k, 1).wait_recv()
                w_side(k, d, 1).start()
            else:
                w_send(k, d).wait_recv()
                w_relay(k, 0 if d == 1 else 1).start()
                for j in (0, 1):
                    w_side(k, d, j).start()
            w_pass(k, d, 0).start()

        w_each(s, act)

    def w_hand_over(s, k):
        def act(d):
            for j in (0, 1):
                w_side(k, d, j).wait_recv()
                w_pass(k, d, 1 + j).start()

        w_each(s, act)

    def w_ready(s, k):
        @pl.when(p == s)
        def _():
            load_w[k].wait()

        def act(d):
            for j in (0, 1, 2):
                w_pass(k, d, j).wait_recv()

        w_each(s, act)

    def x_sem(k, u, d):
        return (k * 2 + u) * 3 + d - 1

    def rs_copy(k, u, d):
        dest = xp(d)
        i = x_sem(k, u, d)
        return remote(
            rs_out.at[k // 2, ds(u * HALF + dest * R, R)], rs_in.at[k // 2, u, d - 1], x_s.at[i], x_r.at[i],
            dev(dest, y, z, c),
        )

    def rs_start(k, u):
        for d in (2, 1, 3):
            rs_copy(k, u, d).start()

    def rs_finish(k, u):
        total = acc[own(u), :]
        for d in (1, 3, 2):
            rs_copy(k, u, d).wait_recv()
            total = total + rs_in[k // 2, u, d - 1].astype(F32)
        return total

    def ag_copy(k, u, ref, d):
        i = x_sem(k, u, d)
        block = ref.at[own(u)]
        return remote(block, block, x_s.at[i], x_r.at[i], dev(xp(d), y, z, c))

    def ag_start(k, u, ref):
        for d in (2, 1, 3):
            ag_copy(k, u, ref, d).start()

    def ag_finish(k, u, ref):
        for d in (1, 3, 2):
            ag_copy(k, u, ref, d).wait_recv()

    def out_copy(i, ref, out, d):
        j = i * 3 + d - 1
        return remote(ref, out.at[ds(y * SEQ, SEQ)], o_s.at[j], o_r.at[j], dev(x, yp(d), z, c))

    def out_local(i, ref, out):
        return pltpu.make_async_copy(ref, out.at[ds(y * SEQ, SEQ)], o_l.at[i])

    def out_start(i, s, ref, out):
        for d in (1, 2, 3):
            @pl.when(lax.rem(y + d, 2) == s)
            def _():
                out_copy(i, ref, out, d).start()

        @pl.when(p == s)
        def _():
            out_local(i, ref, out).start()

    def out_finish(i, s, ref, out):
        for d in (1, 2, 3):
            @pl.when(lax.rem(y + d, 2) == s)
            def _():
                out_copy(i, ref, out, d).wait_send()

        @pl.when(p == s)
        def _():
            out_local(i, ref, out).wait()
            for d in (1, 2, 3):
                out_copy(i, ref, out, d).wait_recv()

    def low_rows(u):
        return ds(y * SEQ + u * HALF + x * R, R)

    def low_copy(u, j):
        dx, dy = grid_peers[j]
        i = u * 15 + j
        return remote(ig0.at[own(u)], ig_out.at[low_rows(u)], d_s.at[i], d_r.at[i], dev(xp(dx), yp(dy), z, c))

    def low_local(u):
        return pltpu.make_async_copy(ig0.at[own(u)], ig_out.at[low_rows(u)], d_l.at[u])

    def low_start(u):
        for j, (dx, dy) in enumerate(grid_peers):
            @pl.when(lax.rem(y + dy, 2) == 0)
            def _():
                low_copy(u, j).start()

        @pl.when(p == 0)
        def _():
            low_local(u).start()

    def low_finish(u):
        for j, (dx, dy) in enumerate(grid_peers):
            @pl.when(lax.rem(y + dy, 2) == 0)
            def _():
                low_copy(u, j).wait_send()

        @pl.when(p == 0)
        def _():
            low_local(u).wait()
            for j in range(15):
                low_copy(u, j).wait_recv()

    def gc_copy(s, k, h):
        i = (s * 4 + k) * 2 + h
        return remote(
            g_all[k].at[(s, h) + at(k, half_rows(k, 1 - c))], c_all[k].at[s, h], gc_s.at[i], gc_r.at[i], core_peer
        )

    def gc_start(s, k):
        for h in (0, 1):
            gc_copy(s, k, h).start()

    def sum_rows(k, target, base, sources, rows, result=None):
        step = min(rows, 64)
        result = target if result is None else result

        def body(r):
            here = at(k, pl.ds(pl.multiple_of(base + r * step, 16), step))
            there = at(k, pl.ds(pl.multiple_of(r * step, 16), step))
            if len(sources) == 1:
                result[here] = target[here] + sources[0][there]
                return
            total = target[here].astype(F32)
            for source in sources:
                total = total + source[there].astype(F32)
            result[here] = total.astype(BF16)

        loop(rows // step, body)

    def piece_base(k, zz):
        return c * (ROWS[k] // 2) + zz * (ROWS[k] // 8)

    def piece(k, zz):
        return at(k, pl.ds(pl.multiple_of(piece_base(k, zz), 16), ROWS[k] // 8))

    def region(k):
        return (piece_base(k, z), ROWS[k] // 8) if k in Z_FIRST else (c * (ROWS[k] // 2), ROWS[k] // 2)

    def y_side(j):
        return yp(1 if j == 0 else 3)

    def relay_copy(s, k, j):
        base, n = region(k)
        rows = at(k, pl.ds(pl.multiple_of(base + j * (n // 2), 16), n // 2))
        i = k * 2 + j
        return remote(
            g_all[k].at[(s, 1 - h_me) + rows], r_all[k].at[j], ry_s.at[i], ry_r.at[i], dev(x, y_side(j), z, c)
        )

    def main_copy(s, k, j):
        base, n = region(k)
        rows = at(k, pl.ds(pl.multiple_of(base, 16), n))
        i = k * 2 + j
        block = lax.div(y_side(j), 2)
        return remote(
            g_all[k].at[(s, block) + rows], y_all[k].at[j], gy_s.at[i], gy_r.at[i], dev(x, y_side(j), z, c)
        )

    def relay_start(s, k):
        @pl.when(p == s)
        def _():
            for j in (0, 1):
                relay_copy(s, k, j).start()

    def main_start(s, k):
        @pl.when(p != s)
        def _():
            base, n = region(k)
            for j in (0, 1):
                relay_copy(s, k, j).wait_recv()
                sum_rows(
                    k, g_all[k].at[s, lax.div(y_side(j), 2)], base + j * (n // 2), [r_all[k].at[j]], n // 2
                )
                main_copy(s, k, j).start()

    def main_arrived(s, k):
        for j in (0, 1):
            main_copy(s, k, j).wait_recv()
        return [y_all[k].at[j] for j in (0, 1)]

    def gz_copy(s, k, h, d):
        zz = zp(d)
        i = ((s * 4 + k) * 2 + h) * 3 + d - 1 if k in Z_FIRST else 48 + k * 3 + d - 1
        block = h if k in Z_FIRST else h_me
        slot = z_all[k].at[s, h, d - 1] if k in Z_FIRST else z_all[k].at[d - 1]
        return remote(g_all[k].at[(s, block) + piece(k, zz)], slot, gz_s.at[i], gz_r.at[i], dev(x, y, zz, c))

    def ga_copy(k, d):
        i = k * 3 + d - 1
        block = fin[k].at[piece(k, z)]
        return remote(block, block, ga_s.at[i], ga_r.at[i], dev(x, y, zp(d), c))

    def gf_copy(k):
        rows = at(k, half_rows(k, c))
        return remote(fin[k].at[rows], g_outs[k].at[rows], gf_s.at[k], gf_r.at[k], core_peer)

    def gf_local(k):
        rows = at(k, half_rows(k, c))
        return pltpu.make_async_copy(fin[k].at[rows], g_outs[k].at[rows], gl.at[k])

    def stage1(s, k):
        for h in (0, 1):
            gc_copy(s, k, h).wait_recv()
            sum_rows(k, g_all[k].at[s, h], c * (ROWS[k] // 2), [c_all[k].at[s, h]], ROWS[k] // 2)
            if k in Z_FIRST:
                for d in (2, 1, 3):
                    gz_copy(s, k, h, d).start()
        if k not in Z_FIRST:
            relay_start(s, k)

    def stage2(s, k):
        if k in Z_FIRST:
            for h in (0, 1):
                for d in (1, 3, 2):
                    gz_copy(s, k, h, d).wait_recv()
                slots = [z_all[k].at[s, h, j] for j in range(3)]
                sum_rows(k, g_all[k].at[s, h], piece_base(k, z), slots, ROWS[k] // 8)
            relay_start(s, k)
        else:
            main_start(s, k)

    def stage3(s, k):
        if k in Z_FIRST:
            main_start(s, k)
        else:
            @pl.when(p == s)
            def _():
                slots = main_arrived(s, k)
                sum_rows(k, g_all[k].at[s, h_me], c * (ROWS[k] // 2), slots, ROWS[k] // 2)
                for d in (2, 1, 3):
                    gz_copy(s, k, 0, d).start()

    def stage4(s, k):
        @pl.when(p == s)
        def _():
            if k in Z_FIRST:
                slots = main_arrived(s, k)
            else:
                for d in (1, 3, 2):
                    gz_copy(s, k, 0, d).wait_recv()
                slots = [z_all[k].at[j] for j in range(3)]
            sum_rows(k, g_all[k].at[s, h_me], piece_base(k, z), slots, ROWS[k] // 8, fin[k])
            for d in (2, 1, 3):
                ga_copy(k, d).start()

    def stage5(s, k):
        @pl.when(p == s)
        def _():
            for d in (1, 3, 2):
                ga_copy(k, d).wait_recv()
            gf_copy(k).start()
            gf_local(k).start()

    def gf_finish(k):
        gf_local(k).wait()
        gf_copy(k).wait()
        for d in (1, 2, 3):
            ga_copy(k, d).wait_send()

    for d in (1, 3, 2):
        send_prm(d).start()
    for k in range(4):
        w_send_kind(0, k)

    seg = jnp.concatenate([seg_in[pl.ds(2 * y, 1), :], seg_in[pl.ds(2 * y + 1, 1), :]], axis=1).astype(F32)
    seg_b = jnp.broadcast_to(seg, (SEQ, SEQ))
    rows_i = lax.broadcasted_iota(jnp.int32, (SEQ, SEQ), 0)
    cols_i = lax.broadcasted_iota(jnp.int32, (SEQ, SEQ), 1)
    mask[...] = jnp.where((rows_i >= cols_i) & (seg_b == seg_b.T), 0.0, MASKED_SCORE)

    def low_lanes(rows):
        return lax.broadcasted_iota(jnp.int32, (rows, 128), 1) < 64

    def pick_head(value, e):
        keep = low_lanes(value.shape[0])
        keep = keep if e == 0 else jnp.logical_not(keep)
        return jnp.where(keep, value, jnp.zeros_like(value))

    def planes(b, rows):
        return jnp.concatenate([wq[b, 0, rows, :], wq[b, 1, rows, :], wq[b, 2, rows, :]], axis=1)

    def first_norm(s, u):
        def body(r):
            rows = ds(u * HALF + r * 64, 64)
            normed, _ = norm(xs_buf[s, rows, :].astype(F32))
            a1[s, rows, :] = (normed * prm[s, 2:3, :] + prm[s, 4:5, :]).astype(BF16)

        unrolled(2, body)

    def first_own(s, u):
        normed, inv = norm(xs_buf[s, own(u), :].astype(F32))
        n1[s, u] = normed
        i1[s, u] = jnp.broadcast_to(inv, (R, 128))

    def attention(s, u):
        keys = (u + 1) * HALF
        rows = stream(u)

        def body(h):
            b = 2 * h + s
            bias = jnp.concatenate(
                [prm[b, 7:8, 0:128], jnp.zeros((1, 128), F32), prm[b, 7:8, 128:256]], axis=1
            )
            qkv[s, h, rows, :] = (dot_nn(a1[s, rows, :], planes(b, slice(None))) + bias).astype(BF16)
            query = qkv[s, h, rows, 0:128]
            key, value = qkv[s, h, 0:keys, 128:256], qkv[s, h, 0:keys, 256:384]
            parts = []
            for e in (0, 1):
                scores = dot_nt(pick_head(query, e), key) * SCALE + mask[rows, 0:keys]
                weights = jnp.exp(scores - jnp.max(scores, axis=-1, keepdims=True))
                probs = (weights / jnp.sum(weights, axis=-1, keepdims=True)).astype(BF16)
                prob[s, h, e, rows, 0:keys] = probs
                parts.append(dot_nn(probs, value))
            mix[s, h, rows, :] = jnp.where(low_lanes(HALF), parts[0], parts[1]).astype(BF16)

        unrolled(2, body)

    def partial(k, u, tile):
        rows = stream(u)

        def body(n):
            cols = ds(n * 256, 256)
            value = tile(rows, cols)
            acc[rows, cols] = value
            rs_out[k // 2, rows, cols] = value.astype(BF16)

        unrolled(4, body)
        rs_start(k, u)

    def feed_up(s, u):
        rows = stream(u)

        def body(i):
            h, n = div(i, 2), rem(i, 2)
            b = 2 * h + s
            cols = ds(n * 256, 256)
            v = dot_nn(a2[s, rows, :], wu[b, :, cols]) + prm[b, 6:7, cols]
            th = jnp.tanh(GELU_COEF * (v + CUBIC_COEF * v * v * v))
            hid[s, h, rows, cols] = (0.5 * v * (1.0 + th)).astype(BF16)
            slope[s, h, rows, cols] = 0.5 * (1.0 + th) + 0.5 * v * (1.0 - th * th) * GELU_COEF * (
                1.0 + 3.0 * CUBIC_COEF * v * v
            )

        unrolled(4, body)

    def forward(s, hooks):
        k = 4 * s
        target = xs_buf.at[1] if s == 0 else xo
        for u in (0, 1):
            if s == 1:
                ag_finish(3, u, xs_buf.at[1])
            first_norm(s, u)
            if u == 0:
                hooks[0]()
                w_ready(s, WQ)
            attention(s, u)
            if u == 0:
                hooks[1]()
                w_ready(s, WO)
            partial(
                k, u,
                lambda rows, cols: dot_nn(mix[s, 0, rows, :], wo[s, :, cols])
                + dot_nn(mix[s, 1, rows, :], wo[s + 2, :, cols]),
            )
        hooks[2]()
        for u in (0, 1):
            first_own(s, u)
            middle = xs_buf[s, own(u), :].astype(F32) + rs_finish(k, u) + prm[s, 0:1, :]
            yrow[u] = middle
            normed, inv = norm(middle)
            a2[s, own(u), :] = (normed * prm[s, 3:4, :] + prm[s, 5:6, :]).astype(BF16)
            ag_start(k + 1, u, a2.at[s])
            n2[s, u] = normed
            i2[s, u] = jnp.broadcast_to(inv, (R, 128))
        hooks[3]()
        w_ready(s, WU)
        for u in (0, 1):
            ag_finish(k + 1, u, a2.at[s])
            feed_up(s, u)
            if u == 0:
                hooks[4]()
                w_ready(s, WD)
            partial(
                k + 2, u,
                lambda rows, cols: dot_nn(hid[s, 0, rows, :], wd[s, :, cols])
                + dot_nn(hid[s, 1, rows, :], wd[s + 2, :, cols]),
            )
        hooks[5]()
        for u in (0, 1):
            target[own(u), :] = (yrow[u] + rs_finish(k + 2, u) + prm[s, 1:2, :]).astype(BF16)
            ag_start(k + 3, u, target)

    load_x.wait()
    for d in (1, 2, 3):
        send_prm(d).wait_recv()

    def f0_0():
        w_spread(0, WQ)
        w_spread(0, WO)
        w_hand_over(0, WQ)

    def f0_1():
        w_hand_over(0, WO)

    def f0_2():
        w_spread(0, WU)

    def f0_3():
        w_spread(0, WD)
        for k in range(4):
            w_send_kind(1, k)
        w_hand_over(0, WU)

    def f0_4():
        w_hand_over(0, WD)

    def f0_5():
        w_spread(1, WQ)
        w_spread(1, WO)
        w_spread(1, WU)

    def f1_0():
        w_hand_over(1, WQ)
        w_hand_over(1, WO)

    def f1_2():
        w_spread(1, WD)
        out_start(0, 0, xs_buf.at[1], so_out)

    def f1_3():
        w_hand_over(1, WU)

    def f1_4():
        w_hand_over(1, WD)

    def nothing():
        pass

    forward(0, [f0_0, f0_1, f0_2, f0_3, f0_4, f0_5])
    forward(1, [f1_0, nothing, f1_2, f1_3, f1_4, nothing])
    load_g.wait()

    def attention_back(s, u):
        rows = stream(u)
        keys = (u + 1) * HALF

        def body(h):
            grad_mix = dot_nt(dyb[s, rows, :], wo[2 * h + s]).astype(BF16)
            query = qkv[s, h, rows, 0:128]
            key, value = qkv[s, h, 0:keys, 128:256], qkv[s, h, 0:keys, 256:384]
            parts = []
            for e in (0, 1):
                probs = prob[s, h, e, rows, 0:keys]
                wide = probs.astype(F32)
                grad_prob = dot_nt(pick_head(grad_mix, e), value)
                delta = jnp.sum(wide * grad_prob, axis=-1, keepdims=True)
                grad_scores = (wide * (grad_prob - delta) * SCALE).astype(BF16)
                parts.append((dot_nn(grad_scores, key), dot_tn(grad_scores, query), dot_tn(probs, grad_mix)))
            dqkv[h, rows, 0:128] = jnp.where(low_lanes(HALF), parts[0][0], parts[1][0]).astype(BF16)
            for j in (1, 2):
                both = jnp.where(low_lanes(keys), parts[0][j], parts[1][j])
                cols = slice(j * 128, j * 128 + 128)
                if u == 1:
                    dqkv[h, rows, cols] = both[HALF:, :].astype(BF16)
                    dkv[h, :, (j - 1) * 128 : j * 128] = both[:HALF, :]
                else:
                    dqkv[h, rows, cols] = (both + dkv[h, :, (j - 1) * 128 : j * 128]).astype(BF16)

        unrolled(2, body)

    def add_row(s, i, value):
        sm[s, i : i + 1, :] = sm[s, i : i + 1, :] + jnp.sum(value, axis=0, keepdims=True)

    def backward(s, k, hooks):
        for u in (1, 0):
            rows = stream(u)
            if s == 0:
                ag_finish(11, u, g_buf.at[0])

            def grad_up_tile(i):
                h, n = div(i, 2), rem(i, 2)
                cols = ds(n * 256, 256)
                value = dot_nt(g_buf[s, rows, :], wd[2 * h + s, cols, :]) * slope[s, h, rows, cols]
                du[h, rows, cols] = value.astype(BF16)

            unrolled(4, grad_up_tile)
            partial(
                k, u,
                lambda rows, cols: dot_nt(du[0, rows, :], wu[s, cols, :]) + dot_nt(du[1, rows, :], wu[s + 2, cols, :]),
            )

        def grad_down(i):
            h, n = div(i, 2), rem(i, 2)
            rows = ds(n * 256, 256)
            gd[s, h, rows, :] = dot_tn(hid[s, h, :, rows], g_buf[s]).astype(BF16)

        unrolled(4, grad_down)
        gc_start(s, WD)
        hooks[0]()
        for u in (1, 0):
            top = g_buf[s, own(u), :].astype(F32)
            g_second = rs_finish(k, u)
            normed = n2[s, u]
            dy = top + norm_back(g_second, normed, i2[s, u, :, 0:1], prm[s, 3:4, :])
            dyb[s, own(u), :] = dy.astype(BF16)
            ag_start(k + 1, u, dyb.at[s])
            dyrow[u] = dy
            add_row(s, 1, top)
            add_row(s, 3, g_second * normed)
            add_row(s, 5, g_second)
            add_row(s, 0, dy)

        def grad_up(i):
            h, n = div(i, 4), rem(i, 4)
            rows = ds(n * 256, 256)
            gu[s, h, rows, :] = dot_tn(a2[s, :, rows], du[h]).astype(BF16)

        unrolled(8, grad_up)
        gc_start(s, WU)
        for h in (0, 1):
            sm[s, 6:7, h * 512 : h * 512 + 512] = jnp.sum(du[h].astype(F32), axis=0, keepdims=True)
        hooks[1]()
        for u in (1, 0):
            ag_finish(k + 1, u, dyb.at[s])
            attention_back(s, u)
            partial(
                k + 2, u,
                lambda rows, cols: dot_nt(dqkv[0, rows, :], planes(s, cols)) + dot_nt(dqkv[1, rows, :], planes(s + 2, cols)),
            )

        def grad_qkv(i):
            h, n = div(i, 4), rem(i, 4)
            rows = ds(n * 256, 256)
            value = dot_tn(a1[s, :, rows], dqkv[h]).astype(BF16)
            for j in range(3):
                gq[s, h, j, rows, :] = value[:, j * 128 : j * 128 + 128]

        unrolled(8, grad_qkv)
        gc_start(s, WQ)
        for h in (0, 1):
            go[s, h] = dot_tn(mix[s, h], dyb[s]).astype(BF16)
        gc_start(s, WO)
        for h in (0, 1):
            sums = jnp.sum(dqkv[h].astype(F32), axis=0, keepdims=True)
            sm[s, 7:8, h * 256 : h * 256 + 128] = sums[:, 0:128]
            sm[s, 7:8, h * 256 + 128 : h * 256 + 256] = sums[:, 256:384]
        hooks[2]()
        target = g_buf.at[0] if s == 1 else ig0
        for u in (1, 0):
            g_first = rs_finish(k + 2, u)
            normed = n1[s, u]
            low = dyrow[u] + norm_back(g_first, normed, i1[s, u, :, 0:1], prm[s, 2:3, :])
            target[own(u), :] = low.astype(BF16)
            if s == 1:
                ag_start(k + 3, u, target)
            else:
                low_start(u)
            add_row(s, 2, g_first * normed)
            add_row(s, 4, g_first)
        hooks[3]()

    def b1_0():
        for u in (0, 1):
            ag_finish(7, u, xo)
        out_start(1, 1, xo, so_out)

    def b1_1():
        stage1(1, WD)

    def b1_2():
        stage1(1, WU)
        stage2(1, WD)

    def b1_3():
        stage1(1, WQ)
        stage1(1, WO)

    backward(1, 8, [b1_0, b1_1, b1_2, b1_3])

    def b0_0():
        out_start(2, 1, g_buf.at[0], ig_out)
        stage2(1, WU)
        stage3(1, WD)
        stage2(1, WO)

    def b0_1():
        stage1(0, WD)
        stage3(1, WU)
        stage2(1, WQ)

    def b0_2():
        stage1(0, WU)
        stage2(0, WD)
        stage1(0, WQ)
        stage1(0, WO)
        stage3(1, WO)
        stage3(1, WQ)
        stage4(1, WD)

    def b0_3():
        stage2(0, WU)
        stage4(1, WU)
        stage2(0, WO)

    backward(0, 12, [b0_0, b0_1, b0_2, b0_3])

    def small_copy(i, src, dst, device):
        return remote(src, dst, sm_s.at[i], sm_r.at[i], device)

    small_c = [small_copy(0, sm, smc, core_peer)]
    small_z = [small_copy(d, sm1, smz.at[d - 1], dev(x, y, zp(d), c)) for d in (1, 2, 3)]
    small_y = [small_copy(3 + d, sm2, smy.at[d - 1], dev(x, yp(d), z, c)) for d in (1, 2, 3)]
    small_x = [small_copy(6 + d, sm3, smx.at[d - 1], dev(xp(d), y, z, c)) for d in (1, 2, 3)]

    def start_all(copies):
        for copy in copies:
            copy.start()

    def arrived(copies):
        for copy in copies:
            copy.wait_recv()

    start_all(small_c)
    stage2(0, WQ)
    stage3(0, WU)
    arrived(small_c)
    sm1[...] = sm[...] + smc[...]
    start_all(small_z)
    stage4(1, WO)
    stage4(1, WQ)
    stage3(0, WD)
    stage3(0, WQ)
    stage3(0, WO)
    arrived(small_z)
    sm2[...] = sm1[...] + smz[0] + smz[1] + smz[2]
    start_all(small_y)
    for k in range(4):
        stage5(1, k)
    stage4(0, WU)
    arrived(small_y)
    sm3[...] = sm2[...] + smy[0] + smy[1] + smy[2]
    start_all(small_x)
    stage4(0, WD)
    stage4(0, WO)
    stage4(0, WQ)
    arrived(small_x)
    mine = sm3[p]
    shared = mine + smx[0, p] + smx[1, p] + smx[2, p]
    row = lax.broadcasted_iota(jnp.int32, (8, D), 0)
    small_out[...] = jnp.where(row < 6, shared, mine)
    for k in (WU, WD, WO, WQ):
        stage5(0, k)
    for k in (WU, WD, WO, WQ):
        gf_finish(k)

    out_finish(0, 0, xs_buf.at[1], so_out)
    out_finish(1, 1, xo, so_out)
    out_finish(2, 1, g_buf.at[0], ig_out)
    for u in (1, 0):
        low_finish(u)
    for d in (1, 2, 3):
        send_prm(d).wait_send()
    for s in (0, 1):
        for k in range(4):
            if k not in Z_FIRST:
                @pl.when(p == s)
                def _():
                    for d in (1, 2, 3):
                        gz_copy(s, k, 0, d).wait_send()

            def sent(d):
                if d == 2:
                    for e in (1, 3):
                        w_send(k, e).wait_send()
                else:
                    w_relay(k, 0 if d == 1 else 1).wait_send()
                for j in (0, 1):
                    w_side(k, d, j).wait_send()
                for j in (0, 1, 2):
                    w_pass(k, d, j).wait_send()

            w_each(s, sent)

            for h in (0, 1):
                gc_copy(s, k, h).wait_send()
                if k in Z_FIRST:
                    for d in (1, 2, 3):
                        gz_copy(s, k, h, d).wait_send()

            for j in (0, 1):
                @pl.when(p == s)
                def _():
                    relay_copy(s, k, j).wait_send()

                @pl.when(p != s)
                def _():
                    main_copy(s, k, j).wait_send()

    gathered = {
        1: a2.at[0], 3: xs_buf.at[1], 5: a2.at[1], 7: xo, 9: dyb.at[1], 11: g_buf.at[0], 13: dyb.at[0],
    }
    for u in (0, 1):
        for d in (1, 2, 3):
            for k in range(0, 16, 2):
                rs_copy(k, u, d).wait_send()
            for k, ref in gathered.items():
                ag_copy(k, u, ref, d).wait_send()
    for copy in small_c + small_z + small_y + small_x:
        copy.wait_send()


def finish_kernel(
    so_in, ig_in, gq_in, go_in, gu_in, gd_in, small_in,
    so_out, ig_out, gq_out, go_out, gu_out, gd_out, outb, downb, gains, shifts, upb, qvb,
    so_buf, ig_buf, gq_buf, go_buf, gu_buf, gd_buf, gq_f, go_f, gu_f, gd_f, l_sem, s_sem,
):
    ins = (gu_in, gd_in, so_in, ig_in, gq_in, go_in)
    bufs = (gu_buf, gd_buf, so_buf, ig_buf, gq_buf, go_buf)
    wide = (gu_f, gd_f, None, None, gq_f, go_f)
    outs = (gu_out, gd_out, so_out, ig_out, gq_out, go_out)
    loads = [pltpu.make_async_copy(ins[i], bufs[i], l_sem.at[i]) for i in range(6)]
    for copy in loads:
        copy.start()
    h = lax.div(lax.axis_index("tensor"), 4)
    outb[...] = small_in[0:1, :]
    downb[...] = small_in[1:2, :]
    gains[...] = small_in[2:4, :]
    shifts[...] = small_in[4:6, :]
    upb[...] = jnp.where(h == 0, small_in[6:7, 0:512], small_in[6:7, 512:1024])
    qvb[0:1, :] = jnp.where(h == 0, small_in[7:8, 0:128], small_in[7:8, 256:384])
    qvb[1:2, :] = jnp.where(h == 0, small_in[7:8, 128:256], small_in[7:8, 384:512])
    stores = []
    for i in range(6):
        loads[i].wait()
        source = bufs[i]
        if wide[i] is not None:
            source = wide[i]
            lead = source.shape[0]
            step = lead if len(source.shape) == 3 else 64

            def body(r):
                if len(source.shape) == 3:
                    rows = ds(r * 128, 128)
                    wide[i][:, rows, :] = bufs[i][:, rows, :].astype(F32)
                else:
                    rows = ds(r * 64, 64)
                    wide[i][rows, :] = bufs[i][rows, :].astype(F32)

            loop(8 if len(source.shape) == 3 else lead // step, body)
        stores.append(pltpu.make_async_copy(source, outs[i], s_sem.at[i]))
        stores[-1].start()
    for copy in stores:
        copy.wait()


def run(x_in, seg, wq, qvb, wo, outb, wu, upb, wd, downb, gain, shift, og):
    any_spec = pl.BlockSpec(memory_space=pl.ANY)
    vmem = pl.BlockSpec(memory_space=pltpu.VMEM)
    V = pltpu.VMEM
    dma = pltpu.SemaphoreType.DMA
    tokens = x_in.shape[0]

    def kinds(lead, shrink):
        return [V(tuple(lead) + shape_of(k, ROWS[k] // shrink), BF16) for k in range(4)]

    scratch = kinds((4,), 1)
    scratch += [
        V((4, 8, D), F32), V((SEQ, SEQ), F32),
        V((2, SEQ, D), BF16), V((2, SEQ, D), BF16), V((2, SEQ, D), BF16), V((2, SEQ, D), BF16), V((2, SEQ, D), BF16),
        V((SEQ, D), BF16), V((SEQ, D), BF16),
        V((2, 2, SEQ, 384), BF16), V((2, 2, 2, SEQ, SEQ), BF16), V((2, 2, SEQ, 128), BF16),
        V((2, 2, SEQ, 512), BF16), V((2, 2, SEQ, 512), F32),
        V((2, SEQ, 512), BF16), V((2, SEQ, 384), BF16), V((2, HALF, 256), F32), V((SEQ, D), F32),
        V((8, SEQ, D), BF16), V((8, 2, 3, R, D), BF16),
        V((2, 2, R, D), F32), V((2, 2, R, D), F32), V((2, 2, R, 128), F32), V((2, 2, R, 128), F32),
        V((2, R, D), F32), V((2, R, D), F32),
    ]
    scratch += kinds((2, 2), 1) + kinds((2, 2), 2)
    scratch += [V((2,) + shape_of(k, ROWS[k] // (8 if k in Z_FIRST else 2)), BF16) for k in range(4)]
    scratch += [V((2,) + shape_of(k, ROWS[k] // (16 if k in Z_FIRST else 4)), BF16) for k in range(4)]
    scratch += [V(((2, 2, 3) if k in Z_FIRST else (3,)) + shape_of(k, ROWS[k] // 8), BF16) for k in range(4)]
    scratch += kinds((), 1)
    scratch += [V((2, 8, D), F32)] * 5 + [V((3, 2, 8, D), F32)] * 3
    sems = (96, 96, 12, 12, 24, 24, 36, 36, 8, 8, 3, 3, 6, 16, 16, 8, 8, 8, 8, 60, 60, 12, 12, 4, 4, 4, 10, 10, 9, 9, 3, 30, 30, 2)
    scratch += [dma((n,)) for n in sems]
    grads = [jax.ShapeDtypeStruct(shape_of(k, ROWS[k]), BF16) for k in range(4)]
    rows = jax.ShapeDtypeStruct((tokens, D), BF16)
    parts = pl.pallas_call(
        kernel,
        out_shape=(rows, rows, *grads, jax.ShapeDtypeStruct((8, D), F32)),
        in_specs=[any_spec, vmem, any_spec, vmem, any_spec, vmem, any_spec, vmem, any_spec, vmem, vmem, vmem, any_spec],
        out_specs=(any_spec,) * 6 + (vmem,),
        scratch_shapes=scratch,
        compiler_params=pltpu.CompilerParams(collective_id=0, has_side_effects=True, vmem_limit_bytes=64 * 1024 * 1024),
    )(x_in, seg, wq, qvb, wo, outb, wu, upb, wd, downb, gain, shift, og)

    def f32(*shape):
        return jax.ShapeDtypeStruct(shape, F32)

    return pl.pallas_call(
        finish_kernel,
        out_shape=(
            rows, rows, *[f32(*shape_of(k, ROWS[k])) for k in range(4)],
            f32(1, D), f32(1, D), f32(2, D), f32(2, D), f32(1, 512), f32(2, 128),
        ),
        in_specs=[any_spec] * 6 + [vmem],
        out_specs=(any_spec,) * 6 + (vmem,) * 6,
        scratch_shapes=[
            V((tokens, D), BF16), V((tokens, D), BF16), *kinds((), 1),
            *[V(shape_of(k, ROWS[k]), F32) for k in range(4)], dma((6,)), dma((6,)),
        ],
        compiler_params=pltpu.CompilerParams(vmem_limit_bytes=62 * 1024 * 1024),
    )(*parts)


def on_device(
    section_input, segment_ids, w_qkv, qv_bias, w_out, out_bias, w_up, up_bias, w_down, down_bias, norm_gains,
    norm_shifts, out_grad,
):
    so, ig, gq, go, gu, gd, outb, downb, gains, shifts, upb, qvb = run(
        section_input, segment_ids.reshape(8, 128), w_qkv[0].transpose(1, 0, 2), qv_bias[0], w_out[0], out_bias,
        w_up[0], up_bias, w_down[0], down_bias, norm_gains[0], norm_shifts[0], out_grad,
    )
    return (
        so[None], ig[None], gq.transpose(1, 0, 2)[None], qvb[None], go[None], outb, gu[None], upb, gd[None], downb,
        gains[None], shifts[None],
    )


def solution(mesh):
    placed = (
        P("dp", None),
        P("dp"),
        P("pipe", None, None, "tensor"),
        P("pipe", None, "tensor"),
        P("pipe", "tensor", None),
        P("pipe", None),
        P("pipe", None, "tensor"),
        P("pipe", "tensor"),
        P("pipe", "tensor", None),
        P("pipe", None),
        P("pipe", None, None),
        P("pipe", None, None),
        P("dp", None),
    )
    return jax.shard_map(
        on_device,
        mesh=mesh,
        in_specs=placed,
        out_specs=(
            P("pipe", "dp", None),
            P("pipe", "dp", None),
            P("pipe", None, None, "tensor"),
            P("pipe", None, "tensor"),
            P("pipe", "tensor", None),
            P("pipe", None),
            P("pipe", None, "tensor"),
            P("pipe", "tensor"),
            P("pipe", "tensor", None),
            P("pipe", None),
            P("pipe", None, None),
            P("pipe", None, None),
        ),
        check_vma=False,
    )
```

```python
import jax
import jax.numpy as jnp
from jax import lax
from jax.experimental import pallas as pl
from jax.experimental.pallas import tpu as pltpu
from jax.sharding import PartitionSpec as P

MESH = pl.DeviceIdType.MESH
F32 = jnp.float32
BF16 = jnp.bfloat16

SEQ = 256
D = 1024
HALF = 128
R = 32
NORM_EPS = 1e-05
GELU_COEF = 0.7978845608028654
CUBIC_COEF = 0.044715
MASKED_SCORE = -1e30
SCALE = 0.125
WQ, WO, WU, WD = range(4)
ROWS = (1024, 128, 1024, 512)
COLS = (128, 1024, 512, 1024)
Z_FIRST = (WQ, WU, WD)


def dot_nn(a, b):
    return jnp.dot(a, b, preferred_element_type=F32)


def dot_nt(a, b):
    return lax.dot_general(a, b, (((1,), (1,)), ((), ())), preferred_element_type=F32)


def dot_tn(a, b):
    return lax.dot_general(a, b, (((0,), (0,)), ((), ())), preferred_element_type=F32)


def loop(n, body):
    lax.fori_loop(0, n, lambda i, c: (body(i), c)[1], 0)


def unrolled(n, body):
    for i in range(n):
        body(i)


def div(a, b):
    return a // b if isinstance(a, int) else lax.div(a, b)


def rem(a, b):
    return a % b if isinstance(a, int) else lax.rem(a, b)


def ds(start, size):
    if isinstance(start, int):
        return pl.ds(start, size)
    return pl.ds(pl.multiple_of(start, size), size)


def norm(rows):
    centred = rows - jnp.mean(rows, axis=-1, keepdims=True)
    inv = lax.rsqrt(jnp.mean(centred * centred, axis=-1, keepdims=True) + NORM_EPS)
    return centred * inv, inv


def norm_back(grad, normed, inv, gain):
    e = grad * gain
    return inv * (
        e - jnp.mean(e, axis=-1, keepdims=True) - normed * jnp.mean(e * normed, axis=-1, keepdims=True)
    )


def shape_of(k, rows):
    return (3, rows, 128) if k == WQ else (rows, COLS[k])


def at(k, rows):
    return (slice(None), rows) if k == WQ else (rows,)


def kernel(
    x_in, seg_in, wq_in, qvb_in, wo_in, outb_in, wu_in, upb_in, wd_in, downb_in, gain_in, shift_in, og_in,
    so_out, ig_out, gq_out, go_out, gu_out, gd_out, small_out,
    wq, wo, wu, wd, prm, mask, xs_buf, g_buf, a1, a2, dyb, xo, ig0, qkv, prob, mix, hid, slope, du, dqkv, dkv, acc,
    rs_out, rs_in, n1, n2, i1, i2, yrow, dyrow,
    gq, go, gu, gd, cq, co, cu, cd, yq, yo, yu, yd, rq, ro, ru, rd, zq, zo, zu, zd, fq, fo, fu, fd,
    sm, sm1, sm2, sm3, smc, smz, smy, smx,
    x_s, x_r, wy_s, wy_r, wz_s, wz_r, wc_s, wc_r, wr_s, wr_r, pr_s, pr_r, loc, gc_s, gc_r, gy_s, gy_r, ry_s, ry_r, gz_s, gz_r, ga_s, ga_r,
    gf_s, gf_r, gl, sm_s, sm_r, o_s, o_r, o_l, d_s, d_r, d_l,
):
    p = lax.axis_index("pipe")
    t = lax.axis_index("tensor")
    dp = lax.axis_index("dp")
    h_me, x = lax.div(t, 4), lax.rem(t, 4)
    z, c = lax.div(dp, 2), lax.rem(dp, 2)
    y = h_me * 2 + p

    def dev(xx, yy, zz, cc):
        return {"pipe": lax.rem(yy, 2), "tensor": lax.div(yy, 2) * 4 + xx, "dp": zz * 2 + cc}

    def xp(d):
        return lax.rem(x + d, 4)

    def yp(d):
        return lax.rem(y + d, 4)

    def zp(d):
        return lax.rem(z + d, 4)

    core_peer = dev(x, y, z, 1 - c)

    def remote(src, dst, ss, rs, device):
        return pltpu.make_async_remote_copy(
            src_ref=src, dst_ref=dst, send_sem=ss, recv_sem=rs, device_id=device, device_id_type=MESH
        )

    def stream(u):
        return pl.ds(u * HALF, HALF)

    def own(u):
        return ds(u * HALF + x * R, R)

    w_in = (wq_in, wo_in, wu_in, wd_in)
    w_all = (wq, wo, wu, wd)
    g_all = (gq, go, gu, gd)
    c_all = (cq, co, cu, cd)
    y_all = (yq, yo, yu, yd)
    z_all = (zq, zo, zu, zd)
    r_all = (rq, ro, ru, rd)
    fin = (fq, fo, fu, fd)
    g_outs = (gq_out, go_out, gu_out, gd_out)
    grid_peers = [(dx, dy) for dx in range(4) for dy in range(4) if (dx, dy) != (0, 0)]

    barrier = pltpu.get_barrier_semaphore()
    peers = [dev(xp(dx), yp(dy), z, c) for dx, dy in grid_peers]
    peers += [dev(x, y, zp(d), c) for d in (1, 2, 3)] + [core_peer]
    for peer in peers:
        pl.semaphore_signal(barrier, inc=1, device_id=peer, device_id_type=MESH)

    load_x = pltpu.make_async_copy(x_in.at[ds(y * SEQ, SEQ)], xs_buf.at[0], loc.at[0])
    load_g = pltpu.make_async_copy(og_in.at[ds(y * SEQ, SEQ)], g_buf.at[1], loc.at[1])
    load_x.start()
    load_w = [pltpu.make_async_copy(w_in[k], w_all[k].at[y], loc.at[2 + k]) for k in range(4)]
    for copy in load_w:
        copy.start()
    load_g.start()

    prm[y] = jnp.zeros((8, D), F32)
    prm[y, 0:1, :] = outb_in[...]
    prm[y, 1:2, :] = downb_in[...]
    prm[y, 2:4, :] = gain_in[...]
    prm[y, 4:6, :] = shift_in[...]
    prm[y, 6:7, 0:512] = upb_in[...]
    prm[y, 7:8, 0:128] = qvb_in[0:1, :]
    prm[y, 7:8, 128:256] = qvb_in[1:2, :]
    sm[...] = jnp.zeros_like(sm)

    pl.semaphore_wait(barrier, len(peers))

    def send_prm(d):
        return remote(prm.at[y], prm.at[y], pr_s.at[d - 1], pr_r.at[d - 1], dev(x, yp(d), z, c))

    even = lax.rem(z, 2)

    def half_rows(k, which):
        return ds(which * (ROWS[k] // 2), ROWS[k] // 2)

    def quarter_rows(k, which):
        q = ROWS[k] // 4
        return pl.ds(pl.multiple_of(c * (2 * q) + which * q, q), q)

    def eighth_rows(k, which, j):
        q = ROWS[k] // 8
        return pl.ds(pl.multiple_of(c * (4 * q) + which * (2 * q) + j * q, q), q)

    def w_send(k, d):
        rows = at(k, quarter_rows(k, even))
        i = k * 3 + d - 1
        return remote(
            w_in[k].at[rows], w_all[k].at[(y,) + rows], wy_s.at[i], wy_r.at[i], dev(x, yp(d), z, c)
        )

    def w_block(k, d, rows):
        return w_all[k].at[(lax.rem(y - d + 4, 4),) + at(k, rows)]

    def w_side(k, d, j):
        i = (k * 3 + d - 1) * 2 + j
        block = w_block(k, d, eighth_rows(k, even, j))
        return remote(block, block, wz_s.at[i], wz_r.at[i], dev(x, y, zp(1 if j == 0 else 3), c))

    def w_pass(k, d, j):
        i = (k * 3 + d - 1) * 3 + j
        block = w_block(k, d, quarter_rows(k, even) if j == 0 else eighth_rows(k, 1 - even, j - 1))
        return remote(block, block, wc_s.at[i], wc_r.at[i], core_peer)

    def w_relay(k, j):
        block = w_block(k, 1 if j == 0 else 3, eighth_rows(k, even, j))
        i = k * 2 + j
        return remote(block, block, wr_s.at[i], wr_r.at[i], dev(x, yp(1 if j == 0 else 3), z, c))

    def w_relayed(k, j):
        block = w_block(k, 2, eighth_rows(k, even, j))
        i = k * 2 + j
        return remote(block, block, wr_s.at[i], wr_r.at[i], dev(x, yp(1 if j == 0 else 3), z, c))

    def w_send_kind(s, k):
        @pl.when(p == s)
        def _():
            for d in (1, 3):
                w_send(k, d).start()

    def w_each(s, act):
        @pl.when(p == s)
        def _():
            act(2)

        @pl.when(p != s)
        def _():
            act(1)
            act(3)

    def w_spread(s, k):
        def act(d):
            if d == 2:
                w_relayed(k, 0).wait_recv()
                w_side(k, d, 0).start()
                w_relayed(k, 1).wait_recv()
                w_side(k, d, 1).start()
            else:
                w_send(k, d).wait_recv()
                w_relay(k, 0 if d == 1 else 1).start()
                for j in (0, 1):
                    w_side(k, d, j).start()
            w_pass(k, d, 0).start()

        w_each(s, act)

    def w_hand_over(s, k):
        def act(d):
            for j in (0, 1):
                w_side(k, d, j).wait_recv()
                w_pass(k, d, 1 + j).start()

        w_each(s, act)

    def w_ready(s, k):
        @pl.when(p == s)
        def _():
            load_w[k].wait()

        def act(d):
            for j in (0, 1, 2):
                w_pass(k, d, j).wait_recv()

        w_each(s, act)

    def x_sem(k, u, d):
        return (k * 2 + u) * 3 + d - 1

    def rs_copy(k, u, d):
        dest = xp(d)
        i = x_sem(k, u, d)
        return remote(
            rs_out.at[k // 2, ds(u * HALF + dest * R, R)], rs_in.at[k // 2, u, d - 1], x_s.at[i], x_r.at[i],
            dev(dest, y, z, c),
        )

    def rs_start(k, u):
        for d in (2, 1, 3):
            rs_copy(k, u, d).start()

    def rs_finish(k, u):
        total = acc[own(u), :]
        for d in (1, 3, 2):
            rs_copy(k, u, d).wait_recv()
            total = total + rs_in[k // 2, u, d - 1].astype(F32)
        return total

    def ag_copy(k, u, ref, d):
        i = x_sem(k, u, d)
        block = ref.at[own(u)]
        return remote(block, block, x_s.at[i], x_r.at[i], dev(xp(d), y, z, c))

    def ag_start(k, u, ref):
        for d in (2, 1, 3):
            ag_copy(k, u, ref, d).start()

    def ag_finish(k, u, ref):
        for d in (1, 3, 2):
            ag_copy(k, u, ref, d).wait_recv()

    def out_copy(i, ref, out, d):
        j = i * 3 + d - 1
        return remote(ref, out.at[ds(y * SEQ, SEQ)], o_s.at[j], o_r.at[j], dev(x, yp(d), z, c))

    def out_local(i, ref, out):
        return pltpu.make_async_copy(ref, out.at[ds(y * SEQ, SEQ)], o_l.at[i])

    def out_start(i, s, ref, out):
        for d in (1, 2, 3):
            @pl.when(lax.rem(y + d, 2) == s)
            def _():
                out_copy(i, ref, out, d).start()

        @pl.when(p == s)
        def _():
            out_local(i, ref, out).start()

    def out_finish(i, s, ref, out):
        for d in (1, 2, 3):
            @pl.when(lax.rem(y + d, 2) == s)
            def _():
                out_copy(i, ref, out, d).wait_send()

        @pl.when(p == s)
        def _():
            out_local(i, ref, out).wait()
            for d in (1, 2, 3):
                out_copy(i, ref, out, d).wait_recv()

    def low_rows(u):
        return ds(y * SEQ + u * HALF + x * R, R)

    def low_copy(u, j):
        dx, dy = grid_peers[j]
        i = u * 15 + j
        return remote(ig0.at[own(u)], ig_out.at[low_rows(u)], d_s.at[i], d_r.at[i], dev(xp(dx), yp(dy), z, c))

    def low_local(u):
        return pltpu.make_async_copy(ig0.at[own(u)], ig_out.at[low_rows(u)], d_l.at[u])

    def low_start(u):
        for j, (dx, dy) in enumerate(grid_peers):
            @pl.when(lax.rem(y + dy, 2) == 0)
            def _():
                low_copy(u, j).start()

        @pl.when(p == 0)
        def _():
            low_local(u).start()

    def low_finish(u):
        for j, (dx, dy) in enumerate(grid_peers):
            @pl.when(lax.rem(y + dy, 2) == 0)
            def _():
                low_copy(u, j).wait_send()

        @pl.when(p == 0)
        def _():
            low_local(u).wait()
            for j in range(15):
                low_copy(u, j).wait_recv()

    def gc_copy(s, k, h):
        i = (s * 4 + k) * 2 + h
        return remote(
            g_all[k].at[(s, h) + at(k, half_rows(k, 1 - c))], c_all[k].at[s, h], gc_s.at[i], gc_r.at[i], core_peer
        )

    def gc_start(s, k):
        for h in (0, 1):
            gc_copy(s, k, h).start()

    def sum_rows(k, target, base, sources, rows, result=None):
        step = min(rows, 64)
        result = target if result is None else result

        def body(r):
            here = at(k, pl.ds(pl.multiple_of(base + r * step, 16), step))
            there = at(k, pl.ds(pl.multiple_of(r * step, 16), step))
            if len(sources) == 1:
                result[here] = target[here] + sources[0][there]
                return
            total = target[here].astype(F32)
            for source in sources:
                total = total + source[there].astype(F32)
            result[here] = total.astype(BF16)

        loop(rows // step, body)

    def piece_base(k, zz):
        return c * (ROWS[k] // 2) + zz * (ROWS[k] // 8)

    def piece(k, zz):
        return at(k, pl.ds(pl.multiple_of(piece_base(k, zz), 16), ROWS[k] // 8))

    def region(k):
        return (piece_base(k, z), ROWS[k] // 8) if k in Z_FIRST else (c * (ROWS[k] // 2), ROWS[k] // 2)

    def y_side(j):
        return yp(1 if j == 0 else 3)

    def relay_copy(s, k, j):
        base, n = region(k)
        rows = at(k, pl.ds(pl.multiple_of(base + j * (n // 2), 16), n // 2))
        i = k * 2 + j
        return remote(
            g_all[k].at[(s, 1 - h_me) + rows], r_all[k].at[j], ry_s.at[i], ry_r.at[i], dev(x, y_side(j), z, c)
        )

    def main_copy(s, k, j):
        base, n = region(k)
        rows = at(k, pl.ds(pl.multiple_of(base, 16), n))
        i = k * 2 + j
        block = lax.div(y_side(j), 2)
        return remote(
            g_all[k].at[(s, block) + rows], y_all[k].at[j], gy_s.at[i], gy_r.at[i], dev(x, y_side(j), z, c)
        )

    def relay_start(s, k):
        @pl.when(p == s)
        def _():
            for j in (0, 1):
                relay_copy(s, k, j).start()

    def main_start(s, k):
        @pl.when(p != s)
        def _():
            base, n = region(k)
            for j in (0, 1):
                relay_copy(s, k, j).wait_recv()
                sum_rows(
                    k, g_all[k].at[s, lax.div(y_side(j), 2)], base + j * (n // 2), [r_all[k].at[j]], n // 2
                )
                main_copy(s, k, j).start()

    def main_arrived(s, k):
        for j in (0, 1):
            main_copy(s, k, j).wait_recv()
        return [y_all[k].at[j] for j in (0, 1)]

    def gz_copy(s, k, h, d):
        zz = zp(d)
        i = ((s * 4 + k) * 2 + h) * 3 + d - 1 if k in Z_FIRST else 48 + k * 3 + d - 1
        block = h if k in Z_FIRST else h_me
        slot = z_all[k].at[s, h, d - 1] if k in Z_FIRST else z_all[k].at[d - 1]
        return remote(g_all[k].at[(s, block) + piece(k, zz)], slot, gz_s.at[i], gz_r.at[i], dev(x, y, zz, c))

    def ga_copy(k, d):
        i = k * 3 + d - 1
        block = fin[k].at[piece(k, z)]
        return remote(block, block, ga_s.at[i], ga_r.at[i], dev(x, y, zp(d), c))

    def gf_copy(k):
        rows = at(k, half_rows(k, c))
        return remote(fin[k].at[rows], g_outs[k].at[rows], gf_s.at[k], gf_r.at[k], core_peer)

    def gf_local(k):
        rows = at(k, half_rows(k, c))
        return pltpu.make_async_copy(fin[k].at[rows], g_outs[k].at[rows], gl.at[k])

    def stage1(s, k):
        for h in (0, 1):
            gc_copy(s, k, h).wait_recv()
            sum_rows(k, g_all[k].at[s, h], c * (ROWS[k] // 2), [c_all[k].at[s, h]], ROWS[k] // 2)
            if k in Z_FIRST:
                for d in (2, 1, 3):
                    gz_copy(s, k, h, d).start()
        if k not in Z_FIRST:
            relay_start(s, k)

    def stage2(s, k):
        if k in Z_FIRST:
            for h in (0, 1):
                for d in (1, 3, 2):
                    gz_copy(s, k, h, d).wait_recv()
                slots = [z_all[k].at[s, h, j] for j in range(3)]
                sum_rows(k, g_all[k].at[s, h], piece_base(k, z), slots, ROWS[k] // 8)
            relay_start(s, k)
        else:
            main_start(s, k)

    def stage3(s, k):
        if k in Z_FIRST:
            main_start(s, k)
        else:
            @pl.when(p == s)
            def _():
                slots = main_arrived(s, k)
                sum_rows(k, g_all[k].at[s, h_me], c * (ROWS[k] // 2), slots, ROWS[k] // 2)
                for d in (2, 1, 3):
                    gz_copy(s, k, 0, d).start()

    def stage4(s, k):
        @pl.when(p == s)
        def _():
            if k in Z_FIRST:
                slots = main_arrived(s, k)
            else:
                for d in (1, 3, 2):
                    gz_copy(s, k, 0, d).wait_recv()
                slots = [z_all[k].at[j] for j in range(3)]
            sum_rows(k, g_all[k].at[s, h_me], piece_base(k, z), slots, ROWS[k] // 8, fin[k])
            for d in (2, 1, 3):
                ga_copy(k, d).start()

    def stage5(s, k):
        @pl.when(p == s)
        def _():
            for d in (1, 3, 2):
                ga_copy(k, d).wait_recv()
            gf_copy(k).start()
            gf_local(k).start()

    def gf_finish(k):
        gf_local(k).wait()
        gf_copy(k).wait()
        for d in (1, 2, 3):
            ga_copy(k, d).wait_send()

    for d in (1, 3, 2):
        send_prm(d).start()
    for k in range(4):
        w_send_kind(0, k)

    seg = jnp.concatenate([seg_in[pl.ds(2 * y, 1), :], seg_in[pl.ds(2 * y + 1, 1), :]], axis=1).astype(F32)
    seg_b = jnp.broadcast_to(seg, (SEQ, SEQ))
    rows_i = lax.broadcasted_iota(jnp.int32, (SEQ, SEQ), 0)
    cols_i = lax.broadcasted_iota(jnp.int32, (SEQ, SEQ), 1)
    mask[...] = jnp.where((rows_i >= cols_i) & (seg_b == seg_b.T), 0.0, MASKED_SCORE)

    def low_lanes(rows):
        return lax.broadcasted_iota(jnp.int32, (rows, 128), 1) < 64

    def pick_head(value, e):
        keep = low_lanes(value.shape[0])
        keep = keep if e == 0 else jnp.logical_not(keep)
        return jnp.where(keep, value, jnp.zeros_like(value))

    def planes(b, rows):
        return jnp.concatenate([wq[b, 0, rows, :], wq[b, 1, rows, :], wq[b, 2, rows, :]], axis=1)

    def first_norm(s, u):
        def body(r):
            rows = ds(u * HALF + r * 64, 64)
            normed, _ = norm(xs_buf[s, rows, :].astype(F32))
            a1[s, rows, :] = (normed * prm[s, 2:3, :] + prm[s, 4:5, :]).astype(BF16)

        unrolled(2, body)

    def first_own(s, u):
        normed, inv = norm(xs_buf[s, own(u), :].astype(F32))
        n1[s, u] = normed
        i1[s, u] = jnp.broadcast_to(inv, (R, 128))

    def attention(s, u):
        keys = (u + 1) * HALF
        rows = stream(u)

        def body(h):
            b = 2 * h + s
            bias = jnp.concatenate(
                [prm[b, 7:8, 0:128], jnp.zeros((1, 128), F32), prm[b, 7:8, 128:256]], axis=1
            )
            qkv[s, h, rows, :] = (dot_nn(a1[s, rows, :], planes(b, slice(None))) + bias).astype(BF16)
            query = qkv[s, h, rows, 0:128]
            key, value = qkv[s, h, 0:keys, 128:256], qkv[s, h, 0:keys, 256:384]
            parts = []
            for e in (0, 1):
                scores = dot_nt(pick_head(query, e), key) * SCALE + mask[rows, 0:keys]
                weights = jnp.exp(scores - jnp.max(scores, axis=-1, keepdims=True))
                probs = (weights / jnp.sum(weights, axis=-1, keepdims=True)).astype(BF16)
                prob[s, h, e, rows, 0:keys] = probs
                parts.append(dot_nn(probs, value))
            mix[s, h, rows, :] = jnp.where(low_lanes(HALF), parts[0], parts[1]).astype(BF16)

        unrolled(2, body)

    def partial(k, u, tile):
        rows = stream(u)

        def body(n):
            cols = ds(n * 256, 256)
            value = tile(rows, cols)
            acc[rows, cols] = value
            rs_out[k // 2, rows, cols] = value.astype(BF16)

        unrolled(4, body)
        rs_start(k, u)

    def feed_up(s, u):
        rows = stream(u)

        def body(i):
            h, n = div(i, 2), rem(i, 2)
            b = 2 * h + s
            cols = ds(n * 256, 256)
            v = dot_nn(a2[s, rows, :], wu[b, :, cols]) + prm[b, 6:7, cols]
            th = jnp.tanh(GELU_COEF * (v + CUBIC_COEF * v * v * v))
            hid[s, h, rows, cols] = (0.5 * v * (1.0 + th)).astype(BF16)
            slope[s, h, rows, cols] = 0.5 * (1.0 + th) + 0.5 * v * (1.0 - th * th) * GELU_COEF * (
                1.0 + 3.0 * CUBIC_COEF * v * v
            )

        unrolled(4, body)

    def forward(s, hooks):
        k = 4 * s
        target = xs_buf.at[1] if s == 0 else xo
        for u in (0, 1):
            if s == 1:
                ag_finish(3, u, xs_buf.at[1])
            first_norm(s, u)
            if u == 0:
                hooks[0]()
                w_ready(s, WQ)
            attention(s, u)
            if u == 0:
                hooks[1]()
                w_ready(s, WO)
            partial(
                k, u,
                lambda rows, cols: dot_nn(mix[s, 0, rows, :], wo[s, :, cols])
                + dot_nn(mix[s, 1, rows, :], wo[s + 2, :, cols]),
            )
        hooks[2]()
        for u in (0, 1):
            first_own(s, u)
            middle = xs_buf[s, own(u), :].astype(F32) + rs_finish(k, u) + prm[s, 0:1, :]
            yrow[u] = middle
            normed, inv = norm(middle)
            a2[s, own(u), :] = (normed * prm[s, 3:4, :] + prm[s, 5:6, :]).astype(BF16)
            ag_start(k + 1, u, a2.at[s])
            n2[s, u] = normed
            i2[s, u] = jnp.broadcast_to(inv, (R, 128))
        hooks[3]()
        w_ready(s, WU)
        for u in (0, 1):
            ag_finish(k + 1, u, a2.at[s])
            feed_up(s, u)
            if u == 0:
                hooks[4]()
                w_ready(s, WD)
            partial(
                k + 2, u,
                lambda rows, cols: dot_nn(hid[s, 0, rows, :], wd[s, :, cols])
                + dot_nn(hid[s, 1, rows, :], wd[s + 2, :, cols]),
            )
        hooks[5]()
        for u in (0, 1):
            target[own(u), :] = (yrow[u] + rs_finish(k + 2, u) + prm[s, 1:2, :]).astype(BF16)
            ag_start(k + 3, u, target)

    load_x.wait()
    for d in (1, 2, 3):
        send_prm(d).wait_recv()

    def f0_0():
        w_spread(0, WQ)
        w_spread(0, WO)
        w_hand_over(0, WQ)

    def f0_1():
        w_hand_over(0, WO)

    def f0_2():
        w_spread(0, WU)

    def f0_3():
        w_spread(0, WD)
        for k in range(4):
            w_send_kind(1, k)
        w_hand_over(0, WU)

    def f0_4():
        w_hand_over(0, WD)

    def f0_5():
        w_spread(1, WQ)
        w_spread(1, WO)
        w_spread(1, WU)

    def f1_0():
        w_hand_over(1, WQ)
        w_hand_over(1, WO)

    def f1_2():
        w_spread(1, WD)
        out_start(0, 0, xs_buf.at[1], so_out)

    def f1_3():
        w_hand_over(1, WU)

    def f1_4():
        w_hand_over(1, WD)

    def nothing():
        pass

    forward(0, [f0_0, f0_1, f0_2, f0_3, f0_4, f0_5])
    forward(1, [f1_0, nothing, f1_2, f1_3, f1_4, nothing])
    load_g.wait()

    def attention_back(s, u):
        rows = stream(u)
        keys = (u + 1) * HALF

        def body(h):
            grad_mix = dot_nt(dyb[s, rows, :], wo[2 * h + s]).astype(BF16)
            query = qkv[s, h, rows, 0:128]
            key, value = qkv[s, h, 0:keys, 128:256], qkv[s, h, 0:keys, 256:384]
            parts = []
            for e in (0, 1):
                probs = prob[s, h, e, rows, 0:keys]
                wide = probs.astype(F32)
                grad_prob = dot_nt(pick_head(grad_mix, e), value)
                delta = jnp.sum(wide * grad_prob, axis=-1, keepdims=True)
                grad_scores = (wide * (grad_prob - delta) * SCALE).astype(BF16)
                parts.append((dot_nn(grad_scores, key), dot_tn(grad_scores, query), dot_tn(probs, grad_mix)))
            dqkv[h, rows, 0:128] = jnp.where(low_lanes(HALF), parts[0][0], parts[1][0]).astype(BF16)
            for j in (1, 2):
                both = jnp.where(low_lanes(keys), parts[0][j], parts[1][j])
                cols = slice(j * 128, j * 128 + 128)
                if u == 1:
                    dqkv[h, rows, cols] = both[HALF:, :].astype(BF16)
                    dkv[h, :, (j - 1) * 128 : j * 128] = both[:HALF, :]
                else:
                    dqkv[h, rows, cols] = (both + dkv[h, :, (j - 1) * 128 : j * 128]).astype(BF16)

        unrolled(2, body)

    def add_row(s, i, value):
        sm[s, i : i + 1, :] = sm[s, i : i + 1, :] + jnp.sum(value, axis=0, keepdims=True)

    def backward(s, k, hooks):
        for u in (1, 0):
            rows = stream(u)
            if s == 0:
                ag_finish(11, u, g_buf.at[0])

            def grad_up_tile(i):
                h, n = div(i, 2), rem(i, 2)
                cols = ds(n * 256, 256)
                value = dot_nt(g_buf[s, rows, :], wd[2 * h + s, cols, :]) * slope[s, h, rows, cols]
                du[h, rows, cols] = value.astype(BF16)

            unrolled(4, grad_up_tile)
            partial(
                k, u,
                lambda rows, cols: dot_nt(du[0, rows, :], wu[s, cols, :]) + dot_nt(du[1, rows, :], wu[s + 2, cols, :]),
            )

        def grad_down(i):
            h, n = div(i, 2), rem(i, 2)
            rows = ds(n * 256, 256)
            gd[s, h, rows, :] = dot_tn(hid[s, h, :, rows], g_buf[s]).astype(BF16)

        unrolled(4, grad_down)
        gc_start(s, WD)
        hooks[0]()
        for u in (1, 0):
            top = g_buf[s, own(u), :].astype(F32)
            g_second = rs_finish(k, u)
            normed = n2[s, u]
            dy = top + norm_back(g_second, normed, i2[s, u, :, 0:1], prm[s, 3:4, :])
            dyb[s, own(u), :] = dy.astype(BF16)
            ag_start(k + 1, u, dyb.at[s])
            dyrow[u] = dy
            add_row(s, 1, top)
            add_row(s, 3, g_second * normed)
            add_row(s, 5, g_second)
            add_row(s, 0, dy)

        def grad_up(i):
            h, n = div(i, 4), rem(i, 4)
            rows = ds(n * 256, 256)
            gu[s, h, rows, :] = dot_tn(a2[s, :, rows], du[h]).astype(BF16)

        unrolled(8, grad_up)
        gc_start(s, WU)
        for h in (0, 1):
            sm[s, 6:7, h * 512 : h * 512 + 512] = jnp.sum(du[h].astype(F32), axis=0, keepdims=True)
        hooks[1]()
        for u in (1, 0):
            ag_finish(k + 1, u, dyb.at[s])
            attention_back(s, u)
            partial(
                k + 2, u,
                lambda rows, cols: dot_nt(dqkv[0, rows, :], planes(s, cols)) + dot_nt(dqkv[1, rows, :], planes(s + 2, cols)),
            )

        def grad_qkv(i):
            h, n = div(i, 4), rem(i, 4)
            rows = ds(n * 256, 256)
            value = dot_tn(a1[s, :, rows], dqkv[h]).astype(BF16)
            for j in range(3):
                gq[s, h, j, rows, :] = value[:, j * 128 : j * 128 + 128]

        unrolled(8, grad_qkv)
        gc_start(s, WQ)
        for h in (0, 1):
            go[s, h] = dot_tn(mix[s, h], dyb[s]).astype(BF16)
        gc_start(s, WO)
        for h in (0, 1):
            sums = jnp.sum(dqkv[h].astype(F32), axis=0, keepdims=True)
            sm[s, 7:8, h * 256 : h * 256 + 128] = sums[:, 0:128]
            sm[s, 7:8, h * 256 + 128 : h * 256 + 256] = sums[:, 256:384]
        hooks[2]()
        target = g_buf.at[0] if s == 1 else ig0
        for u in (1, 0):
            g_first = rs_finish(k + 2, u)
            normed = n1[s, u]
            low = dyrow[u] + norm_back(g_first, normed, i1[s, u, :, 0:1], prm[s, 2:3, :])
            target[own(u), :] = low.astype(BF16)
            if s == 1:
                ag_start(k + 3, u, target)
            elif u == 1:
                low_start(u)
            add_row(s, 2, g_first * normed)
            add_row(s, 4, g_first)
        hooks[3]()

    def b1_0():
        for u in (0, 1):
            ag_finish(7, u, xo)
        stage1(1, WD)
        out_start(1, 1, xo, so_out)

    def b1_1():
        stage1(1, WU)
        stage2(1, WD)

    def b1_2():
        stage1(1, WQ)
        stage1(1, WO)

    def b1_3():
        stage2(1, WO)

    backward(1, 8, [b1_0, b1_1, b1_2, b1_3])

    def b0_0():
        stage1(0, WD)
        stage2(1, WU)
        out_start(2, 1, g_buf.at[0], ig_out)
        stage3(1, WD)

    def b0_1():
        stage1(0, WU)
        stage2(0, WD)
        stage3(1, WU)
        stage2(1, WQ)

    def b0_2():
        stage1(0, WQ)
        stage1(0, WO)
        stage3(1, WO)
        stage3(1, WQ)
        stage4(1, WD)

    def b0_3():
        stage2(0, WU)
        stage2(0, WO)
        stage4(1, WU)

    backward(0, 12, [b0_0, b0_1, b0_2, b0_3])

    def small_copy(i, src, dst, device):
        return remote(src, dst, sm_s.at[i], sm_r.at[i], device)

    small_c = [small_copy(0, sm, smc, core_peer)]
    small_z = [small_copy(d, sm1, smz.at[d - 1], dev(x, y, zp(d), c)) for d in (1, 2, 3)]
    small_y = [small_copy(3 + d, sm2, smy.at[d - 1], dev(x, yp(d), z, c)) for d in (1, 2, 3)]
    small_x = [small_copy(6 + d, sm3, smx.at[d - 1], dev(xp(d), y, z, c)) for d in (1, 2, 3)]

    def start_all(copies):
        for copy in copies:
            copy.start()

    def arrived(copies):
        for copy in copies:
            copy.wait_recv()

    start_all(small_c)
    stage3(0, WU)
    stage2(0, WQ)
    arrived(small_c)
    sm1[...] = sm[...] + smc[...]
    start_all(small_z)
    stage3(0, WQ)
    low_start(0)
    stage3(0, WD)
    stage4(1, WO)
    stage4(1, WQ)
    stage3(0, WO)
    arrived(small_z)
    sm2[...] = sm1[...] + smz[0] + smz[1] + smz[2]
    start_all(small_y)
    for k in range(4):
        stage5(1, k)
    stage4(0, WU)
    arrived(small_y)
    sm3[...] = sm2[...] + smy[0] + smy[1] + smy[2]
    start_all(small_x)
    stage4(0, WD)
    stage4(0, WO)
    stage4(0, WQ)
    arrived(small_x)
    mine = sm3[p]
    shared = mine + smx[0, p] + smx[1, p] + smx[2, p]
    row = lax.broadcasted_iota(jnp.int32, (8, D), 0)
    small_out[...] = jnp.where(row < 6, shared, mine)
    for k in (WU, WD, WO, WQ):
        stage5(0, k)
    for k in (WU, WD, WO, WQ):
        gf_finish(k)

    out_finish(0, 0, xs_buf.at[1], so_out)
    out_finish(1, 1, xo, so_out)
    out_finish(2, 1, g_buf.at[0], ig_out)
    for u in (1, 0):
        low_finish(u)
    for d in (1, 2, 3):
        send_prm(d).wait_send()
    for s in (0, 1):
        for k in range(4):
            if k not in Z_FIRST:
                @pl.when(p == s)
                def _():
                    for d in (1, 2, 3):
                        gz_copy(s, k, 0, d).wait_send()

            def sent(d):
                if d == 2:
                    for e in (1, 3):
                        w_send(k, e).wait_send()
                else:
                    w_relay(k, 0 if d == 1 else 1).wait_send()
                for j in (0, 1):
                    w_side(k, d, j).wait_send()
                for j in (0, 1, 2):
                    w_pass(k, d, j).wait_send()

            w_each(s, sent)

            for h in (0, 1):
                gc_copy(s, k, h).wait_send()
                if k in Z_FIRST:
                    for d in (1, 2, 3):
                        gz_copy(s, k, h, d).wait_send()

            for j in (0, 1):
                @pl.when(p == s)
                def _():
                    relay_copy(s, k, j).wait_send()

                @pl.when(p != s)
                def _():
                    main_copy(s, k, j).wait_send()

    gathered = {
        1: a2.at[0], 3: xs_buf.at[1], 5: a2.at[1], 7: xo, 9: dyb.at[1], 11: g_buf.at[0], 13: dyb.at[0],
    }
    for u in (0, 1):
        for d in (1, 2, 3):
            for k in range(0, 16, 2):
                rs_copy(k, u, d).wait_send()
            for k, ref in gathered.items():
                ag_copy(k, u, ref, d).wait_send()
    for copy in small_c + small_z + small_y + small_x:
        copy.wait_send()


def finish_kernel(
    so_in, ig_in, gq_in, go_in, gu_in, gd_in, small_in,
    so_out, ig_out, gq_out, go_out, gu_out, gd_out, outb, downb, gains, shifts, upb, qvb,
    so_buf, ig_buf, gq_buf, go_buf, gu_buf, gd_buf, gq_f, go_f, gu_f, gd_f, l_sem, s_sem,
):
    ins = (gu_in, gd_in, so_in, ig_in, gq_in, go_in)
    bufs = (gu_buf, gd_buf, so_buf, ig_buf, gq_buf, go_buf)
    wide = (gu_f, gd_f, None, None, gq_f, go_f)
    outs = (gu_out, gd_out, so_out, ig_out, gq_out, go_out)
    loads = [pltpu.make_async_copy(ins[i], bufs[i], l_sem.at[i]) for i in range(6)]
    for copy in loads:
        copy.start()
    h = lax.div(lax.axis_index("tensor"), 4)
    outb[...] = small_in[0:1, :]
    downb[...] = small_in[1:2, :]
    gains[...] = small_in[2:4, :]
    shifts[...] = small_in[4:6, :]
    upb[...] = jnp.where(h == 0, small_in[6:7, 0:512], small_in[6:7, 512:1024])
    qvb[0:1, :] = jnp.where(h == 0, small_in[7:8, 0:128], small_in[7:8, 256:384])
    qvb[1:2, :] = jnp.where(h == 0, small_in[7:8, 128:256], small_in[7:8, 384:512])
    stores = []
    for i in range(6):
        loads[i].wait()
        source = bufs[i]
        if wide[i] is not None:
            source = wide[i]
            lead = source.shape[0]
            step = lead if len(source.shape) == 3 else 64

            def body(r):
                if len(source.shape) == 3:
                    rows = ds(r * 128, 128)
                    wide[i][:, rows, :] = bufs[i][:, rows, :].astype(F32)
                else:
                    rows = ds(r * 64, 64)
                    wide[i][rows, :] = bufs[i][rows, :].astype(F32)

            loop(8 if len(source.shape) == 3 else lead // step, body)
        stores.append(pltpu.make_async_copy(source, outs[i], s_sem.at[i]))
        stores[-1].start()
    for copy in stores:
        copy.wait()


def run(x_in, seg, wq, qvb, wo, outb, wu, upb, wd, downb, gain, shift, og):
    any_spec = pl.BlockSpec(memory_space=pl.ANY)
    vmem = pl.BlockSpec(memory_space=pltpu.VMEM)
    V = pltpu.VMEM
    dma = pltpu.SemaphoreType.DMA
    tokens = x_in.shape[0]

    def kinds(lead, shrink):
        return [V(tuple(lead) + shape_of(k, ROWS[k] // shrink), BF16) for k in range(4)]

    scratch = kinds((4,), 1)
    scratch += [
        V((4, 8, D), F32), V((SEQ, SEQ), F32),
        V((2, SEQ, D), BF16), V((2, SEQ, D), BF16), V((2, SEQ, D), BF16), V((2, SEQ, D), BF16), V((2, SEQ, D), BF16),
        V((SEQ, D), BF16), V((SEQ, D), BF16),
        V((2, 2, SEQ, 384), BF16), V((2, 2, 2, SEQ, SEQ), BF16), V((2, 2, SEQ, 128), BF16),
        V((2, 2, SEQ, 512), BF16), V((2, 2, SEQ, 512), F32),
        V((2, SEQ, 512), BF16), V((2, SEQ, 384), BF16), V((2, HALF, 256), F32), V((SEQ, D), F32),
        V((8, SEQ, D), BF16), V((8, 2, 3, R, D), BF16),
        V((2, 2, R, D), F32), V((2, 2, R, D), F32), V((2, 2, R, 128), F32), V((2, 2, R, 128), F32),
        V((2, R, D), F32), V((2, R, D), F32),
    ]
    scratch += kinds((2, 2), 1) + kinds((2, 2), 2)
    scratch += [V((2,) + shape_of(k, ROWS[k] // (8 if k in Z_FIRST else 2)), BF16) for k in range(4)]
    scratch += [V((2,) + shape_of(k, ROWS[k] // (16 if k in Z_FIRST else 4)), BF16) for k in range(4)]
    scratch += [V(((2, 2, 3) if k in Z_FIRST else (3,)) + shape_of(k, ROWS[k] // 8), BF16) for k in range(4)]
    scratch += kinds((), 1)
    scratch += [V((2, 8, D), F32)] * 5 + [V((3, 2, 8, D), F32)] * 3
    sems = (96, 96, 12, 12, 24, 24, 36, 36, 8, 8, 3, 3, 6, 16, 16, 8, 8, 8, 8, 60, 60, 12, 12, 4, 4, 4, 10, 10, 9, 9, 3, 30, 30, 2)
    scratch += [dma((n,)) for n in sems]
    grads = [jax.ShapeDtypeStruct(shape_of(k, ROWS[k]), BF16) for k in range(4)]
    rows = jax.ShapeDtypeStruct((tokens, D), BF16)
    parts = pl.pallas_call(
        kernel,
        out_shape=(rows, rows, *grads, jax.ShapeDtypeStruct((8, D), F32)),
        in_specs=[any_spec, vmem, any_spec, vmem, any_spec, vmem, any_spec, vmem, any_spec, vmem, vmem, vmem, any_spec],
        out_specs=(any_spec,) * 6 + (vmem,),
        scratch_shapes=scratch,
        compiler_params=pltpu.CompilerParams(collective_id=0, has_side_effects=True, vmem_limit_bytes=64 * 1024 * 1024),
    )(x_in, seg, wq, qvb, wo, outb, wu, upb, wd, downb, gain, shift, og)

    def f32(*shape):
        return jax.ShapeDtypeStruct(shape, F32)

    return pl.pallas_call(
        finish_kernel,
        out_shape=(
            rows, rows, *[f32(*shape_of(k, ROWS[k])) for k in range(4)],
            f32(1, D), f32(1, D), f32(2, D), f32(2, D), f32(1, 512), f32(2, 128),
        ),
        in_specs=[any_spec] * 6 + [vmem],
        out_specs=(any_spec,) * 6 + (vmem,) * 6,
        scratch_shapes=[
            V((tokens, D), BF16), V((tokens, D), BF16), *kinds((), 1),
            *[V(shape_of(k, ROWS[k]), F32) for k in range(4)], dma((6,)), dma((6,)),
        ],
        compiler_params=pltpu.CompilerParams(vmem_limit_bytes=62 * 1024 * 1024),
    )(*parts)


def on_device(
    section_input, segment_ids, w_qkv, qv_bias, w_out, out_bias, w_up, up_bias, w_down, down_bias, norm_gains,
    norm_shifts, out_grad,
):
    so, ig, gq, go, gu, gd, outb, downb, gains, shifts, upb, qvb = run(
        section_input, segment_ids.reshape(8, 128), w_qkv[0].transpose(1, 0, 2), qv_bias[0], w_out[0], out_bias,
        w_up[0], up_bias, w_down[0], down_bias, norm_gains[0], norm_shifts[0], out_grad,
    )
    return (
        so[None], ig[None], gq.transpose(1, 0, 2)[None], qvb[None], go[None], outb, gu[None], upb, gd[None], downb,
        gains[None], shifts[None],
    )


def solution(mesh):
    placed = (
        P("dp", None),
        P("dp"),
        P("pipe", None, None, "tensor"),
        P("pipe", None, "tensor"),
        P("pipe", "tensor", None),
        P("pipe", None),
        P("pipe", None, "tensor"),
        P("pipe", "tensor"),
        P("pipe", "tensor", None),
        P("pipe", None),
        P("pipe", None, None),
        P("pipe", None, None),
        P("dp", None),
    )
    return jax.shard_map(
        on_device,
        mesh=mesh,
        in_specs=placed,
        out_specs=(
            P("pipe", "dp", None),
            P("pipe", "dp", None),
            P("pipe", None, None, "tensor"),
            P("pipe", None, "tensor"),
            P("pipe", "tensor", None),
            P("pipe", None),
            P("pipe", None, "tensor"),
            P("pipe", "tensor"),
            P("pipe", "tensor", None),
            P("pipe", None),
            P("pipe", None, None),
            P("pipe", None, None),
        ),
        check_vma=False,
    )
```
